256 devices in a mesh: seq: 64 (over z, x, core), tp: 4 (over y).
Axes of the slice: x: 4, y: 4, z: 8, core: 2. Of those that a mesh axis runs over, the one named last changes fastest.
Arguments:
- hidden: bfloat16 [32768, 4096], P(('seq', 'tp')), may hold values from -640 to 640
- norm_gain: float32 [4096], replicated, may hold values from 0.5 to 1.5
- w_query: bfloat16 [4096, 2048], P(None, 'tp'), may hold values from -0.078125 to 0.078125
- w_key: bfloat16 [4096, 1024], P(None, 'tp'), may hold values from -2.421875 to 2.421875
- w_value: bfloat16 [4096, 1024], P(None, 'tp'), may hold values from -0.09375 to 0.09375
- doc_start: int32 [32768], P('seq'), may hold values from 0 to 32767, as said below
- block_owner: int32 [1024], P('seq'), may hold values from 0 to 63, as said below
Outputs:
- context_rows: bfloat16 [32768, 2048], P(('seq', 'tp'))
- key_cache: bfloat16 [49152, 1024], P('seq', 'tp')
- value_cache: bfloat16 [49152, 1024], P('seq', 'tp')
The draws below stay inside these ranges and needn't reach their ends.
Inputs may be any that keep to these rules, and one draw needn't show every extreme that they name: `doc_start`: rows with equal values form one document: consecutive rows beginning at the row whose number is that value. Every document has at most 256 rows and one has exactly 256; all but the last have at least 64. `block_owner`: owner numbers never fall along the blocks. Owner o holds the blocks from o * 16 + e(o) up to (o + 1) * 16 + e(o + 1) - 1, where -4 <= e <= 4 and e is 0 at both ends of the axis; so an owner holds between 8 and 24 blocks, and some owner holds exactly 24.
All inputs are finite; a program needn't handle non-finite values.
Results may differ from the reference program's by a relative error of at most 0.0078.
Values may be sent and summed in bfloat16 or wider, within the bound.
No kernel may reach another device: no remote copies, remote signals or barrier semaphores. Data moves between devices by JAX's collectives and lax.ppermute only.
A program may use at most 128 MiB of HBM per device.

```python
import jax
import jax.numpy as jnp
from jax import lax

D = 4096
KVH = 8
HD = 128
QH = 16
TOK_DEV = 512
BLK = 32
DOC_MIN = 64
DOC_MAX = 256
TOKENS = 32768
BPD = 16
SPILL = 4
CAP_BLK = 24
NBLK = 1024
CACHE_ROWS = 49152
N_SEQ = 64


def draw_hidden(key, part):
    base_key = jax.random.fold_in(key, 101)
    row_key = jax.random.fold_in(key, 102)
    column_key = jax.random.fold_in(key, 103)
    row_scale = jnp.exp(jax.random.uniform(row_key, (TOKENS, 1), jnp.float32, 0.0, 2.3))
    column_scale = jnp.exp(jax.random.uniform(column_key, (1, D), jnp.float32, 0.0, 2.3))
    jitter = jnp.clip(jax.random.normal(base_key, (TOKENS, D), jnp.float32), -5.0, 5.0)
    values = jitter * row_scale * column_scale
    return values.astype(jnp.bfloat16)


def query_base(key):
    jitter = jax.random.normal(jax.random.fold_in(key, 201), (D, QH * HD), jnp.float32)
    return jnp.clip(jitter, -5.0, 5.0) * D ** (-0.5)


def draw_w_query(key, part):
    return query_base(key).astype(jnp.bfloat16)


def draw_w_key(key, part):
    jitter = jax.random.normal(jax.random.fold_in(key, 204), (D, KVH * HD), jnp.float32)
    values = jnp.clip(jitter, -5.0, 5.0) * D ** (-0.5)
    return values.astype(jnp.bfloat16)


def draw_doc_start(key, part):
    doc_count = TOKENS // DOC_MIN + 1
    lengths = jax.random.randint(jax.random.fold_in(key, 301), (doc_count,), DOC_MIN, DOC_MAX + 1)
    longest = jax.random.randint(jax.random.fold_in(key, 302), (), 1, TOKENS // DOC_MAX)
    lengths = jnp.where(jnp.arange(doc_count) == longest, DOC_MAX, lengths).astype(jnp.int32)
    last_home = TOKENS - TOK_DEV
    aligned = jnp.any(jnp.cumsum(lengths).astype(jnp.int32) == last_home)
    nudge = jnp.where(lengths[0] < DOC_MAX, 1, -1).astype(jnp.int32)
    lengths = lengths.at[0].add(jnp.where(aligned, nudge, 0).astype(jnp.int32))
    doc_ends = jnp.cumsum(lengths).astype(jnp.int32)
    doc_starts = doc_ends - lengths
    picked = jnp.searchsorted(doc_ends, jnp.arange(TOKENS, dtype=jnp.int32), side='right')
    return doc_starts[picked].astype(jnp.int32)


def draw_block_owner(key, part):
    owners = NBLK // BPD
    shifts = jax.random.randint(jax.random.fold_in(key, 401), (owners + 1,), -SPILL, SPILL + 1)
    marked = jax.random.randint(jax.random.fold_in(key, 402), (), 1, owners - 1)
    places = jnp.arange(owners + 1)
    shifts = jnp.where(places == marked, -SPILL, shifts)
    shifts = jnp.where(places == marked + 1, SPILL, shifts)
    shifts = jnp.where((places == 0) | (places == owners), 0, shifts)
    bounds = places * BPD + shifts
    blocks = jnp.arange(NBLK)
    interior = bounds[1:owners]
    return jnp.sum((blocks[:, None] >= interior[None, :]).astype(jnp.int32), axis=1).astype(jnp.int32)


def block_levels(key, shape, cuts, least, high):
    loudness, own = 1.0, jax.random.fold_in(key, 6)
    for axis_at, shards_of in cuts:
        heights = jnp.exp(jax.random.uniform(jax.random.fold_in(own, axis_at), (shards_of,), jnp.float32, least / len(cuts), high / len(cuts)))
        loudness = loudness * jnp.repeat(heights, shape[axis_at] // shards_of).reshape([-1 if axis == axis_at else 1 for axis in range(len(shape))])
    return loudness


def noise(stream_key, shape, width, bound, pieces=(), kind=jnp.bfloat16):
    entries = width * jax.random.normal(stream_key, shape, jnp.float32)
    if pieces:
        entries = entries * block_levels(stream_key, shape, pieces, -0.22, 0.18)
    return jnp.clip(entries, -bound, bound).astype(kind)


def setup_inputs(seed: int = 0) -> dict:
    splits = jax.random.split(jax.random.key(seed), 8)
    return {
        "hidden": draw_hidden(jax.random.fold_in(splits[7], 71), 0),
        "norm_gain": jnp.clip(1.0 + 0.1 * jax.random.normal(splits[1], (D,), jnp.float32), 0.5, 1.5),
        "w_query": draw_w_query(jax.random.fold_in(splits[7], 71), 0),
        "w_key": draw_w_key(jax.random.fold_in(splits[7], 71), 0),
        "w_value": noise(splits[4], (D, KVH * HD), D ** -0.5, 0.09375, ((1, 4),)),
        "doc_start": draw_doc_start(jax.random.fold_in(splits[7], 71), 0),
        "block_owner": draw_block_owner(jax.random.fold_in(splits[7], 71), 0),
    }


EPS = 1e-05
ROPE_BASE = 500000.0

def rotate(packed, positions, head_count):
    row_count = packed.shape[0]
    head_width = packed.shape[1] // head_count
    half_width = head_width // 2
    frequency = jnp.power(ROPE_BASE, -jnp.arange(half_width, dtype=jnp.float32) * (2.0 / head_width))
    angles = positions.astype(jnp.float32)[:, None] * frequency[None, :]
    cosine = jnp.cos(angles)[:, None, :]
    sine_part = jnp.sin(angles)[:, None, :]
    reshaped = packed.reshape(row_count, head_count, head_width)
    first_half = reshaped[:, :, :half_width]
    second = reshaped[:, :, half_width:]
    rotated = jnp.concatenate([first_half * cosine - second * sine_part, second * cosine + first_half * sine_part], axis=2)
    return rotated.reshape(row_count, head_count * head_width)

def project(rows_in, norm_gain, w_query, w_key, w_value, positions):
    widened = rows_in.astype(jnp.float32)
    inverse_rms = lax.rsqrt(lax.optimization_barrier(jnp.mean(widened * widened, axis=1, keepdims=True)) + EPS)
    normed = (widened * inverse_rms * norm_gain.astype(jnp.float32)[None, :]).astype(jnp.bfloat16)
    queries = jnp.dot(normed, w_query, preferred_element_type=jnp.float32)
    keys_f = jnp.dot(normed, w_key, preferred_element_type=jnp.float32)
    values_f = jnp.dot(normed, w_value, preferred_element_type=jnp.float32)
    queries = rotate(queries, positions, queries.shape[1] // HD).astype(jnp.bfloat16)
    keys_f = rotate(keys_f, positions, keys_f.shape[1] // HD).astype(jnp.bfloat16)
    return (queries, keys_f, values_f.astype(jnp.bfloat16))

def attend(queries, keys_in, values_in, query_doc, query_row, key_doc, key_row, key_live, offset):
    row_count = queries.shape[0]
    key_count = keys_in.shape[0]
    groups = keys_in.shape[1] // HD
    per_group = queries.shape[1] // keys_in.shape[1]
    query_four = queries.astype(jnp.float32).reshape(row_count, groups, per_group, HD)
    key_three = keys_in.astype(jnp.float32).reshape(key_count, groups, HD)
    value_three = values_in.astype(jnp.float32).reshape(key_count, groups, HD)
    scores = jnp.einsum('rgjd,kgd->gjrk', query_four, key_three) * HD ** (-0.5)
    allowed = (query_doc[:, None] == key_doc[None, :]) & (key_row[None, :] <= query_row[:, None]) & (key_live[None, :] > 0)
    allowed = allowed | (jnp.arange(key_count)[None, :] == jnp.arange(row_count)[:, None] + offset)
    scores = jnp.where(allowed[None, None], scores, -jnp.inf)
    highest = lax.optimization_barrier(jnp.max(scores, axis=3, keepdims=True))
    weights = jnp.exp(scores - highest)
    weights = (weights / lax.optimization_barrier(jnp.sum(weights, axis=3, keepdims=True))).astype(jnp.bfloat16)
    blended = jnp.einsum('gjrk,kgd->rgjd', weights.astype(jnp.float32), value_three)
    return blended.astype(jnp.bfloat16).reshape(row_count, groups * per_group * HD)

def reference(hidden, norm_gain, w_query, w_key, w_value, doc_start, block_owner):
    row_number = jnp.arange(TOKENS, dtype=jnp.int32)
    queries, keys_bf, values_bf = project(hidden, norm_gain, w_query, w_key, w_value, row_number - doc_start)
    kv_width = keys_bf.shape[1]
    padded_keys = jnp.concatenate([jnp.zeros((TOK_DEV, kv_width), jnp.bfloat16), keys_bf], axis=0)
    padded_values = jnp.concatenate([jnp.zeros((TOK_DEV, kv_width), jnp.bfloat16), values_bf], axis=0)
    padded_doc = jnp.concatenate([jnp.full((TOK_DEV,), -1, jnp.int32), doc_start.astype(jnp.int32)], axis=0)
    padded_row = jnp.concatenate([jnp.arange(TOK_DEV, dtype=jnp.int32) - TOK_DEV, row_number], axis=0)

    def one_block(index):
        start = (index * TOK_DEV).astype(jnp.int32)
        block_queries = lax.dynamic_slice_in_dim(queries, start, TOK_DEV, 0)
        block_doc = lax.dynamic_slice_in_dim(doc_start.astype(jnp.int32), start, TOK_DEV, 0)
        block_row = lax.dynamic_slice_in_dim(row_number, start, TOK_DEV, 0)
        near_keys = lax.dynamic_slice_in_dim(padded_keys, start, 2 * TOK_DEV, 0)
        near_values = lax.dynamic_slice_in_dim(padded_values, start, 2 * TOK_DEV, 0)
        near_doc = lax.dynamic_slice_in_dim(padded_doc, start, 2 * TOK_DEV, 0)
        near_row = lax.dynamic_slice_in_dim(padded_row, start, 2 * TOK_DEV, 0)
        near_live = (near_doc >= 0).astype(jnp.int32)
        return attend(block_queries, near_keys, near_values, block_doc, block_row, near_doc, near_row, near_live, TOK_DEV)
    context_rows = lax.map(one_block, jnp.arange(N_SEQ, dtype=jnp.int32)).reshape(TOKENS, queries.shape[1])
    owners = jnp.arange(N_SEQ, dtype=jnp.int32)
    frame_block = owners[:, None] * BPD - SPILL + jnp.arange(CAP_BLK, dtype=jnp.int32)[None, :]
    inside = (frame_block >= 0) & (frame_block < NBLK)
    clamped = jnp.clip(frame_block, 0, NBLK - 1)
    owned = inside & (block_owner.astype(jnp.int32)[clamped] == owners[:, None])
    key_blocks = keys_bf.reshape(NBLK, BLK, kv_width)
    value_blocks = values_bf.reshape(NBLK, BLK, kv_width)
    key_cache = jnp.where(owned[:, :, None, None], key_blocks[clamped], jnp.zeros((), jnp.bfloat16)).reshape(CACHE_ROWS, kv_width)
    value_cache = jnp.where(owned[:, :, None, None], value_blocks[clamped], jnp.zeros((), jnp.bfloat16)).reshape(CACHE_ROWS, kv_width)
    return (context_rows, key_cache, value_cache)
```

```python
import functools

import jax
import jax.numpy as jnp
from jax import lax
from jax.experimental import pallas as pl
from jax.experimental.pallas import tpu as pltpu
from jax.sharding import PartitionSpec as P

HD = 128
EPS = 1e-05
ROPE_BASE = 500000.0
CH = 128
VM = pltpu.MemorySpace.VMEM


def ring(array, by):
    n = lax.axis_size("tp")
    return lax.ppermute(array, "tp", [(i, (i + by) % n) for i in range(n)])


def shift(array, by):
    n = lax.axis_size("seq")
    return lax.ppermute(array, "seq", [(i, i + by) for i in range(n) if 0 <= i + by < n])


def vmem(x):
    return pltpu.with_memory_space_constraint(x, VM)


def call(body, outs, scalars, arrays, flops=0):
    smem = pl.BlockSpec(memory_space=pltpu.SMEM)
    inside = pl.BlockSpec(memory_space=VM)
    moved = sum(a.size * a.dtype.itemsize for a in arrays)
    return pl.pallas_call(
        body,
        out_shape=[VM(s, d) for s, d in outs],
        in_specs=[smem] * len(scalars) + [inside] * len(arrays),
        out_specs=[inside] * len(outs),
        compiler_params=pltpu.CompilerParams(vmem_limit_bytes=24 << 20),
        cost_estimate=pl.CostEstimate(flops=flops, bytes_accessed=moved, transcendentals=0),
    )(*scalars, *[vmem(a) for a in arrays])


def normalize(x, gain):
    wide = x.astype(jnp.float32)
    inverse = lax.rsqrt(jnp.mean(wide * wide, axis=1, keepdims=True) + EPS)
    return (wide * inverse * gain).astype(jnp.bfloat16)


def rotate(x, cosine, sine):
    heads = x.shape[1] // HD
    parts = []
    for i in range(heads):
        one = x[:, i * HD : (i + 1) * HD]
        parts.append((one * cosine + pltpu.roll(one, HD // 2, 1) * sine).astype(jnp.bfloat16))
    return parts


def dot(a, b):
    return jnp.dot(a, b, preferred_element_type=jnp.float32)


def project_kv(normed, wk, wv, cosine, sine):
    keys = rotate(dot(normed, wk[...]), cosine, sine)
    values = dot(normed, wv[...]).astype(jnp.bfloat16)
    return keys, values


def project_q(normed, wq, cosine, sine):
    parts = []
    for i in range(wq.shape[1] // 256):
        parts += rotate(dot(normed, wq[:, i * 256 : (i + 1) * 256]), cosine, sine)
    return parts


def early_body(which, place, xa, xb, gain, wq, wk, wv, tables, q_out, kv_out):
    rows = pl.ds(pl.multiple_of(place[which] * CH, CH), CH)
    cosine, sine = tables[rows, 0:HD], tables[rows, HD : 2 * HD]
    normed = jnp.concatenate([normalize(xa[...], gain[...]), normalize(xb[...], gain[...])], axis=0)
    keys, values = project_kv(normed, wk, wv, cosine, sine)
    for i, part in enumerate(keys):
        kv_out[:, i * HD : (i + 1) * HD] = part
    kv_out[:, 256:512] = values
    for i, part in enumerate(project_q(normed, wq, cosine, sine)):
        q_out[:, i * HD : (i + 1) * HD] = part


def last_body(place, owner, xa, xb, gain, wk, wv, tables, kv0, kv1, kv2, normed_out, hi_out, a_out, b_out, left_out, kv_all):
    rows = pl.ds(pl.multiple_of(place[3] * CH, CH), CH)
    cosine, sine = tables[rows, 0:HD], tables[rows, HD : 2 * HD]
    normed = jnp.concatenate([normalize(xa[...], gain[...]), normalize(xb[...], gain[...])], axis=0)
    normed_out[...] = normed
    keys, values = project_kv(normed, wk, wv, cosine, sine)
    for i, part in enumerate(keys):
        kv_all[place[3], :, i * HD : (i + 1) * HD] = part
    kv_all[place[3], :, 256:512] = values
    kv_all[place[0]] = kv0[...]
    kv_all[place[1]] = kv1[...]
    kv_all[place[2]] = kv2[...]
    hi_out[0:CH] = kv_all[2]
    hi_out[CH : 2 * CH] = kv_all[3]
    home = place[4]
    count = jnp.int32(0)
    for j in range(4):
        count += (owner[12 + j] == home + 1).astype(jnp.int32)
    hi_out[2 * CH : 2 * CH + 16] = jnp.full((16, 512), count.astype(jnp.float32), jnp.float32).astype(jnp.bfloat16)
    first = kv_all[0]
    a_out[...] = first
    b_out[...] = kv_all[1]
    for j in range(4):
        part = first[j * 32 : (j + 1) * 32]
        left_out[j * 32 : (j + 1) * 32] = jnp.where(owner[j] == home - 1, part, jnp.zeros_like(part))


def attend_tile(tile, q, key_parts, value_parts, doc):
    window = 3 * CH
    key_row = lax.broadcasted_iota(jnp.int32, (CH, window), 1) + (tile - 2) * CH
    row = lax.broadcasted_iota(jnp.int32, (CH, window), 0) + tile * CH
    allowed = (key_row >= doc) & (key_row <= row)
    allowed = jnp.concatenate([allowed, allowed], axis=0)
    outs = []
    for g in range(2):
        pair = jnp.concatenate([q[:, 2 * g * HD : (2 * g + 1) * HD], q[:, (2 * g + 1) * HD : (2 * g + 2) * HD]], axis=0)
        keys, values = key_parts[g], value_parts[g]
        scores = lax.dot_general(pair, keys, (((1,), (1,)), ((), ())), preferred_element_type=jnp.float32) * HD ** (-0.5)
        scores = jnp.where(allowed, scores, -jnp.inf)
        highest = jnp.max(scores, axis=1, keepdims=True)
        weights = jnp.exp(scores - highest)
        weights = (weights * (1.0 / jnp.sum(weights, axis=1, keepdims=True))).astype(jnp.bfloat16)
        blended = dot(weights, values).astype(jnp.bfloat16)
        outs += [blended[:CH], blended[CH:]]
    return outs


def split_kv(parts):
    joined = jnp.concatenate(parts, axis=0)
    keys = [joined[:, 0:HD], joined[:, HD : 2 * HD]]
    values = [joined[:, 2 * HD : 3 * HD], joined[:, 3 * HD : 4 * HD]]
    return keys, values


def upper_body(place, normed, wq, tables, q0, q1, q2, a, b, hi, ctx_out, q_out, q_all):
    rows = pl.ds(pl.multiple_of(place[3] * CH, CH), CH)
    cosine, sine = tables[rows, 0:HD], tables[rows, HD : 2 * HD]
    for i, part in enumerate(project_q(normed[...], wq, cosine, sine)):
        q_all[place[3], :, i * HD : (i + 1) * HD] = part
    q_all[place[0]] = q0[...]
    q_all[place[1]] = q1[...]
    q_all[place[2]] = q2[...]
    q_out[0] = q_all[0]
    q_out[1] = q_all[1]
    for tile in (2, 3):
        if tile == 2:
            parts = [a[...], b[...], hi[0:CH]]
        else:
            parts = [b[...], hi[0 : 2 * CH]]
        keys, values = split_kv(parts)
        doc = tables[tile * CH : (tile + 1) * CH, 2 * HD : 2 * HD + 1].astype(jnp.int32)
        for i, part in enumerate(attend_tile(tile, q_all[tile], keys, values, doc)):
            ctx_out[tile - 2, :, i * HD : (i + 1) * HD] = part


def lower_body(place, halo, a, b, q, tables, upper, s0, s1, s2, s3, ctx_all):
    for tile in (0, 1):
        if tile == 0:
            parts = [halo[0 : 2 * CH], a[...]]
        else:
            parts = [halo[CH : 2 * CH], a[...], b[...]]
        keys, values = split_kv(parts)
        doc = tables[tile * CH : (tile + 1) * CH, 2 * HD : 2 * HD + 1].astype(jnp.int32)
        for i, part in enumerate(attend_tile(tile, q[tile], keys, values, doc)):
            ctx_all[tile, :, i * HD : (i + 1) * HD] = part
    ctx_all[2] = upper[0]
    ctx_all[3] = upper[1]
    s0[...] = ctx_all[place[0]]
    s1[...] = ctx_all[place[2]]
    s2[...] = ctx_all[place[3]]
    s3[...] = ctx_all[place[1]]


def cache_body(place, owner, halo, a, b, hi, right, key_out, value_out):
    home = place[4]

    def put(row, part):
        key_out[row : row + part.shape[0]] = part[:, 0:256]
        value_out[row : row + part.shape[0]] = part[:, 256:512]

    count = halo[2 * CH : 2 * CH + 1, :].astype(jnp.float32)
    for j in range(4):
        part = halo[CH + j * 32 : CH + (j + 1) * 32]
        put(j * 32, jnp.where(count > 3.5 - j, part.astype(jnp.float32), 0.0).astype(jnp.bfloat16))
    for j in range(16):
        source = (a, b, hi, hi)[j // 4]
        at = j * 32 if j < 4 else (j - 4) * 32 if j < 8 else (j - 8) * 32
        part = source[at : at + 32]
        put(CH + j * 32, jnp.where(owner[j] == home, part, jnp.zeros_like(part)))
    put(CH + 512, right[...])


def join_body(place, s0, r1, r2, r3, out):
    for piece, at in ((s0, place[0]), (r1, place[1]), (r2, place[3]), (r3, place[2])):
        out[:, pl.ds(pl.multiple_of(at * 512, 512), 512)] = piece[...]


def shards(hidden, norm_gain, w_query, w_key, w_value, doc_start, block_owner):
    me, home = lax.axis_index("tp"), lax.axis_index("seq")
    n = lax.axis_size("tp")
    rows = doc_start.shape[0]
    half = CH // 2
    bf = jnp.bfloat16
    place = jnp.stack([me, (me + n - 1) % n, (me + 1) % n, (me + 2) % n, home]).astype(jnp.int32)
    own_a, own_b = hidden[:half], hidden[half:]
    left_a, right_b = ring(own_a, 1), ring(own_b, -1)
    left_b, right_a = ring(own_b, 1), ring(own_a, -1)
    far_a, far_b = ring(left_a, 1), ring(right_b, -1)

    row_number = home * rows + jnp.arange(rows, dtype=jnp.int32)
    frequency = jnp.power(ROPE_BASE, -jnp.arange(HD // 2, dtype=jnp.float32) * (2.0 / HD))
    angles = (row_number - doc_start).astype(jnp.float32)[:, None] * frequency[None, :]
    cosine, sine = jnp.cos(angles), jnp.sin(angles)
    doc = (doc_start - home * rows).astype(jnp.float32)
    tables = jnp.concatenate([cosine, cosine, -sine, sine, jnp.broadcast_to(doc[:, None], (rows, HD))], axis=1)

    gain = norm_gain[None, :]
    flops = 2 * CH * 4096 * 1024
    early = []
    for which, (xa, xb) in enumerate(((own_a, own_b), (left_a, left_b), (right_a, right_b))):
        early.append(
            call(
                functools.partial(early_body, which),
                [((CH, 512), bf), ((CH, 512), bf)],
                [place],
                [xa, xb, gain, w_query, w_key, w_value, tables],
                flops,
            )
        )
    (q0, kv0), (q1, kv1), (q2, kv2) = early

    smem = pl.BlockSpec(memory_space=pltpu.SMEM)
    inside = pl.BlockSpec(memory_space=VM)

    def scratch_call(body, outs, scalars, arrays, flops):
        return pl.pallas_call(
            body,
            out_shape=[VM(s, d) for s, d in outs],
            in_specs=[smem] * len(scalars) + [inside] * len(arrays),
            out_specs=[inside] * len(outs),
            scratch_shapes=[VM((4, CH, 512), bf)],
            compiler_params=pltpu.CompilerParams(vmem_limit_bytes=24 << 20),
            cost_estimate=pl.CostEstimate(flops=flops, bytes_accessed=1 << 20, transcendentals=0),
        )(*scalars, *[vmem(x) for x in arrays])

    normed, hi, a, b, to_left = scratch_call(
        last_body,
        [((CH, 4096), bf), ((2 * CH + 16, 512), bf), ((CH, 512), bf), ((CH, 512), bf), ((CH, 512), bf)],
        [place, block_owner],
        [far_a, far_b, gain, w_key, w_value, tables, kv0, kv1, kv2],
        flops // 2,
    )
    halo = shift(hi, 1)
    from_right = shift(to_left, -1)
    upper, q_low = scratch_call(
        upper_body,
        [((2, CH, 512), bf), ((2, CH, 512), bf)],
        [place],
        [normed, w_query, tables, q0, q1, q2, a, b, hi],
        flops,
    )
    s0, s1, s2, s3 = scratch_call(
        lower_body, [((CH, 512), bf)] * 4, [place], [halo, a, b, q_low, tables, upper], flops // 2
    )
    r1, r2, r3 = ring(s1, 1), ring(s2, 2), ring(s3, 3)
    key_cache, value_cache = pl.pallas_call(
        cache_body,
        out_shape=[jax.ShapeDtypeStruct((rows + 2 * CH, 256), bf)] * 2,
        in_specs=[smem] * 2 + [inside] * 5,
        out_specs=[inside] * 2,
        compiler_params=pltpu.CompilerParams(vmem_limit_bytes=24 << 20),
        cost_estimate=pl.CostEstimate(flops=0, bytes_accessed=2 << 20, transcendentals=0),
    )(place, block_owner, *[vmem(x) for x in (halo, a, b, hi, from_right)])
    context = pl.pallas_call(
        join_body,
        out_shape=jax.ShapeDtypeStruct((CH, 2048), bf),
        in_specs=[smem] + [inside] * 4,
        out_specs=inside,
        cost_estimate=pl.CostEstimate(flops=0, bytes_accessed=1 << 20, transcendentals=0),
    )(place, *[vmem(x) for x in (s0, r1, r2, r3)])
    return (context, key_cache, value_cache)


def solution(mesh):
    return jax.shard_map(
        shards,
        mesh=mesh,
        in_specs=(
            P(("seq", "tp"), None),
            P(),
            P(None, "tp"),
            P(None, "tp"),
            P(None, "tp"),
            P("seq"),
            P("seq"),
        ),
        out_specs=(P(("seq", "tp"), None), P("seq", "tp"), P("seq", "tp")),
        check_vma=False,
    )
```

```python
import functools

import jax
import jax.numpy as jnp
from jax import lax
from jax.experimental import pallas as pl
from jax.experimental.pallas import tpu as pltpu
from jax.sharding import PartitionSpec as P


HD = 128
EPS = 1e-05
ROPE_BASE = 500000.0
CH = 128
VM = pltpu.MemorySpace.VMEM
HB = pltpu.MemorySpace.HBM


def ring(array, by):
    n = lax.axis_size("tp")
    return lax.ppermute(array, "tp", [(i, (i + by) % n) for i in range(n)])


def shift(array, by):
    n = lax.axis_size("seq")
    return lax.ppermute(array, "seq", [(i, i + by) for i in range(n) if 0 <= i + by < n])


def spots():
    me, home = lax.axis_index("tp"), lax.axis_index("seq")
    return [lax.rem(me + k, 4) for k in (0, 3, 1, 2)] + [home]


def vmem(x):
    return pltpu.with_memory_space_constraint(x, VM)


def call(body, outs, scalars, arrays, flops=0):
    smem = pl.BlockSpec(memory_space=pltpu.SMEM)
    inside = pl.BlockSpec(memory_space=VM)
    moved = sum(a.size * a.dtype.itemsize for a in arrays)
    return pl.pallas_call(
        body,
        out_shape=[VM(s, d) for s, d in outs],
        in_specs=[smem] * len(scalars) + [inside] * len(arrays),
        out_specs=[inside] * len(outs),
        compiler_params=pltpu.CompilerParams(vmem_limit_bytes=12 << 20),
        cost_estimate=pl.CostEstimate(flops=flops, bytes_accessed=moved, transcendentals=0),
    )(*scalars, *[vmem(a) for a in arrays])


def normalize(x, gain):
    wide = x.astype(jnp.float32)
    inverse = lax.rsqrt(jnp.mean(wide * wide, axis=1, keepdims=True) + EPS)
    return (wide * inverse * gain).astype(jnp.bfloat16)


def rotate(x, cosine, sine):
    heads = x.shape[1] // HD
    parts = []
    for i in range(heads):
        one = x[:, i * HD : (i + 1) * HD]
        parts.append((one * cosine + pltpu.roll(one, HD // 2, 1) * sine).astype(jnp.bfloat16))
    return parts


def dot(a, b):
    return jnp.dot(a, b, preferred_element_type=jnp.float32)


def project_kv(normed, wk, wv, cosine, sine):
    keys = rotate(dot(normed, wk[...]), cosine, sine)
    values = dot(normed, wv[...]).astype(jnp.bfloat16)
    return keys, values


def project_q(normed, wq, cosine, sine):
    parts = []
    for i in range(wq.shape[1] // 256):
        parts += rotate(dot(normed, wq[:, i * 256 : (i + 1) * 256]), cosine, sine)
    return parts


def run(copies):
    for copy in copies:
        copy.start()
    for copy in copies:
        copy.wait()


def weights_body(wq, wk, wv, after, wq_out, wk_out, wv_out, sems):
    run([pltpu.make_async_copy(w, out, sems.at[i]) for i, (w, out) in enumerate(((wq, wq_out), (wk, wk_out), (wv, wv_out)))])


def prepare(place, which, pieces, gain, cosines, sines):
    rows = pl.ds(pl.multiple_of(place[which] * CH, CH), CH)
    normed = jnp.concatenate([normalize(piece[...], gain[...]) for piece in pieces], axis=0)
    return normed, cosines[rows], sines[rows]


def early_body(which, xa, xb, gain, wq, wk, wv, cosines, sines, q_out, kv_out):
    normed, cosine, sine = prepare(spots(), which, (xa, xb), gain, cosines, sines)
    keys, values = project_kv(normed, wk, wv, cosine, sine)
    for i, part in enumerate(keys):
        kv_out[:, i * HD : (i + 1) * HD] = part
    kv_out[:, 256:512] = values
    for i, part in enumerate(project_q(normed, wq, cosine, sine)):
        q_out[:, i * HD : (i + 1) * HD] = part


def last_body(owner, xa, xb, gain, wk, wv, cosines, sines, kv0, kv1, kv2, normed_out, hi_out, a_out, b_out, kv_all):
    place = spots()
    far = place[3]
    kv_all[place[0]] = kv0[...]
    kv_all[place[1]] = kv1[...]
    kv_all[place[2]] = kv2[...]
    normed, cosine, sine = prepare(place, 3, (xa, xb), gain, cosines, sines)
    normed_out[...] = normed
    keys, values = project_kv(normed, wk, wv, cosine, sine)
    for i, part in enumerate([*keys, values[:, :HD], values[:, HD:]]):
        kv_all[far, :, i * HD : (i + 1) * HD] = part
    hi_out[0:CH] = kv_all[2]
    hi_out[CH : 2 * CH] = kv_all[3]
    count = jnp.int32(0)
    for j in range(4):
        count += (owner[12 + j] == place[4] + 1).astype(jnp.int32)
    hi_out[2 * CH : 2 * CH + 16] = jnp.full((16, 512), count.astype(jnp.float32), jnp.float32).astype(jnp.bfloat16)
    a_out[...] = kv_all[0]
    b_out[...] = kv_all[1]


def attend_tile(tile, q, key_parts, value_parts, doc):
    window = 3 * CH
    key_row = lax.broadcasted_iota(jnp.int32, (CH, window), 1) + (tile - 2) * CH
    row = lax.broadcasted_iota(jnp.int32, (CH, window), 0) + tile * CH
    allowed = (key_row >= doc) & (key_row <= row)
    allowed = jnp.concatenate([allowed, allowed], axis=0)
    outs = []
    for g in range(2):
        pair = jnp.concatenate([q[:, 2 * g * HD : (2 * g + 1) * HD], q[:, (2 * g + 1) * HD : (2 * g + 2) * HD]], axis=0)
        keys, values = key_parts[g], value_parts[g]
        scores = lax.dot_general(pair, keys, (((1,), (1,)), ((), ())), preferred_element_type=jnp.float32) * HD ** (-0.5)
        scores = jnp.where(allowed, scores, -jnp.inf)
        highest = jnp.max(scores, axis=1, keepdims=True)
        weights = jnp.exp(scores - highest)
        weights = (weights * (1.0 / jnp.sum(weights, axis=1, keepdims=True))).astype(jnp.bfloat16)
        blended = dot(weights, values).astype(jnp.bfloat16)
        outs += [blended[:CH], blended[CH:]]
    return outs


def split_kv(parts):
    joined = jnp.concatenate(parts, axis=0)
    keys = [joined[:, 0:HD], joined[:, HD : 2 * HD]]
    values = [joined[:, 2 * HD : 3 * HD], joined[:, 3 * HD : 4 * HD]]
    return keys, values


def upper_body(normed, wq, cosines, sines, docs, q0, q1, q2, a, b, hi, ctx_out, q_out, q_all):
    place = spots()
    far = place[3]
    rows = pl.ds(pl.multiple_of(far * CH, CH), CH)
    q_all[place[0]] = q0[...]
    q_all[place[1]] = q1[...]
    q_all[place[2]] = q2[...]
    for i, part in enumerate(project_q(normed[...], wq, cosines[rows], sines[rows])):
        q_all[far, :, i * HD : (i + 1) * HD] = part
    q_out[0] = q_all[0]
    q_out[1] = q_all[1]
    for tile in (2, 3):
        if tile == 2:
            parts = [a[...], b[...], hi[0:CH]]
        else:
            parts = [b[...], hi[0 : 2 * CH]]
        keys, values = split_kv(parts)
        doc = docs[tile * CH : (tile + 1) * CH, 0:1]
        for i, part in enumerate(attend_tile(tile, q_all[tile], keys, values, doc)):
            ctx_out[tile - 2, :, i * HD : (i + 1) * HD] = part


def lower_body(owner, halo, a, b, q, docs, upper, s0, s1, s2, s3, left_out, ctx_all):
    place = spots()
    for j in range(4):
        part = a[j * 32 : (j + 1) * 32]
        left_out[j * 32 : (j + 1) * 32] = jnp.where(owner[j] == place[4] - 1, part, jnp.zeros_like(part))
    for tile in (0, 1):
        if tile == 0:
            parts = [halo[0 : 2 * CH], a[...]]
        else:
            parts = [halo[CH : 2 * CH], a[...], b[...]]
        keys, values = split_kv(parts)
        doc = docs[tile * CH : (tile + 1) * CH, 0:1]
        for i, part in enumerate(attend_tile(tile, q[tile], keys, values, doc)):
            ctx_all[tile, :, i * HD : (i + 1) * HD] = part
    ctx_all[2] = upper[0]
    ctx_all[3] = upper[1]
    s0[...] = ctx_all[place[0]]
    s1[...] = ctx_all[place[2]]
    s2[...] = ctx_all[place[3]]
    s3[...] = ctx_all[place[1]]


def cache_body(owner, halo, a, b, hi, key_out, value_out, keys, values, sems):
    home = spots()[4]
    total = keys.shape[0]

    def put(row, part):
        keys[row : row + part.shape[0]] = part[:, 0:256]
        values[row : row + part.shape[0]] = part[:, 256:512]

    count = halo[2 * CH : 2 * CH + 1, :].astype(jnp.float32)
    for j in range(4):
        part = halo[CH + j * 32 : CH + (j + 1) * 32]
        put(j * 32, jnp.where(count > 3.5 - j, part.astype(jnp.float32), 0.0).astype(jnp.bfloat16))
    for j in range(16):
        source = (a, b, hi, hi)[j // 4]
        at = j * 32 if j < 4 else (j - 4) * 32 if j < 8 else (j - 8) * 32
        part = source[at : at + 32]
        put(CH + j * 32, jnp.where(owner[j] == home, part, jnp.zeros_like(part)))
    copies = [
        pltpu.make_async_copy(keys, key_out.at[0:total], sems.at[0]),
        pltpu.make_async_copy(values, value_out.at[0:total], sems.at[1]),
    ]
    run(copies)


def join_body(right, s0, r1, r2, r3, key_in, value_in, out, key_out, value_out, sems):
    place = spots()
    first = key_out.shape[0] - CH
    copies = [
        pltpu.make_async_copy(right.at[:, 0:256], key_out.at[first : first + CH], sems.at[4]),
        pltpu.make_async_copy(right.at[:, 256:512], value_out.at[first : first + CH], sems.at[5]),
    ]
    for i, (piece, at) in enumerate(((s0, place[0]), (r1, place[1]), (r2, place[3]), (r3, place[2]))):
        columns = pl.ds(pl.multiple_of(at * 512, 512), 512)
        copies.append(pltpu.make_async_copy(piece, out.at[:, columns], sems.at[i]))
    run(copies)


def layer(hidden, norm_gain, w_query, w_key, w_value, doc_start, block_owner):
    home = lax.axis_index("seq")
    rows = doc_start.shape[0]
    bf = jnp.bfloat16
    smem = pl.BlockSpec(memory_space=pltpu.SMEM)
    inside = pl.BlockSpec(memory_space=VM)
    outside = pl.BlockSpec(memory_space=pltpu.MemorySpace.HBM)
    wide = hidden.shape[1]

    def mover(body, outs, arrays, size):
        return pl.pallas_call(
            body,
            out_shape=[VM(s, bf) for s in outs],
            in_specs=[outside if x.size > CH * wide // 2 else pl.BlockSpec(memory_space=pl.ANY) for x in arrays],
            out_specs=[inside] * len(outs),
            scratch_shapes=[pltpu.SemaphoreType.DMA((len(outs),))],
            compiler_params=pltpu.CompilerParams(vmem_limit_bytes=2 << 20),
            cost_estimate=pl.CostEstimate(flops=0, bytes_accessed=size, transcendentals=0),
        )(*[pltpu.with_memory_space_constraint(x, HB) if x.size > CH * wide // 2 else x for x in arrays])

    own_a, own_b = hidden[: CH // 2], hidden[CH // 2 :]
    left_a = ring(own_a, 1)
    right_b = ring(own_b, -1)
    left_b, right_a = ring(own_b, 1), ring(own_a, -1)
    far_a, far_b = ring(left_a, 1), ring(right_b, -1)
    row_number = home * rows + jnp.arange(rows, dtype=jnp.int32)
    lane = jnp.arange(HD, dtype=jnp.float32)
    lane_half = jnp.where(lane < HD // 2, lane, lane - HD // 2)
    frequency = jnp.power(ROPE_BASE, -lane_half * (2.0 / HD))
    angles = (row_number - doc_start).astype(jnp.float32)[:, None] * frequency[None, :]
    cosines, sines = jnp.cos(angles), jnp.where(lane < HD // 2, -1.0, 1.0)[None, :] * jnp.sin(angles)
    docs = jnp.broadcast_to((doc_start - home * rows)[:, None], (rows, HD))

    w_query, w_key, w_value = mover(
        weights_body, [w.shape for w in (w_query, w_key, w_value)], [w_query, w_key, w_value, docs], 16 << 20
    )
    gain = norm_gain[None, :]
    flops = 2 * CH * 4096 * 1024
    early = []
    for which, (xa, xb) in enumerate(((own_a, own_b), (left_a, left_b), (right_a, right_b))):
        early.append(
            call(
                functools.partial(early_body, which),
                [((CH, 512), bf), ((CH, 512), bf)],
                [],
                [xa, xb, gain, w_query, w_key, w_value, cosines, sines],
                flops,
            )
        )
    (q0, kv0), (q1, kv1), (q2, kv2) = early

    def scratch_call(body, outs, scalars, arrays, flops):
        return pl.pallas_call(
            body,
            out_shape=[VM(s, d) for s, d in outs],
            in_specs=[smem] * len(scalars) + [inside] * len(arrays),
            out_specs=[inside] * len(outs),
            scratch_shapes=[VM((4, CH, 512), bf)],
            compiler_params=pltpu.CompilerParams(vmem_limit_bytes=12 << 20),
            cost_estimate=pl.CostEstimate(flops=flops, bytes_accessed=1 << 20, transcendentals=0),
        )(*scalars, *[vmem(x) for x in arrays])

    normed, hi, a, b = scratch_call(
        last_body,
        [((CH, wide), bf), ((2 * CH + 16, 512), bf), ((CH, 512), bf), ((CH, 512), bf)],
        [block_owner],
        [far_a, far_b, gain, w_key, w_value, cosines, sines, kv0, kv1, kv2],
        flops // 2,
    )
    halo = shift(hi, 1)
    upper, q_low = scratch_call(
        upper_body,
        [((2, CH, 512), bf), ((2, CH, 512), bf)],
        [],
        [normed, w_query, cosines, sines, docs, q0, q1, q2, a, b, hi],
        flops,
    )
    s0, s1, s2, s3, to_left = scratch_call(
        lower_body, [((CH, 512), bf)] * 5, [block_owner], [halo, a, b, q_low, docs, upper], flops // 2
    )
    pieces = []
    for by, piece in ((2, s2), (1, s1), (3, s3)):
        pieces.append(ring(piece, by))
    r2, r1, r3 = pieces
    from_right = shift(to_left, -1)
    cache = jax.ShapeDtypeStruct((rows + 2 * CH, 256), bf)
    key_cache, value_cache = pl.pallas_call(
        cache_body,
        out_shape=[cache, cache],
        in_specs=[smem] + [inside] * 4,
        out_specs=[outside] * 2,
        scratch_shapes=[VM((rows + CH, 256), bf)] * 2 + [pltpu.SemaphoreType.DMA((2,))],
        compiler_params=pltpu.CompilerParams(vmem_limit_bytes=12 << 20),
        cost_estimate=pl.CostEstimate(flops=0, bytes_accessed=2 << 20, transcendentals=0),
    )(block_owner, *[vmem(x) for x in (halo, a, b, hi)])
    context, key_cache, value_cache = pl.pallas_call(
        join_body,
        out_shape=[jax.ShapeDtypeStruct((CH, 2048), bf), cache, cache],
        in_specs=[inside] * 5 + [outside] * 2,
        out_specs=[outside] * 3,
        scratch_shapes=[pltpu.SemaphoreType.DMA((6,))],
        compiler_params=pltpu.CompilerParams(vmem_limit_bytes=2 << 20),
        input_output_aliases={5: 1, 6: 2},
        cost_estimate=pl.CostEstimate(flops=0, bytes_accessed=1 << 20, transcendentals=0),
    )(*[vmem(x) for x in (from_right, s0, r1, r2, r3)], key_cache, value_cache)
    return (context, key_cache, value_cache)


def solution(mesh):
    return jax.shard_map(
        layer,
        mesh=mesh,
        in_specs=(
            P(("seq", "tp"), None),
            P(),
            P(None, "tp"),
            P(None, "tp"),
            P(None, "tp"),
            P("seq"),
            P("seq"),
        ),
        out_specs=(P(("seq", "tp"), None), P("seq", "tp"), P("seq", "tp")),
        check_vma=False,
    )
```

```python
import functools

import jax
import jax.numpy as jnp
from jax import lax
from jax.experimental import pallas as pl
from jax.experimental.pallas import tpu as pltpu
from jax.sharding import PartitionSpec as P


HD = 128
EPS = 1e-05
ROPE_BASE = 500000.0
CH = 128
VM = pltpu.MemorySpace.VMEM
HB = pltpu.MemorySpace.HBM


def ring(array, by):
    n = lax.axis_size("tp")
    return lax.ppermute(array, "tp", [(i, (i + by) % n) for i in range(n)])


def shift(array, by):
    n = lax.axis_size("seq")
    return lax.ppermute(array, "seq", [(i, i + by) for i in range(n) if 0 <= i + by < n])


def spots():
    me, home = lax.axis_index("tp"), lax.axis_index("seq")
    return [lax.rem(me + k, 4) for k in (0, 3, 1, 2)] + [home]


def vmem(x):
    return pltpu.with_memory_space_constraint(x, VM)


def call(body, outs, scalars, arrays, flops=0):
    smem = pl.BlockSpec(memory_space=pltpu.SMEM)
    inside = pl.BlockSpec(memory_space=VM)
    moved = sum(a.size * a.dtype.itemsize for a in arrays)
    return pl.pallas_call(
        body,
        out_shape=[VM(s, d) for s, d in outs],
        in_specs=[smem] * len(scalars) + [inside] * len(arrays),
        out_specs=[inside] * len(outs),
        compiler_params=pltpu.CompilerParams(vmem_limit_bytes=12 << 20),
        cost_estimate=pl.CostEstimate(flops=flops, bytes_accessed=moved, transcendentals=0),
    )(*scalars, *[vmem(a) for a in arrays])


def normalize(x, gain):
    wide = x.astype(jnp.float32)
    inverse = lax.rsqrt(jnp.mean(wide * wide, axis=1, keepdims=True) + EPS)
    return (wide * inverse * gain).astype(jnp.bfloat16)


def rotate(x, cosine, sine):
    heads = x.shape[1] // HD
    parts = []
    for i in range(heads):
        one = x[:, i * HD : (i + 1) * HD]
        parts.append((one * cosine + pltpu.roll(one, HD // 2, 1) * sine).astype(jnp.bfloat16))
    return parts


def dot(a, b):
    return jnp.dot(a, b, preferred_element_type=jnp.float32)


def project_kv(normed, wk, wv, cosine, sine):
    keys = rotate(dot(normed, wk[...]), cosine, sine)
    values = dot(normed, wv[...]).astype(jnp.bfloat16)
    return keys, values


def project_q(normed, wq, cosine, sine):
    parts = []
    for i in range(wq.shape[1] // 256):
        parts += rotate(dot(normed, wq[:, i * 256 : (i + 1) * 256]), cosine, sine)
    return parts


def run(copies):
    for copy in copies:
        copy.start()
    for copy in copies:
        copy.wait()


def weights_body(wq, wk, wv, after, wq_out, wk_out, wv_out, sems):
    run([pltpu.make_async_copy(w, out, sems.at[i]) for i, (w, out) in enumerate(((wq, wq_out), (wk, wk_out), (wv, wv_out)))])


def prepare(place, which, pieces, gain, cosines, sines):
    rows = pl.ds(pl.multiple_of(place[which] * CH, CH), CH)
    normed = jnp.concatenate([normalize(piece[...], gain[...]) for piece in pieces], axis=0)
    return normed, cosines[rows], sines[rows]


def early_body(which, xa, xb, gain, wq, wk, wv, cosines, sines, q_out, kv_out):
    normed, cosine, sine = prepare(spots(), which, (xa, xb), gain, cosines, sines)
    keys, values = project_kv(normed, wk, wv, cosine, sine)
    for i, part in enumerate(keys):
        kv_out[:, i * HD : (i + 1) * HD] = part
    kv_out[:, 256:512] = values
    for i, part in enumerate(project_q(normed, wq, cosine, sine)):
        q_out[:, i * HD : (i + 1) * HD] = part


def last_body(owner, xa, xb, gain, wk, wv, cosines, sines, kv0, kv1, kv2, normed_out, hi_out, a_out, b_out, kv_all):
    place = spots()
    far = place[3]
    kv_all[place[0]] = kv0[...]
    kv_all[place[1]] = kv1[...]
    kv_all[place[2]] = kv2[...]
    normed, cosine, sine = prepare(place, 3, (xa, xb), gain, cosines, sines)
    normed_out[...] = normed
    keys, values = project_kv(normed, wk, wv, cosine, sine)
    for i, part in enumerate([*keys, values[:, :HD], values[:, HD:]]):
        kv_all[far, :, i * HD : (i + 1) * HD] = part
    hi_out[0:CH] = kv_all[2]
    hi_out[CH : 2 * CH] = kv_all[3]
    count = jnp.int32(0)
    for j in range(4):
        count += (owner[12 + j] == place[4] + 1).astype(jnp.int32)
    hi_out[2 * CH : 2 * CH + 16] = jnp.full((16, 512), count.astype(jnp.float32), jnp.float32).astype(jnp.bfloat16)
    a_out[...] = kv_all[0]
    b_out[...] = kv_all[1]


def attend_tile(tile, q, key_parts, value_parts, doc):
    window = 3 * CH
    key_row = lax.broadcasted_iota(jnp.int32, (CH, window), 1) + (tile - 2) * CH
    row = lax.broadcasted_iota(jnp.int32, (CH, window), 0) + tile * CH
    allowed = (key_row >= doc) & (key_row <= row)
    allowed = jnp.concatenate([allowed, allowed], axis=0)
    outs = []
    for g in range(2):
        pair = jnp.concatenate([q[:, 2 * g * HD : (2 * g + 1) * HD], q[:, (2 * g + 1) * HD : (2 * g + 2) * HD]], axis=0)
        keys, values = key_parts[g], value_parts[g]
        scores = lax.dot_general(pair, keys, (((1,), (1,)), ((), ())), preferred_element_type=jnp.float32) * HD ** (-0.5)
        scores = jnp.where(allowed, scores, -jnp.inf)
        highest = jnp.max(scores, axis=1, keepdims=True)
        weights = jnp.exp(scores - highest)
        weights = (weights * (1.0 / jnp.sum(weights, axis=1, keepdims=True))).astype(jnp.bfloat16)
        blended = dot(weights, values).astype(jnp.bfloat16)
        outs += [blended[:CH], blended[CH:]]
    return outs


def split_kv(parts):
    joined = jnp.concatenate(parts, axis=0)
    keys = [joined[:, 0:HD], joined[:, HD : 2 * HD]]
    values = [joined[:, 2 * HD : 3 * HD], joined[:, 3 * HD : 4 * HD]]
    return keys, values


def upper_body(owner, normed, wq, cosines, sines, docs, q0, q1, q2, a, b, hi, ctx_out, q_out, left_out, q_all):
    place = spots()
    for j in range(4):
        part = a[j * 32 : (j + 1) * 32]
        left_out[j * 32 : (j + 1) * 32] = jnp.where(owner[j] == place[4] - 1, part, jnp.zeros_like(part))
    far = place[3]
    rows = pl.ds(pl.multiple_of(far * CH, CH), CH)
    q_all[place[0]] = q0[...]
    q_all[place[1]] = q1[...]
    q_all[place[2]] = q2[...]
    for i, part in enumerate(project_q(normed[...], wq, cosines[rows], sines[rows])):
        q_all[far, :, i * HD : (i + 1) * HD] = part
    q_out[0] = q_all[0]
    q_out[1] = q_all[1]
    for tile in (2, 3):
        if tile == 2:
            parts = [a[...], b[...], hi[0:CH]]
        else:
            parts = [b[...], hi[0 : 2 * CH]]
        keys, values = split_kv(parts)
        doc = docs[tile * CH : (tile + 1) * CH, 0:1]
        for i, part in enumerate(attend_tile(tile, q_all[tile], keys, values, doc)):
            ctx_out[tile - 2, :, i * HD : (i + 1) * HD] = part


def lower_body(halo, a, b, q, docs, upper, s0, s1, s2, s3, ctx_all):
    place = spots()
    for tile in (0, 1):
        if tile == 0:
            parts = [halo[0 : 2 * CH], a[...]]
        else:
            parts = [halo[CH : 2 * CH], a[...], b[...]]
        keys, values = split_kv(parts)
        doc = docs[tile * CH : (tile + 1) * CH, 0:1]
        for i, part in enumerate(attend_tile(tile, q[tile], keys, values, doc)):
            ctx_all[tile, :, i * HD : (i + 1) * HD] = part
    ctx_all[2] = upper[0]
    ctx_all[3] = upper[1]
    s0[...] = ctx_all[place[0]]
    s1[...] = ctx_all[place[2]]
    s2[...] = ctx_all[place[3]]
    s3[...] = ctx_all[place[1]]


def cache_body(owner, halo, a, b, hi, key_out, value_out, keys, values, sems):
    home = spots()[4]
    total = keys.shape[0]

    def put(row, part):
        keys[row : row + part.shape[0]] = part[:, 0:256]
        values[row : row + part.shape[0]] = part[:, 256:512]

    count = halo[2 * CH : 2 * CH + 1, :].astype(jnp.float32)
    for j in range(4):
        part = halo[CH + j * 32 : CH + (j + 1) * 32]
        put(j * 32, jnp.where(count > 3.5 - j, part.astype(jnp.float32), 0.0).astype(jnp.bfloat16))
    for j in range(16):
        source = (a, b, hi, hi)[j // 4]
        at = j * 32 if j < 4 else (j - 4) * 32 if j < 8 else (j - 8) * 32
        part = source[at : at + 32]
        put(CH + j * 32, jnp.where(owner[j] == home, part, jnp.zeros_like(part)))
    copies = [
        pltpu.make_async_copy(keys, key_out.at[0:total], sems.at[0]),
        pltpu.make_async_copy(values, value_out.at[0:total], sems.at[1]),
    ]
    run(copies)


def join_body(right, s0, r1, r2, r3, key_in, value_in, out, key_out, value_out, sems):
    place = spots()
    first = key_out.shape[0] - CH
    copies = [
        pltpu.make_async_copy(right.at[:, 0:256], key_out.at[first : first + CH], sems.at[4]),
        pltpu.make_async_copy(right.at[:, 256:512], value_out.at[first : first + CH], sems.at[5]),
    ]
    for i, (piece, at) in enumerate(((s0, place[0]), (r1, place[1]), (r2, place[3]), (r3, place[2]))):
        columns = pl.ds(pl.multiple_of(at * 512, 512), 512)
        copies.append(pltpu.make_async_copy(piece, out.at[:, columns], sems.at[i]))
    run(copies)


def layer(hidden, norm_gain, w_query, w_key, w_value, doc_start, block_owner):
    home = lax.axis_index("seq")
    rows = doc_start.shape[0]
    bf = jnp.bfloat16
    smem = pl.BlockSpec(memory_space=pltpu.SMEM)
    inside = pl.BlockSpec(memory_space=VM)
    outside = pl.BlockSpec(memory_space=pltpu.MemorySpace.HBM)
    wide = hidden.shape[1]

    def mover(body, outs, arrays, size):
        return pl.pallas_call(
            body,
            out_shape=[VM(s, bf) for s in outs],
            in_specs=[outside if x.size > CH * wide // 2 else pl.BlockSpec(memory_space=pl.ANY) for x in arrays],
            out_specs=[inside] * len(outs),
            scratch_shapes=[pltpu.SemaphoreType.DMA((len(outs),))],
            compiler_params=pltpu.CompilerParams(vmem_limit_bytes=2 << 20),
            cost_estimate=pl.CostEstimate(flops=0, bytes_accessed=size, transcendentals=0),
        )(*[pltpu.with_memory_space_constraint(x, HB) if x.size > CH * wide // 2 else x for x in arrays])

    own_a, own_b = hidden[: CH // 2], hidden[CH // 2 :]
    left_a = ring(own_a, 1)
    right_b = ring(own_b, -1)
    left_b = ring(own_b, 1)
    right_a = ring(own_a, -1)
    far_a, far_b = ring(left_a, 1), ring(right_b, -1)
    row_number = home * rows + jnp.arange(rows, dtype=jnp.int32)
    lane = jnp.arange(HD, dtype=jnp.float32)
    lane_half = jnp.where(lane < HD // 2, lane, lane - HD // 2)
    frequency = jnp.power(ROPE_BASE, -lane_half * (2.0 / HD))
    angles = (row_number - doc_start).astype(jnp.float32)[:, None] * frequency[None, :]
    cosines, sines = jnp.cos(angles), jnp.where(lane < HD // 2, -1.0, 1.0)[None, :] * jnp.sin(angles)
    docs = jnp.broadcast_to((doc_start - home * rows)[:, None], (rows, HD))

    w_query, w_key, w_value = mover(
        weights_body, [w.shape for w in (w_query, w_key, w_value)], [w_query, w_key, w_value, docs], 16 << 20
    )
    gain = norm_gain[None, :]
    flops = 2 * CH * 4096 * 1024
    early = []
    for which, (xa, xb) in enumerate(((own_a, own_b), (left_a, left_b), (right_a, right_b))):
        early.append(
            call(
                functools.partial(early_body, which),
                [((CH, 512), bf), ((CH, 512), bf)],
                [],
                [xa, xb, gain, w_query, w_key, w_value, cosines, sines],
                flops,
            )
        )
    (q0, kv0), (q1, kv1), (q2, kv2) = early

    def scratch_call(body, outs, scalars, arrays, flops):
        return pl.pallas_call(
            body,
            out_shape=[VM(s, d) for s, d in outs],
            in_specs=[smem] * len(scalars) + [inside] * len(arrays),
            out_specs=[inside] * len(outs),
            scratch_shapes=[VM((4, CH, 512), bf)],
            compiler_params=pltpu.CompilerParams(vmem_limit_bytes=12 << 20),
            cost_estimate=pl.CostEstimate(flops=flops, bytes_accessed=1 << 20, transcendentals=0),
        )(*scalars, *[vmem(x) for x in arrays])

    normed, hi, a, b = scratch_call(
        last_body,
        [((CH, wide), bf), ((2 * CH + 16, 512), bf), ((CH, 512), bf), ((CH, 512), bf)],
        [block_owner],
        [far_a, far_b, gain, w_key, w_value, cosines, sines, kv0, kv1, kv2],
        flops // 2,
    )
    halo = shift(hi, 1)
    upper, q_low, to_left = scratch_call(
        upper_body,
        [((2, CH, 512), bf), ((2, CH, 512), bf), ((CH, 512), bf)],
        [block_owner],
        [normed, w_query, cosines, sines, docs, q0, q1, q2, a, b, hi],
        flops,
    )
    from_right = shift(to_left, -1)
    s0, s1, s2, s3 = scratch_call(
        lower_body, [((CH, 512), bf)] * 4, [], [halo, a, b, q_low, docs, upper], flops // 2
    )
    pieces = []
    for by, piece in ((2, s2), (1, s1), (3, s3)):
        pieces.append(ring(piece, by))
    r2, r1, r3 = pieces
    cache = jax.ShapeDtypeStruct((rows + 2 * CH, 256), bf)
    key_cache, value_cache = pl.pallas_call(
        cache_body,
        out_shape=[cache, cache],
        in_specs=[smem] + [inside] * 4,
        out_specs=[outside] * 2,
        scratch_shapes=[VM((rows + CH, 256), bf)] * 2 + [pltpu.SemaphoreType.DMA((2,))],
        compiler_params=pltpu.CompilerParams(vmem_limit_bytes=12 << 20),
        cost_estimate=pl.CostEstimate(flops=0, bytes_accessed=2 << 20, transcendentals=0),
    )(block_owner, *[vmem(x) for x in (halo, a, b, hi)])
    context, key_cache, value_cache = pl.pallas_call(
        join_body,
        out_shape=[jax.ShapeDtypeStruct((CH, 2048), bf), cache, cache],
        in_specs=[inside] * 5 + [outside] * 2,
        out_specs=[outside] * 3,
        scratch_shapes=[pltpu.SemaphoreType.DMA((6,))],
        compiler_params=pltpu.CompilerParams(vmem_limit_bytes=2 << 20),
        input_output_aliases={5: 1, 6: 2},
        cost_estimate=pl.CostEstimate(flops=0, bytes_accessed=1 << 20, transcendentals=0),
    )(*[vmem(x) for x in (from_right, s0, r1, r2, r3)], key_cache, value_cache)
    return (context, key_cache, value_cache)


def solution(mesh):
    return jax.shard_map(
        layer,
        mesh=mesh,
        in_specs=(
            P(("seq", "tp"), None),
            P(),
            P(None, "tp"),
            P(None, "tp"),
            P(None, "tp"),
            P("seq"),
            P("seq"),
        ),
        out_specs=(P(("seq", "tp"), None), P("seq", "tp"), P("seq", "tp")),
        check_vma=False,
    )
```

```python
import jax
import jax.numpy as jnp
from jax import lax
from jax.experimental import pallas as pl
from jax.experimental.pallas import tpu as pltpu
from jax.sharding import PartitionSpec as P


HD = 128
EPS = 1e-05
ROPE_BASE = 500000.0
CH = 128
VM = pltpu.MemorySpace.VMEM
HB = pltpu.MemorySpace.HBM


def ring(array, by):
    n = lax.axis_size("tp")
    return lax.ppermute(array, "tp", [(i, (i + by) % n) for i in range(n)])


def across(array, moves):
    homes, n = lax.axis_size("seq"), lax.axis_size("tp")
    pairs = [(h * n + t, (h + by) * n + t) for h in range(homes) for t, by in moves.items() if 0 <= h + by < homes]
    return lax.ppermute(array, ("seq", "tp"), pairs)


def spots():
    me, home = lax.axis_index("tp"), lax.axis_index("seq")
    return [lax.rem(me + k, 4) for k in (0, 3, 1, 2)] + [home]


def vmem(x):
    return pltpu.with_memory_space_constraint(x, VM)


def call(body, outs, arrays, flops=0, owner=None, alias=None, scratch=()):
    smem = pl.BlockSpec(memory_space=pltpu.SMEM)
    inside = pl.BlockSpec(memory_space=VM)
    lead = [] if owner is None else [owner]
    moved = sum(x.size * x.dtype.itemsize for x in arrays)
    return pl.pallas_call(
        body,
        out_shape=[o if isinstance(o, jax.ShapeDtypeStruct) else VM(o, jnp.bfloat16) for o in outs],
        in_specs=[smem] * len(lead) + [inside] * len(arrays),
        out_specs=[
            pl.BlockSpec(memory_space=HB) if isinstance(o, jax.ShapeDtypeStruct) else inside for o in outs
        ],
        scratch_shapes=list(scratch),
        input_output_aliases={} if alias is None else {len(lead) + alias: 0},
        compiler_params=pltpu.CompilerParams(vmem_limit_bytes=12 << 20),
        cost_estimate=pl.CostEstimate(flops=flops, bytes_accessed=moved, transcendentals=0),
    )(*lead, *[vmem(x) for x in arrays])


def normalize(x, gain):
    wide = x.astype(jnp.float32)
    inverse = lax.rsqrt(jnp.mean(wide * wide, axis=1, keepdims=True) + EPS)
    return (wide * inverse * gain).astype(jnp.bfloat16)


def rotate(x, cosine, sine):
    heads = x.shape[1] // HD
    parts = []
    for i in range(heads):
        one = x[:, i * HD : (i + 1) * HD]
        parts.append((one * cosine + pltpu.roll(one, HD // 2, 1) * sine).astype(jnp.bfloat16))
    return parts


def dot(a, b):
    return jnp.dot(a, b, preferred_element_type=jnp.float32)


def project_kv(normed, wk, wv, cosine, sine):
    keys = rotate(dot(normed, wk[...]), cosine, sine)
    values = dot(normed, wv[...]).astype(jnp.bfloat16)
    return keys, values


def project_q(normed, wq, cosine, sine):
    parts = []
    for i in range(wq.shape[1] // 256):
        parts += rotate(dot(normed, wq[:, i * 256 : (i + 1) * 256]), cosine, sine)
    return parts


def run(copies):
    for copy in copies:
        copy.start()
    for copy in copies:
        copy.wait()


def weights_body(wq, wk, wv, after, wq_out, wk_out, wv_out, sems):
    run([pltpu.make_async_copy(w, out, sems.at[i]) for i, (w, out) in enumerate(((wq, wq_out), (wk, wk_out), (wv, wv_out)))])


def chunk_rows(at):
    return pl.ds(pl.multiple_of(at * CH, CH), CH)


def normalize_all(pieces, gain):
    return jnp.concatenate([normalize(piece[...], gain[...]) for piece in pieces], axis=0)


def put(ref, index, rows, parts):
    for i, part in enumerate(parts):
        ref[index, :, i * HD : (i + 1) * HD] = part[rows]


def kv_parts(normed, wk, wv, cosine, sine):
    keys, values = project_kv(normed, wk, wv, cosine, sine)
    return [*keys, values[:, :HD], values[:, HD:]]


def own_body(xa, xb, gain, wq, wk, wv, cosines, sines, ext, q_out):
    own = spots()[0]
    rows = chunk_rows(own)
    normed = normalize_all((xa, xb), gain)
    put(ext, 2 + own, slice(None), kv_parts(normed, wk, wv, cosines[rows], sines[rows]))
    for i, part in enumerate(project_q(normed, wq, cosines[rows], sines[rows])):
        q_out[:, i * HD : (i + 1) * HD] = part


def owned_part(part, live):
    return jnp.where(live, part, jnp.zeros_like(part))


def sides_body(owner, ext_in, ra, rb, la, lb, gain, wk, wv, cosines, sines, ext, normed_out, hi_out, left_out):
    _, left, right, _, home = spots()
    normed = normalize_all((ra, rb, la, lb), gain)
    normed_out[...] = normed
    rows = [chunk_rows(right), chunk_rows(left)]
    cosine = jnp.concatenate([cosines[r] for r in rows], axis=0)
    sine = jnp.concatenate([sines[r] for r in rows], axis=0)
    parts = kv_parts(normed, wk, wv, cosine, sine)
    put(ext, 2 + right, slice(0, CH), parts)
    put(ext, 2 + left, slice(CH, 2 * CH), parts)
    hi_out[0:CH] = ext[4]
    hi_out[CH : 2 * CH] = ext[5]
    count = jnp.int32(0)
    for j in range(4):
        count += (owner[12 + j] == home + 1).astype(jnp.int32)
    hi_out[2 * CH : 2 * CH + 16] = jnp.full((16, 512), count.astype(jnp.float32), jnp.float32).astype(jnp.bfloat16)
    for j in range(4):
        left_out[j * 32 : (j + 1) * 32] = owned_part(ext[2, j * 32 : (j + 1) * 32], owner[j] == home - 1)


def sides_q_body(normed, wq, cosines, sines, right_out, left_out):
    _, left, right, _, _ = spots()
    rows = [chunk_rows(right), chunk_rows(left)]
    cosine = jnp.concatenate([cosines[r] for r in rows], axis=0)
    sine = jnp.concatenate([sines[r] for r in rows], axis=0)
    for i, part in enumerate(project_q(normed[...], wq, cosine, sine)):
        right_out[:, i * HD : (i + 1) * HD] = part[:CH]
        left_out[:, i * HD : (i + 1) * HD] = part[CH:]


def attend(tile, q, ext, docs):
    window = 3 * CH
    doc = docs[chunk_rows(tile), 0:1]
    key_row = lax.broadcasted_iota(jnp.int32, (CH, window), 1) + (tile - 2) * CH
    row = lax.broadcasted_iota(jnp.int32, (CH, window), 0) + tile * CH
    allowed = (key_row >= doc) & (key_row <= row)
    allowed = jnp.concatenate([allowed, allowed], axis=0)
    near = ext[pl.ds(tile, 3)].reshape(window, 512)
    outs = []
    for g in range(2):
        pair = jnp.concatenate(q[2 * g : 2 * g + 2], axis=0)
        keys, values = near[:, g * HD : (g + 1) * HD], near[:, (2 + g) * HD : (3 + g) * HD]
        scores = lax.dot_general(pair, keys, (((1,), (1,)), ((), ())), preferred_element_type=jnp.float32) * HD ** (-0.5)
        scores = jnp.where(allowed, scores, -jnp.inf)
        highest = jnp.max(scores, axis=1, keepdims=True)
        weights = jnp.exp(scores - highest)
        weights = (weights * (1.0 / jnp.sum(weights, axis=1, keepdims=True))).astype(jnp.bfloat16)
        blended = dot(weights, values).astype(jnp.bfloat16)
        outs += [blended[:CH], blended[CH:]]
    return outs


def heads(q):
    return [q[:, i * HD : (i + 1) * HD] for i in range(4)]


def emit(out, parts):
    for i, part in enumerate(parts):
        out[:, i * HD : (i + 1) * HD] = part


def first_body(ext_in, halo, q, docs, ext, out):
    _, _, right, _, _ = spots()
    ext[0] = halo[0:CH]
    ext[1] = halo[CH : 2 * CH]
    emit(out, attend(right, heads(q), ext, docs))


def last_body(owner, ext_in, xa, xb, gain, wk, wv, cosines, sines, ext, normed_out, late_out):
    _, _, _, far, home = spots()
    rows = chunk_rows(far)
    normed = normalize_all((xa, xb), gain)
    normed_out[...] = normed
    parts = kv_parts(normed, wk, wv, cosines[rows], sines[rows])
    put(ext, 2 + far, slice(None), parts)
    for j in range(4):
        live = (far > 0) | (owner[j] == home - 1)
        for i, part in enumerate(parts):
            late_out[j * 32 : (j + 1) * 32, i * HD : (i + 1) * HD] = owned_part(part[j * 32 : (j + 1) * 32], live)


def far_body(ext_in, normed, wq, cosines, sines, docs, ext, out):
    far = spots()[3]
    rows = chunk_rows(far)
    q = project_q(normed[...], wq, cosines[rows], sines[rows])
    emit(out, attend(far, q, ext, docs))


def left_body(ext_in, late, q, docs, ext, out):
    own, left, _, _, _ = spots()

    @pl.when(own < 2)
    def _():
        ext[own] = late[...]

    emit(out, attend(left, heads(q), ext, docs))


def own_tile_body(owner, ext, late, halo, from_right, q, docs, out, key_out, value_out, keys, values, sems):
    own, _, _, _, home = spots()

    def put_cache(row, part):
        keys[row : row + part.shape[0]] = part[:, 0:256]
        values[row : row + part.shape[0]] = part[:, 256:512]

    count = halo[2 * CH : 2 * CH + 1, :].astype(jnp.float32)
    for j in range(4):
        part = ext[1, j * 32 : (j + 1) * 32]
        put_cache(j * 32, jnp.where(count > 3.5 - j, part.astype(jnp.float32), 0.0).astype(jnp.bfloat16))
    for j in range(16):
        part = ext[2 + j // 4, (j % 4) * 32 : (j % 4 + 1) * 32]
        put_cache(CH + j * 32, owned_part(part, owner[j] == home))

    @pl.when(own == 2)
    def _():
        put_cache(5 * CH, late[...])

    @pl.when(own != 2)
    def _():
        put_cache(5 * CH, from_right[...])

    copies = [
        pltpu.make_async_copy(keys, key_out, sems.at[0]),
        pltpu.make_async_copy(values, value_out, sems.at[1]),
    ]
    for copy in copies:
        copy.start()
    emit(out, attend(own, heads(q), ext, docs))
    for copy in copies:
        copy.wait()


def join_body(s0, r1, r2, r3, out, sems):
    own, left, right, far, _ = spots()
    copies = []
    for i, (piece, at) in enumerate(((s0, own), (r1, left), (r2, far), (r3, right))):
        columns = pl.ds(pl.multiple_of(at * 512, 512), 512)
        copies.append(pltpu.make_async_copy(piece, out.at[:, columns], sems.at[i]))
    run(copies)


def layer(hidden, norm_gain, w_query, w_key, w_value, doc_start, block_owner):
    home = lax.axis_index("seq")
    rows = doc_start.shape[0]
    bf = jnp.bfloat16
    inside = pl.BlockSpec(memory_space=VM)
    outside = pl.BlockSpec(memory_space=pltpu.MemorySpace.HBM)
    wide = hidden.shape[1]

    def mover(body, outs, arrays, size):
        return pl.pallas_call(
            body,
            out_shape=[VM(s, bf) for s in outs],
            in_specs=[outside if x.size > CH * wide // 2 else pl.BlockSpec(memory_space=pl.ANY) for x in arrays],
            out_specs=[inside] * len(outs),
            scratch_shapes=[pltpu.SemaphoreType.DMA((len(outs),))],
            compiler_params=pltpu.CompilerParams(vmem_limit_bytes=2 << 20),
            cost_estimate=pl.CostEstimate(flops=0, bytes_accessed=size, transcendentals=0),
        )(*[pltpu.with_memory_space_constraint(x, HB) if x.size > CH * wide // 2 else x for x in arrays])

    own_a, own_b = hidden[: CH // 2], hidden[CH // 2 :]
    left_a = ring(own_a, 1)
    right_b = ring(own_b, -1)
    left_b = ring(own_b, 1)
    right_a = ring(own_a, -1)
    far_a, far_b = ring(left_a, 1), ring(right_b, -1)
    row_number = home * rows + jnp.arange(rows, dtype=jnp.int32)
    lane = jnp.arange(HD, dtype=jnp.float32)
    lane_half = jnp.where(lane < HD // 2, lane, lane - HD // 2)
    frequency = jnp.power(ROPE_BASE, -lane_half * (2.0 / HD))
    angles = (row_number - doc_start).astype(jnp.float32)[:, None] * frequency[None, :]
    cosines, sines = jnp.cos(angles), jnp.where(lane < HD // 2, -1.0, 1.0)[None, :] * jnp.sin(angles)
    docs = jnp.broadcast_to((doc_start - home * rows)[:, None], (rows, HD))

    w_query, w_key, w_value = mover(
        weights_body, [w.shape for w in (w_query, w_key, w_value)], [w_query, w_key, w_value, docs], 16 << 20
    )
    gain = norm_gain[None, :]
    flops = 2 * CH * wide * 1024
    scores = 8 * 2 * CH * 3 * CH * HD
    slots = (6, CH, 512)
    piece = (CH, 512)
    ext, q_own = call(own_body, [slots, piece], [own_a, own_b, gain, w_query, w_key, w_value, cosines, sines], flops)
    ext, normed, hi, to_left = call(
        sides_body,
        [slots, (2 * CH, wide), (2 * CH + 16, 512), piece],
        [ext, right_a, right_b, left_a, left_b, gain, w_key, w_value, cosines, sines],
        flops,
        owner=block_owner,
        alias=0,
    )
    halo = across(hi, {t: 1 for t in range(4)})
    from_right = across(to_left, {t: -1 for t in (0, 1, 3)})
    q_right, q_left = call(sides_q_body, [piece, piece], [normed, w_query, cosines, sines], flops)
    ext, s1 = call(first_body, [slots, piece], [ext, halo, q_right, docs], scores, alias=0)
    r1 = ring(s1, 1)
    ext, normed, far = call(
        last_body,
        [slots, (CH, wide), piece],
        [ext, far_a, far_b, gain, w_key, w_value, cosines, sines],
        flops // 2,
        owner=block_owner,
        alias=0,
    )
    late = across(far, {0: 1, 1: 1, 2: -1})
    ext, s2 = call(far_body, [slots, piece], [ext, normed, w_query, cosines, sines, docs], flops, alias=0)
    r2 = ring(s2, 2)
    ext, s3 = call(left_body, [slots, piece], [ext, late, q_left, docs], scores, alias=0)
    r3 = ring(s3, 3)
    cache = jax.ShapeDtypeStruct((rows + 2 * CH, 256), bf)
    s0, key_cache, value_cache = call(
        own_tile_body,
        [piece, cache, cache],
        [ext, late, halo, from_right, q_own, docs],
        scores,
        owner=block_owner,
        scratch=[VM((rows + 2 * CH, 256), bf)] * 2 + [pltpu.SemaphoreType.DMA((2,))],
    )
    (context,) = call(
        join_body,
        [jax.ShapeDtypeStruct((CH, 2048), bf)],
        [s0, r1, r2, r3],
        scratch=[pltpu.SemaphoreType.DMA((4,))],
    )
    return (context, key_cache, value_cache)


def solution(mesh):
    return jax.shard_map(
        layer,
        mesh=mesh,
        in_specs=(
            P(("seq", "tp"), None),
            P(),
            P(None, "tp"),
            P(None, "tp"),
            P(None, "tp"),
            P("seq"),
            P("seq"),
        ),
        out_specs=(P(("seq", "tp"), None), P("seq", "tp"), P("seq", "tp")),
        check_vma=False,
    )
```

```python
import jax
import jax.numpy as jnp
from jax import lax
from jax.experimental import pallas as pl
from jax.experimental.pallas import tpu as pltpu
from jax.sharding import PartitionSpec as P


HD = 128
EPS = 1e-05
ROPE_BASE = 500000.0
CH = 128
VM = pltpu.MemorySpace.VMEM
HB = pltpu.MemorySpace.HBM


def ring(array, by):
    n = lax.axis_size("tp")
    return lax.ppermute(array, "tp", [(i, (i + by) % n) for i in range(n)])


def across(array, moves):
    homes, n = lax.axis_size("seq"), lax.axis_size("tp")
    pairs = [(h * n + t, (h + by) * n + t) for h in range(homes) for t, by in moves.items() if 0 <= h + by < homes]
    return lax.ppermute(array, ("seq", "tp"), pairs)


def swap(array, first):
    homes = lax.axis_size("seq")
    pairs = [p for h in range(first, homes - 1, 2) for p in ((h, h + 1), (h + 1, h))]
    return lax.ppermute(array, "seq", pairs)


def spots():
    me, home = lax.axis_index("tp"), lax.axis_index("seq")
    return [lax.rem(me + k, 4) for k in (0, 3, 1, 2)] + [home]


def vmem(x):
    return pltpu.with_memory_space_constraint(x, VM)


def call(body, outs, arrays, flops=0, owner=None, alias=None, scratch=()):
    smem = pl.BlockSpec(memory_space=pltpu.SMEM)
    inside = pl.BlockSpec(memory_space=VM)
    lead = [] if owner is None else [owner]
    moved = sum(x.size * x.dtype.itemsize for x in arrays)
    return pl.pallas_call(
        body,
        out_shape=[o if isinstance(o, jax.ShapeDtypeStruct) else VM(o, jnp.bfloat16) for o in outs],
        in_specs=[smem] * len(lead) + [inside] * len(arrays),
        out_specs=[
            pl.BlockSpec(memory_space=HB) if isinstance(o, jax.ShapeDtypeStruct) else inside for o in outs
        ],
        scratch_shapes=list(scratch),
        input_output_aliases={} if alias is None else {len(lead) + alias: 0},
        compiler_params=pltpu.CompilerParams(vmem_limit_bytes=12 << 20),
        cost_estimate=pl.CostEstimate(flops=flops, bytes_accessed=moved, transcendentals=0),
    )(*lead, *[vmem(x) for x in arrays])


def normalize(x, gain):
    wide = x.astype(jnp.float32)
    inverse = lax.rsqrt(jnp.mean(wide * wide, axis=1, keepdims=True) + EPS)
    return (wide * inverse * gain).astype(jnp.bfloat16)


def rotate(x, cosine, sine):
    heads = x.shape[1] // HD
    parts = []
    for i in range(heads):
        one = x[:, i * HD : (i + 1) * HD]
        parts.append((one * cosine + pltpu.roll(one, HD // 2, 1) * sine).astype(jnp.bfloat16))
    return parts


def dot(a, b):
    return jnp.dot(a, b, preferred_element_type=jnp.float32)


def project_kv(normed, wk, wv, cosine, sine):
    keys = rotate(dot(normed, wk[...]), cosine, sine)
    values = dot(normed, wv[...]).astype(jnp.bfloat16)
    return keys, values


def project_q(normed, wq, cosine, sine):
    parts = []
    for i in range(wq.shape[1] // 256):
        parts += rotate(dot(normed, wq[:, i * 256 : (i + 1) * 256]), cosine, sine)
    return parts


def run(copies):
    for copy in copies:
        copy.start()
    for copy in copies:
        copy.wait()


def weights_body(wq, wk, wv, after, wq_out, wk_out, wv_out, sems):
    run([pltpu.make_async_copy(w, out, sems.at[i]) for i, (w, out) in enumerate(((wq, wq_out), (wk, wk_out), (wv, wv_out)))])


def chunk_rows(at):
    return pl.ds(pl.multiple_of(at * CH, CH), CH)


def half_rows(at, offset):
    return pl.ds(pl.multiple_of(at * CH + offset, CH // 2), CH // 2)


def normalize_all(pieces, gain):
    return jnp.concatenate([normalize(piece[...], gain[...]) for piece in pieces], axis=0)


def put(ref, index, rows, parts):
    for i, part in enumerate(parts):
        ref[index, :, i * HD : (i + 1) * HD] = part[rows]


def kv_parts(normed, wk, wv, cosine, sine):
    keys, values = project_kv(normed, wk, wv, cosine, sine)
    return [*keys, values[:, :HD], values[:, HD:]]


def own_body(xa, xb, gain, wq, wk, wv, cosines, sines, ext, q_out):
    own = spots()[0]
    rows = chunk_rows(own)
    normed = normalize_all((xa, xb), gain)
    put(ext, 2 + own, slice(None), kv_parts(normed, wk, wv, cosines[rows], sines[rows]))
    for i, part in enumerate(project_q(normed, wq, cosines[rows], sines[rows])):
        q_out[:, i * HD : (i + 1) * HD] = part


def owned_part(part, live):
    return jnp.where(live, part, jnp.zeros_like(part))


def near_body(ext_in, la, rb, gain, wq, wk, wv, cosines, sines, ext, q_out):
    _, left, right, _, _ = spots()
    half = CH // 2
    first, second = half_rows(left, 0), half_rows(right, half)
    cosine = jnp.concatenate([cosines[first], cosines[second]], axis=0)
    sine = jnp.concatenate([sines[first], sines[second]], axis=0)
    normed = normalize_all((la, rb), gain)
    for i, part in enumerate(kv_parts(normed, wk, wv, cosine, sine)):
        ext[2 + left, 0:half, i * HD : (i + 1) * HD] = part[:half]
        ext[2 + right, half:CH, i * HD : (i + 1) * HD] = part[half:]
    for i, part in enumerate(project_q(normed, wq, cosine, sine)):
        q_out[:, i * HD : (i + 1) * HD] = part


def rest_turns(cosines, sines):
    _, left, right, _, _ = spots()
    half = CH // 2
    first, second = half_rows(right, 0), half_rows(left, half)
    cosine = jnp.concatenate([cosines[first], cosines[second]], axis=0)
    sine = jnp.concatenate([sines[first], sines[second]], axis=0)
    return cosine, sine


def rest_body(owner, ext_in, ra, lb, gain, wk, wv, cosines, sines, ext, normed_out, inside_out, outside_out):
    _, left, right, _, home = spots()
    half = CH // 2
    normed = normalize_all((ra, lb), gain)
    normed_out[...] = normed
    for i, part in enumerate(kv_parts(normed, wk, wv, *rest_turns(cosines, sines))):
        ext[2 + right, 0:half, i * HD : (i + 1) * HD] = part[:half]
        ext[2 + left, half:CH, i * HD : (i + 1) * HD] = part[half:]
    count = jnp.int32(0)
    for j in range(4):
        count += (owner[12 + j] == home + 1).astype(jnp.int32)

    def fill(to_right, to_left):
        to_right[0:CH] = ext[4]
        to_right[CH : 2 * CH] = ext[5]
        to_right[2 * CH :] = jnp.full((16, 512), count.astype(jnp.float32), jnp.float32).astype(jnp.bfloat16)
        for j in range(4):
            to_left[j * 32 : (j + 1) * 32] = owned_part(ext[2, j * 32 : (j + 1) * 32], owner[j] == home - 1)

    @pl.when(lax.rem(home, 2) == 0)
    def _():
        fill(inside_out, outside_out)

    @pl.when(lax.rem(home, 2) == 1)
    def _():
        fill(outside_out, inside_out)


def rest_q_body(normed, wq, cosines, sines, q_out):
    for i, part in enumerate(project_q(normed[...], wq, *rest_turns(cosines, sines))):
        q_out[:, i * HD : (i + 1) * HD] = part


def attend(tile, q, ext, docs):
    window = 3 * CH
    doc = docs[chunk_rows(tile), 0:1]
    key_row = lax.broadcasted_iota(jnp.int32, (CH, window), 1) + (tile - 2) * CH
    row = lax.broadcasted_iota(jnp.int32, (CH, window), 0) + tile * CH
    allowed = (key_row >= doc) & (key_row <= row)
    allowed = jnp.concatenate([allowed, allowed], axis=0)
    near = ext[pl.ds(tile, 3)].reshape(window, 512)
    outs = []
    for g in range(2):
        pair = jnp.concatenate(q[2 * g : 2 * g + 2], axis=0)
        keys, values = near[:, g * HD : (g + 1) * HD], near[:, (2 + g) * HD : (3 + g) * HD]
        scores = lax.dot_general(pair, keys, (((1,), (1,)), ((), ())), preferred_element_type=jnp.float32) * HD ** (-0.5)
        scores = jnp.where(allowed, scores, -jnp.inf)
        highest = jnp.max(scores, axis=1, keepdims=True)
        weights = jnp.exp(scores - highest)
        weights = (weights * (1.0 / jnp.sum(weights, axis=1, keepdims=True))).astype(jnp.bfloat16)
        blended = dot(weights, values).astype(jnp.bfloat16)
        outs += [blended[:CH], blended[CH:]]
    return outs


def heads(q):
    return [q[:, i * HD : (i + 1) * HD] for i in range(4)]


def emit(out, parts):
    for i, part in enumerate(parts):
        out[:, i * HD : (i + 1) * HD] = part


def first_body(ext_in, inner, outer, q_near, q_rest, docs, ext, out):
    _, _, right, _, home = spots()
    half = CH // 2

    @pl.when(lax.rem(home, 2) == 1)
    def _():
        ext[0] = inner[0:CH]
        ext[1] = inner[CH : 2 * CH]

    @pl.when(lax.rem(home, 2) == 0)
    def _():
        ext[0] = outer[0:CH]
        ext[1] = outer[CH : 2 * CH]

    q = jnp.concatenate([q_rest[0:half], q_near[half:CH]], axis=0)
    emit(out, attend(right, heads(q), ext, docs))


def last_body(owner, ext_in, xa, xb, gain, wk, wv, cosines, sines, ext, normed_out, late_out):
    _, _, _, far, home = spots()
    rows = chunk_rows(far)
    normed = normalize_all((xa, xb), gain)
    normed_out[...] = normed
    parts = kv_parts(normed, wk, wv, cosines[rows], sines[rows])
    put(ext, 2 + far, slice(None), parts)
    for j in range(4):
        live = (far > 0) | (owner[j] == home - 1)
        for i, part in enumerate(parts):
            late_out[j * 32 : (j + 1) * 32, i * HD : (i + 1) * HD] = owned_part(part[j * 32 : (j + 1) * 32], live)


def far_body(ext_in, normed, wq, cosines, sines, docs, ext, out):
    far = spots()[3]
    rows = chunk_rows(far)
    q = project_q(normed[...], wq, cosines[rows], sines[rows])
    emit(out, attend(far, q, ext, docs))


def left_body(ext_in, late, q_near, q_rest, docs, ext, out):
    own, left, _, _, _ = spots()
    half = CH // 2

    @pl.when(own < 2)
    def _():
        ext[own] = late[...]

    q = jnp.concatenate([q_near[0:half], q_rest[half:CH]], axis=0)
    emit(out, attend(left, heads(q), ext, docs))


def own_tile_body(owner, ext, late, inner, outer, q, docs, out, key_out, value_out, keys, values, sems):
    own, _, _, _, home = spots()

    def put_cache(row, part):
        keys[row : row + part.shape[0]] = part[:, 0:256]
        values[row : row + part.shape[0]] = part[:, 256:512]

    count = jnp.where(lax.rem(home, 2) == 1, inner[2 * CH : 2 * CH + 1, :], outer[2 * CH : 2 * CH + 1, :]).astype(jnp.float32)
    for j in range(4):
        part = ext[1, j * 32 : (j + 1) * 32]
        put_cache(j * 32, jnp.where(count > 3.5 - j, part.astype(jnp.float32), 0.0).astype(jnp.bfloat16))
    for j in range(16):
        part = ext[2 + j // 4, (j % 4) * 32 : (j % 4 + 1) * 32]
        put_cache(CH + j * 32, owned_part(part, owner[j] == home))

    @pl.when(own == 2)
    def _():
        put_cache(5 * CH, late[...])

    @pl.when((own != 2) & (lax.rem(home, 2) == 0))
    def _():
        put_cache(5 * CH, inner[0:CH])

    @pl.when((own != 2) & (lax.rem(home, 2) == 1))
    def _():
        put_cache(5 * CH, outer[0:CH])

    copies = [
        pltpu.make_async_copy(keys, key_out, sems.at[0]),
        pltpu.make_async_copy(values, value_out, sems.at[1]),
    ]
    for copy in copies:
        copy.start()
    emit(out, attend(own, heads(q), ext, docs))
    for copy in copies:
        copy.wait()


def join_body(s0, r1, r2, r3, out, sems):
    own, left, right, far, _ = spots()
    copies = []
    for i, (piece, at) in enumerate(((s0, own), (r1, left), (r2, far), (r3, right))):
        columns = pl.ds(pl.multiple_of(at * 512, 512), 512)
        copies.append(pltpu.make_async_copy(piece, out.at[:, columns], sems.at[i]))
    run(copies)


def layer(hidden, norm_gain, w_query, w_key, w_value, doc_start, block_owner):
    home = lax.axis_index("seq")
    rows = doc_start.shape[0]
    bf = jnp.bfloat16
    inside = pl.BlockSpec(memory_space=VM)
    outside = pl.BlockSpec(memory_space=pltpu.MemorySpace.HBM)
    wide = hidden.shape[1]

    def mover(body, outs, arrays, size):
        return pl.pallas_call(
            body,
            out_shape=[VM(s, bf) for s in outs],
            in_specs=[outside if x.size > CH * wide // 2 else pl.BlockSpec(memory_space=pl.ANY) for x in arrays],
            out_specs=[inside] * len(outs),
            scratch_shapes=[pltpu.SemaphoreType.DMA((len(outs),))],
            compiler_params=pltpu.CompilerParams(vmem_limit_bytes=2 << 20),
            cost_estimate=pl.CostEstimate(flops=0, bytes_accessed=size, transcendentals=0),
        )(*[pltpu.with_memory_space_constraint(x, HB) if x.size > CH * wide // 2 else x for x in arrays])

    own_a, own_b = hidden[: CH // 2], hidden[CH // 2 :]
    left_a = ring(own_a, 1)
    right_b = ring(own_b, -1)
    left_b = ring(own_b, 1)
    right_a = ring(own_a, -1)
    far_a = ring(left_a, 1)
    far_b = ring(right_b, -1)
    row_number = home * rows + jnp.arange(rows, dtype=jnp.int32)
    lane = jnp.arange(HD, dtype=jnp.float32)
    lane_half = jnp.where(lane < HD // 2, lane, lane - HD // 2)
    frequency = jnp.power(ROPE_BASE, -lane_half * (2.0 / HD))
    angles = (row_number - doc_start).astype(jnp.float32)[:, None] * frequency[None, :]
    cosines, sines = jnp.cos(angles), jnp.where(lane < HD // 2, -1.0, 1.0)[None, :] * jnp.sin(angles)
    docs = jnp.broadcast_to((doc_start - home * rows)[:, None], (rows, HD))

    w_query, w_key, w_value = mover(
        weights_body, [w.shape for w in (w_query, w_key, w_value)], [w_query, w_key, w_value, docs], 16 << 20
    )
    gain = norm_gain[None, :]
    flops = 2 * CH * wide * 1024
    scores = 8 * 2 * CH * 3 * CH * HD
    slots = (6, CH, 512)
    piece = (CH, 512)
    ext, q_own = call(own_body, [slots, piece], [own_a, own_b, gain, w_query, w_key, w_value, cosines, sines], flops)
    ext, q_near = call(
        near_body,
        [slots, piece],
        [ext, left_a, right_b, gain, w_query, w_key, w_value, cosines, sines],
        flops,
        alias=0,
    )
    ext, normed, inside_out, outside_out = call(
        rest_body,
        [slots, (CH, wide), (2 * CH + 16, 512), (2 * CH + 16, 512)],
        [ext, right_a, left_b, gain, w_key, w_value, cosines, sines],
        flops // 2,
        owner=block_owner,
        alias=0,
    )
    outer = swap(outside_out, 1)
    inner = swap(inside_out, 0)
    (q_rest,) = call(rest_q_body, [piece], [normed, w_query, cosines, sines], flops // 2)
    ext, normed, far = call(
        last_body,
        [slots, (CH, wide), piece],
        [ext, far_a, far_b, gain, w_key, w_value, cosines, sines],
        flops // 2,
        owner=block_owner,
        alias=0,
    )
    late = across(far, {0: 1, 1: 1, 2: -1})
    ext, s1 = call(first_body, [slots, piece], [ext, inner, outer, q_near, q_rest, docs], scores, alias=0)
    r1 = ring(s1, 1)
    ext, s2 = call(far_body, [slots, piece], [ext, normed, w_query, cosines, sines, docs], flops, alias=0)
    r2 = ring(s2, 2)
    ext, s3 = call(left_body, [slots, piece], [ext, late, q_near, q_rest, docs], scores, alias=0)
    r3 = ring(s3, 3)
    cache = jax.ShapeDtypeStruct((rows + 2 * CH, 256), bf)
    s0, key_cache, value_cache = call(
        own_tile_body,
        [piece, cache, cache],
        [ext, late, inner, outer, q_own, docs],
        scores,
        owner=block_owner,
        scratch=[VM((rows + 2 * CH, 256), bf)] * 2 + [pltpu.SemaphoreType.DMA((2,))],
    )
    (context,) = call(
        join_body,
        [jax.ShapeDtypeStruct((CH, 2048), bf)],
        [s0, r1, r2, r3],
        scratch=[pltpu.SemaphoreType.DMA((4,))],
    )
    return (context, key_cache, value_cache)


def solution(mesh):
    return jax.shard_map(
        layer,
        mesh=mesh,
        in_specs=(
            P(("seq", "tp"), None),
            P(),
            P(None, "tp"),
            P(None, "tp"),
            P(None, "tp"),
            P("seq"),
            P("seq"),
        ),
        out_specs=(P(("seq", "tp"), None), P("seq", "tp"), P("seq", "tp")),
        check_vma=False,
    )
```

```python
import jax
import jax.numpy as jnp
from jax import lax
from jax.experimental import pallas as pl
from jax.experimental.pallas import tpu as pltpu
from jax.sharding import PartitionSpec as P


HD = 128
EPS = 1e-05
ROPE_BASE = 500000.0
CH = 128
BLK = 32
VM = pltpu.MemorySpace.VMEM
HB = pltpu.MemorySpace.HBM


def ring(array, by):
    n = lax.axis_size("tp")
    return lax.ppermute(array, "tp", [(i, (i + by) % n) for i in range(n)])


def across(array, moves):
    homes, n = lax.axis_size("seq"), lax.axis_size("tp")
    pairs = [(h * n + t, (h + by) * n + t) for h in range(homes) for t, by in moves.items() if 0 <= h + by < homes]
    return lax.ppermute(array, ("seq", "tp"), pairs)


def swap(array, first):
    homes = lax.axis_size("seq")
    pairs = [p for h in range(first, homes - 1, 2) for p in ((h, h + 1), (h + 1, h))]
    return lax.ppermute(array, "seq", pairs)


def spots():
    me, home = lax.axis_index("tp"), lax.axis_index("seq")
    return [lax.rem(me + k, 4) for k in (0, 3, 1, 2)] + [home]


def vmem(x):
    return pltpu.with_memory_space_constraint(x, VM)


def call(body, outs, arrays, flops=0, alias=None, scratch=()):
    inside = pl.BlockSpec(memory_space=VM)
    moved = sum(x.size * x.dtype.itemsize for x in arrays)
    return pl.pallas_call(
        body,
        out_shape=[o if isinstance(o, jax.ShapeDtypeStruct) else VM(o, jnp.bfloat16) for o in outs],
        in_specs=[inside] * len(arrays),
        out_specs=[
            pl.BlockSpec(memory_space=HB) if isinstance(o, jax.ShapeDtypeStruct) else inside for o in outs
        ],
        scratch_shapes=list(scratch),
        input_output_aliases={} if alias is None else {alias: 0},
        compiler_params=pltpu.CompilerParams(vmem_limit_bytes=12 << 20),
        cost_estimate=pl.CostEstimate(flops=flops, bytes_accessed=moved, transcendentals=0),
    )(*[vmem(x) for x in arrays])


def normalize(x, gain):
    wide = x.astype(jnp.float32)
    inverse = lax.rsqrt(jnp.mean(wide * wide, axis=1, keepdims=True) + EPS)
    return (wide * inverse * gain).astype(jnp.bfloat16)


def rotate(x, cosine, sine):
    heads = x.shape[1] // HD
    parts = []
    for i in range(heads):
        one = x[:, i * HD : (i + 1) * HD]
        parts.append((one * cosine + pltpu.roll(one, HD // 2, 1) * sine).astype(jnp.bfloat16))
    return parts


def dot(a, b):
    return jnp.dot(a, b, preferred_element_type=jnp.float32)


def project_kv(normed, wk, wv, cosine, sine):
    keys = rotate(dot(normed, wk[...]), cosine, sine)
    values = dot(normed, wv[...]).astype(jnp.bfloat16)
    return keys, values


def project_q(normed, wq, cosine, sine):
    parts = []
    for i in range(wq.shape[1] // 256):
        parts += rotate(dot(normed, wq[:, i * 256 : (i + 1) * 256]), cosine, sine)
    return parts


def run(copies):
    for copy in copies:
        copy.start()
    for copy in copies:
        copy.wait()


def weights_body(wq, wk, wv, after, after_too, wq_out, wk_out, wv_out, sems):
    run([pltpu.make_async_copy(w, out, sems.at[i]) for i, (w, out) in enumerate(((wq, wq_out), (wk, wk_out), (wv, wv_out)))])


def chunk_rows(at):
    return pl.ds(pl.multiple_of(at * CH, CH), CH)


def half_rows(at, offset):
    return pl.ds(pl.multiple_of(at * CH + offset, CH // 2), CH // 2)


def normalize_all(pieces, gain):
    return jnp.concatenate([normalize(piece[...], gain[...]) for piece in pieces], axis=0)


def put(ref, index, rows, parts):
    for i, part in enumerate(parts):
        ref[index, :, i * HD : (i + 1) * HD] = part[rows]


def kv_parts(normed, wk, wv, cosine, sine):
    keys, values = project_kv(normed, wk, wv, cosine, sine)
    return [*keys, values[:, :HD], values[:, HD:]]


def own_body(xa, xb, gain, wq, wk, wv, cosines, sines, ext, q_out):
    own = spots()[0]
    rows = chunk_rows(own)
    normed = normalize_all((xa, xb), gain)
    put(ext, 2 + own, slice(None), kv_parts(normed, wk, wv, cosines[rows], sines[rows]))
    for i, part in enumerate(project_q(normed, wq, cosines[rows], sines[rows])):
        q_out[:, i * HD : (i + 1) * HD] = part


def owned_part(part, live):
    live = jnp.concatenate([live] * (part.shape[1] // HD), axis=1)
    return jnp.where(live, part.astype(jnp.float32), 0.0).astype(jnp.bfloat16)


def near_body(ext_in, la, rb, gain, wq, wk, wv, cosines, sines, ext, q_out):
    _, left, right, _, _ = spots()
    half = CH // 2
    first, second = half_rows(left, 0), half_rows(right, half)
    cosine = jnp.concatenate([cosines[first], cosines[second]], axis=0)
    sine = jnp.concatenate([sines[first], sines[second]], axis=0)
    normed = normalize_all((la, rb), gain)
    for i, part in enumerate(kv_parts(normed, wk, wv, cosine, sine)):
        ext[2 + left, 0:half, i * HD : (i + 1) * HD] = part[:half]
        ext[2 + right, half:CH, i * HD : (i + 1) * HD] = part[half:]
    for i, part in enumerate(project_q(normed, wq, cosine, sine)):
        q_out[:, i * HD : (i + 1) * HD] = part


def rest_turns(cosines, sines):
    _, left, right, _, _ = spots()
    half = CH // 2
    first, second = half_rows(right, 0), half_rows(left, half)
    cosine = jnp.concatenate([cosines[first], cosines[second]], axis=0)
    sine = jnp.concatenate([sines[first], sines[second]], axis=0)
    return cosine, sine


def rest_body(ext_in, owners, ra, lb, gain, wk, wv, cosines, sines, ext, normed_out, inside_out, outside_out):
    _, left, right, _, home = spots()
    half = CH // 2
    normed = normalize_all((ra, lb), gain)
    normed_out[...] = normed
    for i, part in enumerate(kv_parts(normed, wk, wv, *rest_turns(cosines, sines))):
        ext[2 + right, 0:half, i * HD : (i + 1) * HD] = part[:half]
        ext[2 + left, half:CH, i * HD : (i + 1) * HD] = part[half:]
    count = jnp.sum(jnp.where(owners[3 * CH :] == home + 1, 1.0 / 32, 0.0), axis=0, keepdims=True)
    count = jnp.broadcast_to(jnp.concatenate([count] * 4, axis=1), (16, 512)).astype(jnp.bfloat16)

    def fill(to_right, to_left):
        to_right[0:CH] = ext[4]
        to_right[CH : 2 * CH] = ext[5]
        to_right[2 * CH :] = count
        to_left[0:CH] = owned_part(ext[2], owners[0:CH] == home - 1)

    @pl.when(lax.rem(home, 2) == 0)
    def _():
        fill(inside_out, outside_out)

    @pl.when(lax.rem(home, 2) == 1)
    def _():
        fill(outside_out, inside_out)


def rest_q_body(normed, wq, cosines, sines, q_out):
    for i, part in enumerate(project_q(normed[...], wq, *rest_turns(cosines, sines))):
        q_out[:, i * HD : (i + 1) * HD] = part


def attend(tile, q, ext, docs):
    window = 3 * CH
    doc = docs[chunk_rows(tile), 0:1]
    key_row = lax.broadcasted_iota(jnp.int32, (CH, window), 1) + (tile - 2) * CH
    row = lax.broadcasted_iota(jnp.int32, (CH, window), 0) + tile * CH
    allowed = (key_row >= doc) & (key_row <= row)
    allowed = jnp.concatenate([allowed, allowed], axis=0)
    near = ext[pl.ds(tile, 3)].reshape(window, 512)
    outs = []
    for g in range(2):
        pair = jnp.concatenate(q[2 * g : 2 * g + 2], axis=0)
        keys, values = near[:, g * HD : (g + 1) * HD], near[:, (2 + g) * HD : (3 + g) * HD]
        scores = lax.dot_general(pair, keys, (((1,), (1,)), ((), ())), preferred_element_type=jnp.float32) * HD ** (-0.5)
        scores = jnp.where(allowed, scores, -jnp.inf)
        highest = jnp.max(scores, axis=1, keepdims=True)
        weights = jnp.exp(scores - highest)
        weights = (weights * (1.0 / jnp.sum(weights, axis=1, keepdims=True))).astype(jnp.bfloat16)
        blended = dot(weights, values).astype(jnp.bfloat16)
        outs += [blended[:CH], blended[CH:]]
    return outs


def heads(q):
    return [q[:, i * HD : (i + 1) * HD] for i in range(4)]


def emit(out, parts):
    for i, part in enumerate(parts):
        out[:, i * HD : (i + 1) * HD] = part


def far_body(ext_in, inner, outer, normed, wq, cosines, sines, docs, ext, out):
    _, _, _, far, home = spots()
    rows = chunk_rows(far)

    @pl.when(lax.rem(home, 2) == 1)
    def _():
        ext[0] = inner[0:CH]
        ext[1] = inner[CH : 2 * CH]

    @pl.when(lax.rem(home, 2) == 0)
    def _():
        ext[0] = outer[0:CH]
        ext[1] = outer[CH : 2 * CH]

    q = project_q(normed[...], wq, cosines[rows], sines[rows])
    emit(out, attend(far, q, ext, docs))


def last_body(ext_in, owners, xa, xb, gain, wk, wv, cosines, sines, ext, normed_out, late_out):
    _, _, _, far, home = spots()
    rows = chunk_rows(far)
    normed = normalize_all((xa, xb), gain)
    normed_out[...] = normed
    parts = kv_parts(normed, wk, wv, cosines[rows], sines[rows])
    put(ext, 2 + far, slice(None), parts)
    live = (owners[0:CH] == home - 1) | (far > 0)
    for i, part in enumerate(parts):
        late_out[:, i * HD : (i + 1) * HD] = owned_part(part, live)


def first_body(ext_in, q_near, q_rest, docs, ext, out):
    right = spots()[2]
    half = CH // 2
    q = jnp.concatenate([q_rest[0:half], q_near[half:CH]], axis=0)
    emit(out, attend(right, heads(q), ext, docs))


def left_body(ext_in, late, q_near, q_rest, docs, ext, out):
    own, left, _, _, _ = spots()
    half = CH // 2

    @pl.when(own < 2)
    def _():
        ext[own] = late[...]

    q = jnp.concatenate([q_near[0:half], q_rest[half:CH]], axis=0)
    emit(out, attend(left, heads(q), ext, docs))


def own_tile_body(ext, owners, late, inner, outer, q, docs, out, key_out, value_out, keys, values, sems):
    own, _, _, _, home = spots()

    def put_cache(row, part):
        keys[row : row + part.shape[0]] = part[:, 0:256]
        values[row : row + part.shape[0]] = part[:, 256:512]

    count = jnp.where(lax.rem(home, 2) == 1, inner[2 * CH : 2 * CH + 1, :], outer[2 * CH : 2 * CH + 1, :]).astype(jnp.float32)
    for j in range(4):
        part = ext[1, j * 32 : (j + 1) * 32]
        put_cache(j * 32, jnp.where(count > 3.5 - j, part.astype(jnp.float32), 0.0).astype(jnp.bfloat16))
    for j in range(4):
        put_cache(CH + j * CH, owned_part(ext[2 + j], owners[j * CH : (j + 1) * CH] == home))

    @pl.when(own == 2)
    def _():
        put_cache(5 * CH, late[...])

    @pl.when((own != 2) & (lax.rem(home, 2) == 0))
    def _():
        put_cache(5 * CH, inner[0:CH])

    @pl.when((own != 2) & (lax.rem(home, 2) == 1))
    def _():
        put_cache(5 * CH, outer[0:CH])

    copies = [
        pltpu.make_async_copy(keys, key_out, sems.at[0]),
        pltpu.make_async_copy(values, value_out, sems.at[1]),
    ]
    for copy in copies:
        copy.start()
    emit(out, attend(own, heads(q), ext, docs))
    for copy in copies:
        copy.wait()


def join_body(s0, r1, r2, r3, out, sems):
    own, left, right, far, _ = spots()
    copies = []
    for i, (piece, at) in enumerate(((s0, own), (r1, left), (r2, far), (r3, right))):
        columns = pl.ds(pl.multiple_of(at * 512, 512), 512)
        copies.append(pltpu.make_async_copy(piece, out.at[:, columns], sems.at[i]))
    run(copies)


def layer(hidden, norm_gain, w_query, w_key, w_value, doc_start, block_owner):
    home = lax.axis_index("seq")
    rows = doc_start.shape[0]
    bf = jnp.bfloat16
    inside = pl.BlockSpec(memory_space=VM)
    outside = pl.BlockSpec(memory_space=pltpu.MemorySpace.HBM)
    wide = hidden.shape[1]

    def mover(body, outs, arrays, size):
        return pl.pallas_call(
            body,
            out_shape=[VM(s, bf) for s in outs],
            in_specs=[outside if x.size > CH * wide // 2 else pl.BlockSpec(memory_space=pl.ANY) for x in arrays],
            out_specs=[inside] * len(outs),
            scratch_shapes=[pltpu.SemaphoreType.DMA((len(outs),))],
            compiler_params=pltpu.CompilerParams(vmem_limit_bytes=2 << 20),
            cost_estimate=pl.CostEstimate(flops=0, bytes_accessed=size, transcendentals=0),
        )(*[pltpu.with_memory_space_constraint(x, HB) if x.size > CH * wide // 2 else x for x in arrays])

    own_a, own_b = hidden[: CH // 2], hidden[CH // 2 :]
    left_a = ring(own_a, 1)
    right_b = ring(own_b, -1)
    left_b = ring(own_b, 1)
    right_a = ring(own_a, -1)
    far_a = ring(left_a, 1)
    far_b = ring(right_b, -1)
    row_number = home * rows + jnp.arange(rows, dtype=jnp.int32)
    lane = jnp.arange(HD, dtype=jnp.float32)
    lane_half = jnp.where(lane < HD // 2, lane, lane - HD // 2)
    frequency = jnp.power(ROPE_BASE, -lane_half * (2.0 / HD))
    angles = (row_number - doc_start).astype(jnp.float32)[:, None] * frequency[None, :]
    cosines, sines = jnp.cos(angles), jnp.where(lane < HD // 2, -1.0, 1.0)[None, :] * jnp.sin(angles)
    docs = jnp.broadcast_to((doc_start - home * rows)[:, None], (rows, HD))
    owners = jnp.broadcast_to(block_owner[:, None, None], (block_owner.shape[0], BLK, HD)).reshape(rows, HD)

    w_query, w_key, w_value = mover(
        weights_body, [w.shape for w in (w_query, w_key, w_value)], [w_query, w_key, w_value, docs, owners], 16 << 20
    )
    gain = norm_gain[None, :]
    flops = 2 * CH * wide * 1024
    scores = 8 * 2 * CH * 3 * CH * HD
    slots = (6, CH, 512)
    piece = (CH, 512)
    ext, q_own = call(own_body, [slots, piece], [own_a, own_b, gain, w_query, w_key, w_value, cosines, sines], flops)
    ext, q_near = call(
        near_body,
        [slots, piece],
        [ext, left_a, right_b, gain, w_query, w_key, w_value, cosines, sines],
        flops,
        alias=0,
    )
    ext, normed, inside_out, outside_out = call(
        rest_body,
        [slots, (CH, wide), (2 * CH + 16, 512), (2 * CH + 16, 512)],
        [ext, owners, right_a, left_b, gain, w_key, w_value, cosines, sines],
        flops // 2,
        alias=0,
    )
    outer = swap(outside_out, 1)
    inner = swap(inside_out, 0)
    (q_rest,) = call(rest_q_body, [piece], [normed, w_query, cosines, sines], flops // 2)
    ext, normed, far = call(
        last_body,
        [slots, (CH, wide), piece],
        [ext, owners, far_a, far_b, gain, w_key, w_value, cosines, sines],
        flops // 2,
        alias=0,
    )
    late = across(far, {0: 1, 1: 1, 2: -1})
    ext, s2 = call(far_body, [slots, piece], [ext, inner, outer, normed, w_query, cosines, sines, docs], flops, alias=0)
    r2 = ring(s2, 2)
    ext, s1 = call(first_body, [slots, piece], [ext, q_near, q_rest, docs], scores, alias=0)
    r1 = ring(s1, 1)
    ext, s3 = call(left_body, [slots, piece], [ext, late, q_near, q_rest, docs], scores, alias=0)
    r3 = ring(s3, 3)
    cache = jax.ShapeDtypeStruct((rows + 2 * CH, 256), bf)
    s0, key_cache, value_cache = call(
        own_tile_body,
        [piece, cache, cache],
        [ext, owners, late, inner, outer, q_own, docs],
        scores,
        scratch=[VM((rows + 2 * CH, 256), bf)] * 2 + [pltpu.SemaphoreType.DMA((2,))],
    )
    (context,) = call(
        join_body,
        [jax.ShapeDtypeStruct((CH, 2048), bf)],
        [s0, r1, r2, r3],
        scratch=[pltpu.SemaphoreType.DMA((4,))],
    )
    return (context, key_cache, value_cache)


def solution(mesh):
    return jax.shard_map(
        layer,
        mesh=mesh,
        in_specs=(
            P(("seq", "tp"), None),
            P(),
            P(None, "tp"),
            P(None, "tp"),
            P(None, "tp"),
            P("seq"),
            P("seq"),
        ),
        out_specs=(P(("seq", "tp"), None), P("seq", "tp"), P("seq", "tp")),
        check_vma=False,
    )
```

```python
import jax
import jax.numpy as jnp
from jax import lax
from jax.experimental import pallas as pl
from jax.experimental.pallas import tpu as pltpu
from jax.sharding import PartitionSpec as P


HD = 128
EPS = 1e-05
ROPE_BASE = 500000.0
CH = 128
BLK = 32
VM = pltpu.MemorySpace.VMEM
HB = pltpu.MemorySpace.HBM


def ring(array, by):
    n = lax.axis_size("tp")
    return lax.ppermute(array, "tp", [(i, (i + by) % n) for i in range(n)])


def across(array, moves):
    homes, n = lax.axis_size("seq"), lax.axis_size("tp")
    pairs = [(h * n + t, (h + by) * n + t) for h in range(homes) for t, by in moves.items() if 0 <= h + by < homes]
    return lax.ppermute(array, ("seq", "tp"), pairs)


def turn_of(array, parity):
    homes, n = lax.axis_size("seq"), lax.axis_size("tp")
    pairs = [(h * n + t, h * n + (t + 1) % n) for h in range(parity, homes, 2) for t in range(n)]
    return lax.ppermute(array, ("seq", "tp"), pairs)


def swap(array, first):
    homes = lax.axis_size("seq")
    pairs = [p for h in range(first, homes - 1, 2) for p in ((h, h + 1), (h + 1, h))]
    return lax.ppermute(array, "seq", pairs)


def spots():
    me, home = lax.axis_index("tp"), lax.axis_index("seq")
    return [lax.rem(me + k, 4) for k in (0, 3, 1, 2)] + [home]


def vmem(x):
    return pltpu.with_memory_space_constraint(x, VM)


def call(body, outs, arrays, flops=0, alias=None, aliases=1, scratch=()):
    inside = pl.BlockSpec(memory_space=VM)
    moved = sum(x.size * x.dtype.itemsize for x in arrays)
    return pl.pallas_call(
        body,
        out_shape=[o if isinstance(o, jax.ShapeDtypeStruct) else VM(o, jnp.bfloat16) for o in outs],
        in_specs=[inside] * len(arrays),
        out_specs=[
            pl.BlockSpec(memory_space=HB) if isinstance(o, jax.ShapeDtypeStruct) else inside for o in outs
        ],
        scratch_shapes=list(scratch),
        input_output_aliases={} if alias is None else {alias + i: i for i in range(aliases)},
        compiler_params=pltpu.CompilerParams(vmem_limit_bytes=12 << 20),
        cost_estimate=pl.CostEstimate(flops=flops, bytes_accessed=moved, transcendentals=0),
    )(*[vmem(x) for x in arrays])


def normalize(x, gain):
    wide = x.astype(jnp.float32)
    inverse = lax.rsqrt(jnp.mean(wide * wide, axis=1, keepdims=True) + EPS)
    return (wide * inverse * gain).astype(jnp.bfloat16)


def rotate(x, cosine, sine):
    heads = x.shape[1] // HD
    parts = []
    for i in range(heads):
        one = x[:, i * HD : (i + 1) * HD]
        parts.append((one * cosine + pltpu.roll(one, HD // 2, 1) * sine).astype(jnp.bfloat16))
    return parts


def dot(a, b):
    return jnp.dot(a, b, preferred_element_type=jnp.float32)


def project_kv(normed, wk, wv, cosine, sine):
    keys = rotate(dot(normed, wk[...]), cosine, sine)
    values = dot(normed, wv[...]).astype(jnp.bfloat16)
    return keys, values


def project_q(normed, wq, cosine, sine):
    parts = []
    for i in range(wq.shape[1] // 256):
        parts += rotate(dot(normed, wq[:, i * 256 : (i + 1) * 256]), cosine, sine)
    return parts


def run(copies):
    for copy in copies:
        copy.start()
    for copy in copies:
        copy.wait()


def halves_body(hidden, a, b, sems):
    size = CH // 2
    run([pltpu.make_async_copy(hidden.at[i * size : (i + 1) * size], out, sems.at[i]) for i, out in enumerate((a, b))])


def weights_body(wq, wk, wv, after, after_too, wq_out, wk_out, wv_out, sems):
    run([pltpu.make_async_copy(w, out, sems.at[i]) for i, (w, out) in enumerate(((wq, wq_out), (wk, wk_out), (wv, wv_out)))])


def chunk_rows(at):
    return pl.ds(pl.multiple_of(at * CH, CH), CH)


def half_rows(at, offset):
    return pl.ds(pl.multiple_of(at * CH + offset, CH // 2), CH // 2)


def normalize_all(pieces, gain):
    return jnp.concatenate([normalize(piece[...], gain[...]) for piece in pieces], axis=0)


def put(ref, index, rows, parts):
    for i, part in enumerate(parts):
        ref[index, :, i * HD : (i + 1) * HD] = part[rows]


def kv_parts(normed, wk, wv, cosine, sine):
    keys, values = project_kv(normed, wk, wv, cosine, sine)
    return [*keys, values[:, :HD], values[:, HD:]]


def own_body(xa, xb, gain, wq, wk, wv, cosines, sines, ext, q_out):
    own = spots()[0]
    rows = chunk_rows(own)
    normed = normalize_all((xa, xb), gain)
    put(ext, 2 + own, slice(None), kv_parts(normed, wk, wv, cosines[rows], sines[rows]))
    for i, part in enumerate(project_q(normed, wq, cosines[rows], sines[rows])):
        q_out[:, i * HD : (i + 1) * HD] = part


def owned_part(part, live):
    live = jnp.concatenate([live] * (part.shape[1] // HD), axis=1)
    return jnp.where(live, part.astype(jnp.float32), 0.0).astype(jnp.bfloat16)


def near_body(ext_in, la, rb, gain, wq, wk, wv, cosines, sines, ext, q_out):
    _, left, right, _, _ = spots()
    half = CH // 2
    first, second = half_rows(left, 0), half_rows(right, half)
    cosine = jnp.concatenate([cosines[first], cosines[second]], axis=0)
    sine = jnp.concatenate([sines[first], sines[second]], axis=0)
    normed = normalize_all((la, rb), gain)
    for i, part in enumerate(kv_parts(normed, wk, wv, cosine, sine)):
        ext[2 + left, 0:half, i * HD : (i + 1) * HD] = part[:half]
        ext[2 + right, half:CH, i * HD : (i + 1) * HD] = part[half:]
    for i, part in enumerate(project_q(normed, wq, cosine, sine)):
        q_out[:, i * HD : (i + 1) * HD] = part


def rest_turns(cosines, sines):
    _, left, right, _, _ = spots()
    half = CH // 2
    first, second = half_rows(right, 0), half_rows(left, half)
    cosine = jnp.concatenate([cosines[first], cosines[second]], axis=0)
    sine = jnp.concatenate([sines[first], sines[second]], axis=0)
    return cosine, sine


def rest_body(ext_in, owners, ra, lb, gain, wk, wv, cosines, sines, ext, normed_out, inside_out, outside_out):
    _, left, right, _, home = spots()
    half = CH // 2
    normed = normalize_all((ra, lb), gain)
    normed_out[...] = normed
    for i, part in enumerate(kv_parts(normed, wk, wv, *rest_turns(cosines, sines))):
        ext[2 + right, 0:half, i * HD : (i + 1) * HD] = part[:half]
        ext[2 + left, half:CH, i * HD : (i + 1) * HD] = part[half:]
    count = jnp.sum(jnp.where(owners[3 * CH :] == home + 1, 1.0 / 32, 0.0), axis=0, keepdims=True)
    count = jnp.broadcast_to(jnp.concatenate([count] * 4, axis=1), (16, 512)).astype(jnp.bfloat16)

    def fill(to_right, to_left):
        to_right[0:CH] = ext[4]
        to_right[CH : 2 * CH] = ext[5]
        to_right[2 * CH :] = count
        to_left[0:CH] = owned_part(ext[2], owners[0:CH] == home - 1)

    @pl.when(lax.rem(home, 2) == 0)
    def _():
        fill(inside_out, outside_out)

    @pl.when(lax.rem(home, 2) == 1)
    def _():
        fill(outside_out, inside_out)


def rest_q_body(normed, wq, cosines, sines, q_out):
    for i, part in enumerate(project_q(normed[...], wq, *rest_turns(cosines, sines))):
        q_out[:, i * HD : (i + 1) * HD] = part


def attend(tile, q, ext, docs):
    window = 3 * CH
    doc = docs[chunk_rows(tile), 0:1]
    key_row = lax.broadcasted_iota(jnp.int32, (CH, window), 1) + (tile - 2) * CH
    row = lax.broadcasted_iota(jnp.int32, (CH, window), 0) + tile * CH
    allowed = (key_row >= doc) & (key_row <= row)
    allowed = jnp.concatenate([allowed, allowed], axis=0)
    near = ext[pl.ds(tile, 3)].reshape(window, 512)
    outs = []
    for g in range(2):
        pair = jnp.concatenate(q[2 * g : 2 * g + 2], axis=0)
        keys, values = near[:, g * HD : (g + 1) * HD], near[:, (2 + g) * HD : (3 + g) * HD]
        scores = lax.dot_general(pair, keys, (((1,), (1,)), ((), ())), preferred_element_type=jnp.float32) * HD ** (-0.5)
        scores = jnp.where(allowed, scores, -jnp.inf)
        highest = jnp.max(scores, axis=1, keepdims=True)
        weights = jnp.exp(scores - highest)
        weights = (weights * (1.0 / jnp.sum(weights, axis=1, keepdims=True))).astype(jnp.bfloat16)
        blended = dot(weights, values).astype(jnp.bfloat16)
        outs += [blended[:CH], blended[CH:]]
    return outs


def heads(q):
    return [q[:, i * HD : (i + 1) * HD] for i in range(4)]


def emit(out, parts):
    for i, part in enumerate(parts):
        out[:, i * HD : (i + 1) * HD] = part


def far_body(ext_in, outer, normed, wq, cosines, sines, docs, ext, out):
    _, _, _, far, home = spots()
    rows = chunk_rows(far)

    @pl.when(lax.rem(home, 2) == 0)
    def _():
        ext[0] = outer[0:CH]
        ext[1] = outer[CH : 2 * CH]

    q = project_q(normed[...], wq, cosines[rows], sines[rows])
    emit(out, attend(far, q, ext, docs))


def last_body(ext_in, owners, xa, xb, gain, wk, wv, cosines, sines, ext, normed_out, late_out):
    _, _, _, far, home = spots()
    rows = chunk_rows(far)
    normed = normalize_all((xa, xb), gain)
    normed_out[...] = normed
    parts = kv_parts(normed, wk, wv, cosines[rows], sines[rows])
    put(ext, 2 + far, slice(None), parts)
    live = (owners[0:CH] == home - 1) | (far > 0)
    for i, part in enumerate(parts):
        late_out[:, i * HD : (i + 1) * HD] = owned_part(part, live)


def first_tile(ext, q_near, q_rest, docs, out):
    half = CH // 2
    q = jnp.concatenate([q_rest[0:half], q_near[half:CH]], axis=0)
    emit(out, attend(spots()[2], heads(q), ext, docs))


def first_is_early():
    own, _, _, _, home = spots()
    return (lax.rem(home, 2) == 1) | (own == 1) | (own == 2)


def first_body(ext_in, inner, q_near, q_rest, docs, ext, out):
    @pl.when(lax.rem(spots()[4], 2) == 1)
    def _():
        ext[0] = inner[0:CH]
        ext[1] = inner[CH : 2 * CH]

    @pl.when(first_is_early())
    def _():
        first_tile(ext, q_near, q_rest, docs, out)


def second_body(out_in, far_in, ext, q_near, q_rest, docs, out, far_out):
    @pl.when(jnp.logical_not(first_is_early()))
    def _():
        first_tile(ext, q_near, q_rest, docs, out)


def left_body(ext_in, late, q_near, q_rest, docs, ext, out):
    own, left, _, _, _ = spots()
    half = CH // 2

    @pl.when(own < 2)
    def _():
        ext[own] = late[...]

    q = jnp.concatenate([q_near[0:half], q_rest[half:CH]], axis=0)
    emit(out, attend(left, heads(q), ext, docs))


def own_tile_body(ext, owners, late, inner, outer, q, docs, out, key_out, value_out, keys, values, sems):
    own, _, _, _, home = spots()

    def put_cache(row, part):
        keys[row : row + part.shape[0]] = part[:, 0:256]
        values[row : row + part.shape[0]] = part[:, 256:512]

    count = jnp.where(lax.rem(home, 2) == 1, inner[2 * CH : 2 * CH + 1, :], outer[2 * CH : 2 * CH + 1, :]).astype(jnp.float32)
    for j in range(4):
        part = ext[1, j * 32 : (j + 1) * 32]
        put_cache(j * 32, jnp.where(count > 3.5 - j, part.astype(jnp.float32), 0.0).astype(jnp.bfloat16))
    for j in range(4):
        put_cache(CH + j * CH, owned_part(ext[2 + j], owners[j * CH : (j + 1) * CH] == home))

    @pl.when(own == 2)
    def _():
        put_cache(5 * CH, late[...])

    @pl.when((own != 2) & (lax.rem(home, 2) == 0))
    def _():
        put_cache(5 * CH, inner[0:CH])

    @pl.when((own != 2) & (lax.rem(home, 2) == 1))
    def _():
        put_cache(5 * CH, outer[0:CH])

    copies = [
        pltpu.make_async_copy(keys, key_out, sems.at[0]),
        pltpu.make_async_copy(values, value_out, sems.at[1]),
    ]
    for copy in copies:
        copy.start()
    emit(out, attend(own, heads(q), ext, docs))
    for copy in copies:
        copy.wait()


def join_body(s0, r1_odd, r1_even, r2, r3, out, sems):
    own, left, right, far, home = spots()

    def place(piece, at, i):
        columns = pl.ds(pl.multiple_of(at * 512, 512), 512)
        return pltpu.make_async_copy(piece, out.at[:, columns], sems.at[i])

    copies = [place(s0, own, 0), place(r2, far, 2), place(r3, right, 3)]
    for copy in copies:
        copy.start()
    for parity, piece in ((1, r1_odd), (0, r1_even)):

        @pl.when(lax.rem(home, 2) == parity)
        def _():
            copy = place(piece, left, 1)
            copy.start()
            copy.wait()

    for copy in copies:
        copy.wait()


def layer(hidden, norm_gain, w_query, w_key, w_value, doc_start, block_owner):
    home = lax.axis_index("seq")
    rows = doc_start.shape[0]
    bf = jnp.bfloat16
    inside = pl.BlockSpec(memory_space=VM)
    outside = pl.BlockSpec(memory_space=pltpu.MemorySpace.HBM)
    wide = hidden.shape[1]

    def mover(body, outs, arrays, size):
        return pl.pallas_call(
            body,
            out_shape=[VM(s, bf) for s in outs],
            in_specs=[outside if x.size > CH * wide // 2 else pl.BlockSpec(memory_space=pl.ANY) for x in arrays],
            out_specs=[inside] * len(outs),
            scratch_shapes=[pltpu.SemaphoreType.DMA((len(outs),))],
            compiler_params=pltpu.CompilerParams(vmem_limit_bytes=2 << 20),
            cost_estimate=pl.CostEstimate(flops=0, bytes_accessed=size, transcendentals=0),
        )(*[pltpu.with_memory_space_constraint(x, HB) if x.size > CH * wide // 2 else x for x in arrays])

    own_a, own_b = mover(halves_body, [(CH // 2, wide)] * 2, [hidden], 2 << 20)
    left_a = ring(own_a, 1)
    right_b = ring(own_b, -1)
    left_b = ring(own_b, 1)
    right_a = ring(own_a, -1)
    far_a = ring(left_a, 1)
    far_b = ring(right_b, -1)
    row_number = home * rows + jnp.arange(rows, dtype=jnp.int32)
    lane = jnp.arange(HD, dtype=jnp.float32)
    lane_half = jnp.where(lane < HD // 2, lane, lane - HD // 2)
    frequency = jnp.power(ROPE_BASE, -lane_half * (2.0 / HD))
    angles = (row_number - doc_start).astype(jnp.float32)[:, None] * frequency[None, :]
    cosines, sines = jnp.cos(angles), jnp.where(lane < HD // 2, -1.0, 1.0)[None, :] * jnp.sin(angles)
    docs = jnp.broadcast_to((doc_start - home * rows)[:, None], (rows, HD))
    owners = jnp.broadcast_to(block_owner[:, None, None], (block_owner.shape[0], BLK, HD)).reshape(rows, HD)

    w_query, w_key, w_value = mover(
        weights_body, [w.shape for w in (w_query, w_key, w_value)], [w_query, w_key, w_value, docs, owners], 16 << 20
    )
    gain = norm_gain[None, :]
    flops = 2 * CH * wide * 1024
    scores = 8 * 2 * CH * 3 * CH * HD
    slots = (6, CH, 512)
    piece = (CH, 512)
    ext, q_own = call(own_body, [slots, piece], [own_a, own_b, gain, w_query, w_key, w_value, cosines, sines], flops)
    ext, q_near = call(
        near_body,
        [slots, piece],
        [ext, left_a, right_b, gain, w_query, w_key, w_value, cosines, sines],
        flops,
        alias=0,
    )
    ext, normed, inside_out, outside_out = call(
        rest_body,
        [slots, (CH, wide), (2 * CH + 16, 512), (2 * CH + 16, 512)],
        [ext, owners, right_a, left_b, gain, w_key, w_value, cosines, sines],
        flops // 2,
        alias=0,
    )
    outer = swap(outside_out, 1)
    inner = swap(inside_out, 0)
    (q_rest,) = call(rest_q_body, [piece], [normed, w_query, cosines, sines], flops // 2)
    ext, s1 = call(first_body, [slots, piece], [ext, inner, q_near, q_rest, docs], scores, alias=0)
    r1_odd = turn_of(s1, 1)
    ext, normed, far = call(
        last_body,
        [slots, (CH, wide), piece],
        [ext, owners, far_a, far_b, gain, w_key, w_value, cosines, sines],
        flops // 2,
        alias=0,
    )
    late = across(far, {0: 1, 1: 1, 2: -1})
    ext, s2 = call(
        far_body, [slots, piece], [ext, outer, normed, w_query, cosines, sines, docs], flops, alias=0
    )
    s1, s2 = call(second_body, [piece, piece], [s1, s2, ext, q_near, q_rest, docs], scores, alias=0, aliases=2)
    r2 = ring(s2, 2)
    r1_even = turn_of(s1, 0)
    ext, s3 = call(left_body, [slots, piece], [ext, late, q_near, q_rest, docs], scores, alias=0)
    r3 = ring(s3, 3)
    cache = jax.ShapeDtypeStruct((rows + 2 * CH, 256), bf)
    s0, key_cache, value_cache = call(
        own_tile_body,
        [piece, cache, cache],
        [ext, owners, late, inner, outer, q_own, docs],
        scores,
        scratch=[VM((rows + 2 * CH, 256), bf)] * 2 + [pltpu.SemaphoreType.DMA((2,))],
    )
    (context,) = call(
        join_body,
        [jax.ShapeDtypeStruct((CH, 2048), bf)],
        [s0, r1_odd, r1_even, r2, r3],
        scratch=[pltpu.SemaphoreType.DMA((4,))],
    )
    return (context, key_cache, value_cache)


def solution(mesh):
    return jax.shard_map(
        layer,
        mesh=mesh,
        in_specs=(
            P(("seq", "tp"), None),
            P(),
            P(None, "tp"),
            P(None, "tp"),
            P(None, "tp"),
            P("seq"),
            P("seq"),
        ),
        out_specs=(P(("seq", "tp"), None), P("seq", "tp"), P("seq", "tp")),
        check_vma=False,
    )
```

```python
import jax
import jax.numpy as jnp
from jax import lax
from jax.experimental import pallas as pl
from jax.experimental.pallas import tpu as pltpu
from jax.sharding import PartitionSpec as P


HD = 128
EPS = 1e-05
ROPE_BASE = 500000.0
CH = 128
BLK = 32
VM = pltpu.MemorySpace.VMEM
HB = pltpu.MemorySpace.HBM


def ring(array, by):
    n = lax.axis_size("tp")
    return lax.ppermute(array, "tp", [(i, (i + by) % n) for i in range(n)])


def across(array, moves):
    homes, n = lax.axis_size("seq"), lax.axis_size("tp")
    pairs = [(h * n + t, (h + by) * n + t) for h in range(homes) for t, by in moves.items() if 0 <= h + by < homes]
    return lax.ppermute(array, ("seq", "tp"), pairs)


def swap(array, first):
    homes = lax.axis_size("seq")
    pairs = [p for h in range(first, homes - 1, 2) for p in ((h, h + 1), (h + 1, h))]
    return lax.ppermute(array, "seq", pairs)


def spots():
    me, home = lax.axis_index("tp"), lax.axis_index("seq")
    return [lax.rem(me + k, 4) for k in (0, 3, 1, 2)] + [home]


def vmem(x):
    return pltpu.with_memory_space_constraint(x, VM)


def call(body, outs, arrays, flops=0, alias=None, aliases=1, scratch=()):
    inside = pl.BlockSpec(memory_space=VM)
    moved = sum(x.size * x.dtype.itemsize for x in arrays)
    return pl.pallas_call(
        body,
        out_shape=[o if isinstance(o, jax.ShapeDtypeStruct) else VM(o, jnp.bfloat16) for o in outs],
        in_specs=[inside] * len(arrays),
        out_specs=[
            pl.BlockSpec(memory_space=HB) if isinstance(o, jax.ShapeDtypeStruct) else inside for o in outs
        ],
        scratch_shapes=list(scratch),
        input_output_aliases={} if alias is None else {alias + i: i for i in range(aliases)},
        compiler_params=pltpu.CompilerParams(vmem_limit_bytes=12 << 20),
        cost_estimate=pl.CostEstimate(flops=flops, bytes_accessed=moved, transcendentals=0),
    )(*[vmem(x) for x in arrays])


def normalize(x, gain):
    wide = x.astype(jnp.float32)
    inverse = lax.rsqrt(jnp.mean(wide * wide, axis=1, keepdims=True) + EPS)
    return (wide * inverse * gain).astype(jnp.bfloat16)


def rotate(x, cosine, sine):
    heads = x.shape[1] // HD
    parts = []
    for i in range(heads):
        one = x[:, i * HD : (i + 1) * HD]
        parts.append((one * cosine + pltpu.roll(one, HD // 2, 1) * sine).astype(jnp.bfloat16))
    return parts


def dot(a, b):
    return jnp.dot(a, b, preferred_element_type=jnp.float32)


def project_kv(normed, wk, wv, cosine, sine):
    keys = rotate(dot(normed, wk[...]), cosine, sine)
    values = dot(normed, wv[...]).astype(jnp.bfloat16)
    return keys, values


def project_q(normed, wq, cosine, sine):
    parts = []
    for i in range(wq.shape[1] // 256):
        parts += rotate(dot(normed, wq[:, i * 256 : (i + 1) * 256]), cosine, sine)
    return parts


def run(copies):
    for copy in copies:
        copy.start()
    for copy in copies:
        copy.wait()


def halves_body(hidden, a, b, sems):
    size = CH // 2
    run([pltpu.make_async_copy(hidden.at[i * size : (i + 1) * size], out, sems.at[i]) for i, out in enumerate((a, b))])


def weights_body(wq, wk, wv, after, after_too, wq_out, wk_out, wv_out, sems):
    run([pltpu.make_async_copy(w, out, sems.at[i]) for i, (w, out) in enumerate(((wq, wq_out), (wk, wk_out), (wv, wv_out)))])


def chunk_rows(at):
    return pl.ds(pl.multiple_of(at * CH, CH), CH)


def half_rows(at, offset):
    return pl.ds(pl.multiple_of(at * CH + offset, CH // 2), CH // 2)


def normalize_all(pieces, gain):
    return jnp.concatenate([normalize(piece[...], gain[...]) for piece in pieces], axis=0)


def put(ref, index, rows, parts):
    for i, part in enumerate(parts):
        ref[index, :, i * HD : (i + 1) * HD] = part[rows]


def kv_parts(normed, wk, wv, cosine, sine):
    keys, values = project_kv(normed, wk, wv, cosine, sine)
    return [*keys, values[:, :HD], values[:, HD:]]


def own_body(xa, xb, gain, wq, wk, wv, cosines, sines, ext, q_out):
    own = spots()[0]
    rows = chunk_rows(own)
    normed = normalize_all((xa, xb), gain)
    put(ext, 2 + own, slice(None), kv_parts(normed, wk, wv, cosines[rows], sines[rows]))
    for i, part in enumerate(project_q(normed, wq, cosines[rows], sines[rows])):
        q_out[:, i * HD : (i + 1) * HD] = part


def owned_part(part, live):
    live = jnp.concatenate([live] * (part.shape[1] // HD), axis=1)
    return jnp.where(live, part.astype(jnp.float32), 0.0).astype(jnp.bfloat16)


def near_body(ext_in, la, rb, gain, wq, wk, wv, cosines, sines, ext, q_out):
    _, left, right, _, _ = spots()
    half = CH // 2
    first, second = half_rows(left, 0), half_rows(right, half)
    cosine = jnp.concatenate([cosines[first], cosines[second]], axis=0)
    sine = jnp.concatenate([sines[first], sines[second]], axis=0)
    normed = normalize_all((la, rb), gain)
    for i, part in enumerate(kv_parts(normed, wk, wv, cosine, sine)):
        ext[2 + left, 0:half, i * HD : (i + 1) * HD] = part[:half]
        ext[2 + right, half:CH, i * HD : (i + 1) * HD] = part[half:]
    for i, part in enumerate(project_q(normed, wq, cosine, sine)):
        q_out[:, i * HD : (i + 1) * HD] = part


def rest_turns(cosines, sines):
    _, left, right, _, _ = spots()
    half = CH // 2
    first, second = half_rows(right, 0), half_rows(left, half)
    cosine = jnp.concatenate([cosines[first], cosines[second]], axis=0)
    sine = jnp.concatenate([sines[first], sines[second]], axis=0)
    return cosine, sine


def rest_body(ext_in, owners, ra, lb, gain, wk, wv, cosines, sines, ext, normed_out, inside_out, outside_out):
    _, left, right, _, home = spots()
    half = CH // 2
    normed = normalize_all((ra, lb), gain)
    normed_out[...] = normed
    for i, part in enumerate(kv_parts(normed, wk, wv, *rest_turns(cosines, sines))):
        ext[2 + right, 0:half, i * HD : (i + 1) * HD] = part[:half]
        ext[2 + left, half:CH, i * HD : (i + 1) * HD] = part[half:]
    count = jnp.sum(jnp.where(owners[3 * CH :] == home + 1, 1.0 / 32, 0.0), axis=0, keepdims=True)
    count = jnp.broadcast_to(jnp.concatenate([count] * 4, axis=1), (16, 512)).astype(jnp.bfloat16)

    def fill(to_right, to_left):
        to_right[0:CH] = ext[4]
        to_right[CH : 2 * CH] = ext[5]
        to_right[2 * CH :] = count
        to_left[0:CH] = owned_part(ext[2], owners[0:CH] == home - 1)

    @pl.when(lax.rem(home, 2) == 0)
    def _():
        fill(inside_out, outside_out)

    @pl.when(lax.rem(home, 2) == 1)
    def _():
        fill(outside_out, inside_out)


def rest_q_body(normed, wq, cosines, sines, q_out):
    for i, part in enumerate(project_q(normed[...], wq, *rest_turns(cosines, sines))):
        q_out[:, i * HD : (i + 1) * HD] = part


def attend(tile, q, ext, docs):
    window = 3 * CH
    doc = docs[chunk_rows(tile), 0:1]
    key_row = lax.broadcasted_iota(jnp.int32, (CH, window), 1) + (tile - 2) * CH
    row = lax.broadcasted_iota(jnp.int32, (CH, window), 0) + tile * CH
    allowed = (key_row >= doc) & (key_row <= row)
    allowed = jnp.concatenate([allowed, allowed], axis=0)
    near = ext[pl.ds(tile, 3)].reshape(window, 512)
    outs = []
    for g in range(2):
        pair = jnp.concatenate(q[2 * g : 2 * g + 2], axis=0)
        keys, values = near[:, g * HD : (g + 1) * HD], near[:, (2 + g) * HD : (3 + g) * HD]
        scores = lax.dot_general(pair, keys, (((1,), (1,)), ((), ())), preferred_element_type=jnp.float32) * HD ** (-0.5)
        scores = jnp.where(allowed, scores, -jnp.inf)
        highest = jnp.max(scores, axis=1, keepdims=True)
        weights = jnp.exp(scores - highest)
        weights = (weights * (1.0 / jnp.sum(weights, axis=1, keepdims=True))).astype(jnp.bfloat16)
        blended = dot(weights, values).astype(jnp.bfloat16)
        outs += [blended[:CH], blended[CH:]]
    return outs


def heads(q):
    return [q[:, i * HD : (i + 1) * HD] for i in range(4)]


def emit(out, parts):
    for i, part in enumerate(parts):
        out[:, i * HD : (i + 1) * HD] = part


def far_body(ext_in, outer, normed, wq, cosines, sines, docs, ext, out):
    _, _, _, far, home = spots()
    rows = chunk_rows(far)

    @pl.when(lax.rem(home, 2) == 0)
    def _():
        ext[0] = outer[0:CH]
        ext[1] = outer[CH : 2 * CH]

    q = project_q(normed[...], wq, cosines[rows], sines[rows])
    emit(out, attend(far, q, ext, docs))


def last_body(ext_in, owners, xa, xb, gain, wk, wv, cosines, sines, ext, normed_out, late_out):
    _, _, _, far, home = spots()
    rows = chunk_rows(far)
    normed = normalize_all((xa, xb), gain)
    normed_out[...] = normed
    parts = kv_parts(normed, wk, wv, cosines[rows], sines[rows])
    put(ext, 2 + far, slice(None), parts)
    live = (owners[0:CH] == home - 1) | (far > 0)
    for i, part in enumerate(parts):
        late_out[:, i * HD : (i + 1) * HD] = owned_part(part, live)


def first_tile(ext, q_near, q_rest, docs, out):
    half = CH // 2
    q = jnp.concatenate([q_rest[0:half], q_near[half:CH]], axis=0)
    emit(out, attend(spots()[2], heads(q), ext, docs))


def first_is_early():
    own, _, _, _, home = spots()
    return (lax.rem(home, 2) == 1) | (own == 1) | (own == 2)


def first_body(ext_in, inner, q_near, q_rest, docs, ext, out):
    @pl.when(lax.rem(spots()[4], 2) == 1)
    def _():
        ext[0] = inner[0:CH]
        ext[1] = inner[CH : 2 * CH]

    @pl.when(first_is_early())
    def _():
        first_tile(ext, q_near, q_rest, docs, out)


def second_body(out_in, far_in, ext, q_near, q_rest, docs, out, far_out):
    @pl.when(jnp.logical_not(first_is_early()))
    def _():
        first_tile(ext, q_near, q_rest, docs, out)


def left_body(ext_in, late, q_near, q_rest, docs, ext, out):
    own, left, _, _, _ = spots()
    half = CH // 2

    @pl.when(own < 2)
    def _():
        ext[own] = late[...]

    q = jnp.concatenate([q_near[0:half], q_rest[half:CH]], axis=0)
    emit(out, attend(left, heads(q), ext, docs))


def own_tile_body(ext, owners, late, inner, outer, q, docs, out, key_out, value_out, keys, values, sems):
    own, _, _, _, home = spots()

    def put_cache(row, part):
        keys[row : row + part.shape[0]] = part[:, 0:256]
        values[row : row + part.shape[0]] = part[:, 256:512]

    count = jnp.where(lax.rem(home, 2) == 1, inner[2 * CH : 2 * CH + 1, :], outer[2 * CH : 2 * CH + 1, :]).astype(jnp.float32)
    for j in range(4):
        part = ext[1, j * 32 : (j + 1) * 32]
        put_cache(j * 32, jnp.where(count > 3.5 - j, part.astype(jnp.float32), 0.0).astype(jnp.bfloat16))
    for j in range(4):
        put_cache(CH + j * CH, owned_part(ext[2 + j], owners[j * CH : (j + 1) * CH] == home))

    @pl.when(own == 2)
    def _():
        put_cache(5 * CH, late[...])

    @pl.when((own != 2) & (lax.rem(home, 2) == 0))
    def _():
        put_cache(5 * CH, inner[0:CH])

    @pl.when((own != 2) & (lax.rem(home, 2) == 1))
    def _():
        put_cache(5 * CH, outer[0:CH])

    copies = [
        pltpu.make_async_copy(keys, key_out, sems.at[0]),
        pltpu.make_async_copy(values, value_out, sems.at[1]),
    ]
    for copy in copies:
        copy.start()
    emit(out, attend(own, heads(q), ext, docs))
    for copy in copies:
        copy.wait()


def join_body(s0, r1, r2, r3, out, sems):
    own, left, right, far, _ = spots()
    copies = []
    for i, (piece, at) in enumerate(((s0, own), (r1, left), (r2, far), (r3, right))):
        columns = pl.ds(pl.multiple_of(at * 512, 512), 512)
        copies.append(pltpu.make_async_copy(piece, out.at[:, columns], sems.at[i]))
    run(copies)


def layer(hidden, norm_gain, w_query, w_key, w_value, doc_start, block_owner):
    home = lax.axis_index("seq")
    rows = doc_start.shape[0]
    bf = jnp.bfloat16
    inside = pl.BlockSpec(memory_space=VM)
    outside = pl.BlockSpec(memory_space=pltpu.MemorySpace.HBM)
    wide = hidden.shape[1]

    def mover(body, outs, arrays, size):
        return pl.pallas_call(
            body,
            out_shape=[VM(s, bf) for s in outs],
            in_specs=[outside if x.size > CH * wide // 2 else pl.BlockSpec(memory_space=pl.ANY) for x in arrays],
            out_specs=[inside] * len(outs),
            scratch_shapes=[pltpu.SemaphoreType.DMA((len(outs),))],
            compiler_params=pltpu.CompilerParams(vmem_limit_bytes=2 << 20),
            cost_estimate=pl.CostEstimate(flops=0, bytes_accessed=size, transcendentals=0),
        )(*[pltpu.with_memory_space_constraint(x, HB) if x.size > CH * wide // 2 else x for x in arrays])

    own_a, own_b = mover(halves_body, [(CH // 2, wide)] * 2, [hidden], 2 << 20)
    left_a = ring(own_a, 1)
    right_b = ring(own_b, -1)
    left_b = ring(own_b, 1)
    right_a = ring(own_a, -1)
    far_a = ring(left_a, 1)
    far_b = ring(right_b, -1)
    row_number = home * rows + jnp.arange(rows, dtype=jnp.int32)
    lane = jnp.arange(HD, dtype=jnp.float32)
    lane_half = jnp.where(lane < HD // 2, lane, lane - HD // 2)
    frequency = jnp.power(ROPE_BASE, -lane_half * (2.0 / HD))
    angles = (row_number - doc_start).astype(jnp.float32)[:, None] * frequency[None, :]
    cosines, sines = jnp.cos(angles), jnp.where(lane < HD // 2, -1.0, 1.0)[None, :] * jnp.sin(angles)
    docs = jnp.broadcast_to((doc_start - home * rows)[:, None], (rows, HD))
    owners = jnp.broadcast_to(block_owner[:, None, None], (block_owner.shape[0], BLK, HD)).reshape(rows, HD)

    w_query, w_key, w_value = mover(
        weights_body, [w.shape for w in (w_query, w_key, w_value)], [w_query, w_key, w_value, docs, owners], 16 << 20
    )
    gain = norm_gain[None, :]
    flops = 2 * CH * wide * 1024
    scores = 8 * 2 * CH * 3 * CH * HD
    slots = (6, CH, 512)
    piece = (CH, 512)
    ext, q_own = call(own_body, [slots, piece], [own_a, own_b, gain, w_query, w_key, w_value, cosines, sines], flops)
    ext, q_near = call(
        near_body,
        [slots, piece],
        [ext, left_a, right_b, gain, w_query, w_key, w_value, cosines, sines],
        flops,
        alias=0,
    )
    ext, normed, inside_out, outside_out = call(
        rest_body,
        [slots, (CH, wide), (2 * CH + 16, 512), (2 * CH + 16, 512)],
        [ext, owners, right_a, left_b, gain, w_key, w_value, cosines, sines],
        flops // 2,
        alias=0,
    )
    outer = swap(outside_out, 1)
    inner = swap(inside_out, 0)
    (q_rest,) = call(rest_q_body, [piece], [normed, w_query, cosines, sines], flops // 2)
    ext, s1 = call(first_body, [slots, piece], [ext, inner, q_near, q_rest, docs], scores, alias=0)
    ext, normed, far = call(
        last_body,
        [slots, (CH, wide), piece],
        [ext, owners, far_a, far_b, gain, w_key, w_value, cosines, sines],
        flops // 2,
        alias=0,
    )
    late = across(far, {0: 1, 1: 1, 2: -1})
    ext, s2 = call(
        far_body, [slots, piece], [ext, outer, normed, w_query, cosines, sines, docs], flops, alias=0
    )
    s1, s2 = call(second_body, [piece, piece], [s1, s2, ext, q_near, q_rest, docs], scores, alias=0, aliases=2)
    r2 = ring(s2, 2)
    r1 = ring(s1, 1)
    ext, s3 = call(left_body, [slots, piece], [ext, late, q_near, q_rest, docs], scores, alias=0)
    r3 = ring(s3, 3)
    cache = jax.ShapeDtypeStruct((rows + 2 * CH, 256), bf)
    s0, key_cache, value_cache = call(
        own_tile_body,
        [piece, cache, cache],
        [ext, owners, late, inner, outer, q_own, docs],
        scores,
        scratch=[VM((rows + 2 * CH, 256), bf)] * 2 + [pltpu.SemaphoreType.DMA((2,))],
    )
    (context,) = call(
        join_body,
        [jax.ShapeDtypeStruct((CH, 2048), bf)],
        [s0, r1, r2, r3],
        scratch=[pltpu.SemaphoreType.DMA((4,))],
    )
    return (context, key_cache, value_cache)


def solution(mesh):
    return jax.shard_map(
        layer,
        mesh=mesh,
        in_specs=(
            P(("seq", "tp"), None),
            P(),
            P(None, "tp"),
            P(None, "tp"),
            P(None, "tp"),
            P("seq"),
            P("seq"),
        ),
        out_specs=(P(("seq", "tp"), None), P("seq", "tp"), P("seq", "tp")),
        check_vma=False,
    )
```

```python
import jax
import jax.numpy as jnp
from jax import lax
from jax.experimental import pallas as pl
from jax.experimental.pallas import tpu as pltpu
from jax.sharding import PartitionSpec as P


HD = 128
EPS = 1e-05
ROPE_BASE = 500000.0
CH = 128
BLK = 32
VM = pltpu.MemorySpace.VMEM
HB = pltpu.MemorySpace.HBM


def ring(array, by):
    n = lax.axis_size("tp")
    return lax.ppermute(array, "tp", [(i, (i + by) % n) for i in range(n)])


def across(array, moves):
    homes, n = lax.axis_size("seq"), lax.axis_size("tp")
    pairs = [(h * n + t, (h + by) * n + t) for h in range(homes) for t, by in moves.items() if 0 <= h + by < homes]
    return lax.ppermute(array, ("seq", "tp"), pairs)


def swap(array, first):
    homes = lax.axis_size("seq")
    pairs = [p for h in range(first, homes - 1, 2) for p in ((h, h + 1), (h + 1, h))]
    return lax.ppermute(array, "seq", pairs)


def spots():
    me, home = lax.axis_index("tp"), lax.axis_index("seq")
    return [lax.rem(me + k, 4) for k in (0, 3, 1, 2)] + [home]


def vmem(x):
    return pltpu.with_memory_space_constraint(x, VM)


def call(body, outs, arrays, flops=0, alias=None, aliases=1, scratch=()):
    inside = pl.BlockSpec(memory_space=VM)
    moved = sum(x.size * x.dtype.itemsize for x in arrays)
    return pl.pallas_call(
        body,
        out_shape=[o if isinstance(o, jax.ShapeDtypeStruct) else VM(o, jnp.bfloat16) for o in outs],
        in_specs=[inside] * len(arrays),
        out_specs=[
            pl.BlockSpec(memory_space=HB) if isinstance(o, jax.ShapeDtypeStruct) else inside for o in outs
        ],
        scratch_shapes=list(scratch),
        input_output_aliases={} if alias is None else {alias + i: i for i in range(aliases)},
        compiler_params=pltpu.CompilerParams(vmem_limit_bytes=12 << 20),
        cost_estimate=pl.CostEstimate(flops=flops, bytes_accessed=moved, transcendentals=0),
    )(*[vmem(x) for x in arrays])


def normalize(x, gain):
    wide = x.astype(jnp.float32)
    inverse = lax.rsqrt(jnp.mean(wide * wide, axis=1, keepdims=True) + EPS)
    return (wide * inverse * gain).astype(jnp.bfloat16)


def rotate(x, cosine, sine):
    heads = x.shape[1] // HD
    parts = []
    for i in range(heads):
        one = x[:, i * HD : (i + 1) * HD]
        parts.append((one * cosine + pltpu.roll(one, HD // 2, 1) * sine).astype(jnp.bfloat16))
    return parts


def dot(a, b):
    return jnp.dot(a, b, preferred_element_type=jnp.float32)


def project_kv(normed, wk, wv, cosine, sine):
    keys = rotate(dot(normed, wk[...]), cosine, sine)
    values = dot(normed, wv[...]).astype(jnp.bfloat16)
    return keys, values


def project_q(normed, wq, cosine, sine):
    parts = []
    for i in range(wq.shape[1] // 256):
        parts += rotate(dot(normed, wq[:, i * 256 : (i + 1) * 256]), cosine, sine)
    return parts


def run(copies):
    for copy in copies:
        copy.start()
    for copy in copies:
        copy.wait()


def halves_body(hidden, a, b, sems):
    size = CH // 2
    run([pltpu.make_async_copy(hidden.at[i * size : (i + 1) * size], out, sems.at[i]) for i, out in enumerate((a, b))])


def weights_body(wq, wk, wv, after, after_too, wq_out, wk_out, wv_out, sems):
    run([pltpu.make_async_copy(w, out, sems.at[i]) for i, (w, out) in enumerate(((wq, wq_out), (wk, wk_out), (wv, wv_out)))])


def chunk_rows(at):
    return pl.ds(pl.multiple_of(at * CH, CH), CH)


def half_rows(at, offset):
    return pl.ds(pl.multiple_of(at * CH + offset, CH // 2), CH // 2)


def normalize_all(pieces, gain):
    return jnp.concatenate([normalize(piece[...], gain[...]) for piece in pieces], axis=0)


def put(ref, index, rows, parts):
    for i, part in enumerate(parts):
        ref[index, :, i * HD : (i + 1) * HD] = part[rows]


def kv_parts(normed, wk, wv, cosine, sine):
    keys, values = project_kv(normed, wk, wv, cosine, sine)
    return [*keys, values[:, :HD], values[:, HD:]]


def own_body(xa, xb, gain, wq, wk, wv, cosines, sines, ext, q_out):
    own = spots()[0]
    rows = chunk_rows(own)
    normed = normalize_all((xa, xb), gain)
    put(ext, 2 + own, slice(None), kv_parts(normed, wk, wv, cosines[rows], sines[rows]))
    for i, part in enumerate(project_q(normed, wq, cosines[rows], sines[rows])):
        q_out[:, i * HD : (i + 1) * HD] = part


def owned_part(part, live):
    live = jnp.concatenate([live] * (part.shape[1] // HD), axis=1)
    return jnp.where(live, part.astype(jnp.float32), 0.0).astype(jnp.bfloat16)


def near_body(ext_in, la, rb, gain, wq, wk, wv, cosines, sines, ext, q_out):
    _, left, right, _, _ = spots()
    half = CH // 2
    first, second = half_rows(left, 0), half_rows(right, half)
    cosine = jnp.concatenate([cosines[first], cosines[second]], axis=0)
    sine = jnp.concatenate([sines[first], sines[second]], axis=0)
    normed = normalize_all((la, rb), gain)
    for i, part in enumerate(kv_parts(normed, wk, wv, cosine, sine)):
        ext[2 + left, 0:half, i * HD : (i + 1) * HD] = part[:half]
        ext[2 + right, half:CH, i * HD : (i + 1) * HD] = part[half:]
    for i, part in enumerate(project_q(normed, wq, cosine, sine)):
        q_out[:, i * HD : (i + 1) * HD] = part


def rest_turns(cosines, sines):
    _, left, right, _, _ = spots()
    half = CH // 2
    first, second = half_rows(right, 0), half_rows(left, half)
    cosine = jnp.concatenate([cosines[first], cosines[second]], axis=0)
    sine = jnp.concatenate([sines[first], sines[second]], axis=0)
    return cosine, sine


def rest_body(ext_in, owners, ra, lb, gain, wk, wv, cosines, sines, ext, normed_out, inside_out, outside_out):
    _, left, right, _, home = spots()
    half = CH // 2
    normed = normalize_all((ra, lb), gain)
    normed_out[...] = normed
    for i, part in enumerate(kv_parts(normed, wk, wv, *rest_turns(cosines, sines))):
        ext[2 + right, 0:half, i * HD : (i + 1) * HD] = part[:half]
        ext[2 + left, half:CH, i * HD : (i + 1) * HD] = part[half:]
    count = jnp.sum(jnp.where(owners[3 * CH :] == home + 1, 1.0 / 32, 0.0), axis=0, keepdims=True)
    count = jnp.broadcast_to(jnp.concatenate([count] * 4, axis=1), (16, 512)).astype(jnp.bfloat16)

    def fill(to_right, to_left):
        to_right[0:CH] = ext[4]
        to_right[CH : 2 * CH] = ext[5]
        to_right[2 * CH :] = count
        to_left[0:CH] = owned_part(ext[2], owners[0:CH] == home - 1)

    @pl.when(lax.rem(home, 2) == 0)
    def _():
        fill(inside_out, outside_out)

    @pl.when(lax.rem(home, 2) == 1)
    def _():
        fill(outside_out, inside_out)


def rest_q_body(normed, wq, cosines, sines, q_out):
    for i, part in enumerate(project_q(normed[...], wq, *rest_turns(cosines, sines))):
        q_out[:, i * HD : (i + 1) * HD] = part


def attend(tile, q, ext, docs):
    window = 3 * CH
    doc = docs[chunk_rows(tile), 0:1]
    key_row = lax.broadcasted_iota(jnp.int32, (CH, window), 1) + (tile - 2) * CH
    row = lax.broadcasted_iota(jnp.int32, (CH, window), 0) + tile * CH
    allowed = (key_row >= doc) & (key_row <= row)
    allowed = jnp.concatenate([allowed, allowed], axis=0)
    near = ext[pl.ds(tile, 3)].reshape(window, 512)
    outs = []
    for g in range(2):
        pair = jnp.concatenate(q[2 * g : 2 * g + 2], axis=0)
        keys, values = near[:, g * HD : (g + 1) * HD], near[:, (2 + g) * HD : (3 + g) * HD]
        scores = lax.dot_general(pair, keys, (((1,), (1,)), ((), ())), preferred_element_type=jnp.float32) * HD ** (-0.5)
        scores = jnp.where(allowed, scores, -jnp.inf)
        highest = jnp.max(scores, axis=1, keepdims=True)
        weights = jnp.exp(scores - highest)
        weights = (weights * (1.0 / jnp.sum(weights, axis=1, keepdims=True))).astype(jnp.bfloat16)
        blended = dot(weights, values).astype(jnp.bfloat16)
        outs += [blended[:CH], blended[CH:]]
    return outs


def heads(q):
    return [q[:, i * HD : (i + 1) * HD] for i in range(4)]


def emit(out, parts):
    for i, part in enumerate(parts):
        out[:, i * HD : (i + 1) * HD] = part


def far_tile(ext, normed, wq, cosines, sines, docs, out):
    far = spots()[3]
    rows = chunk_rows(far)
    q = project_q(normed[...], wq, cosines[rows], sines[rows])
    emit(out, attend(far, q, ext, docs))


def ahead_body(ext_in, late_in, normed, wq, cosines, sines, docs, ext, late_out, out):
    @pl.when(lax.rem(spots()[4], 2) == 1)
    def _():
        far_tile(ext, normed, wq, cosines, sines, docs, out)


def far_body(ext_in, out_in, outer, normed, wq, cosines, sines, docs, ext, out):
    @pl.when(lax.rem(spots()[4], 2) == 0)
    def _():
        ext[0] = outer[0:CH]
        ext[1] = outer[CH : 2 * CH]
        far_tile(ext, normed, wq, cosines, sines, docs, out)


def last_body(ext_in, owners, xa, xb, gain, wk, wv, cosines, sines, ext, normed_out, late_out):
    _, _, _, far, home = spots()
    rows = chunk_rows(far)
    normed = normalize_all((xa, xb), gain)
    normed_out[...] = normed
    parts = kv_parts(normed, wk, wv, cosines[rows], sines[rows])
    put(ext, 2 + far, slice(None), parts)
    live = (owners[0:CH] == home - 1) | (far > 0)
    for i, part in enumerate(parts):
        late_out[:, i * HD : (i + 1) * HD] = owned_part(part, live)


def first_tile(ext, q_near, q_rest, docs, out):
    half = CH // 2
    q = jnp.concatenate([q_rest[0:half], q_near[half:CH]], axis=0)
    emit(out, attend(spots()[2], heads(q), ext, docs))


def first_is_early():
    own, _, _, _, home = spots()
    return (lax.rem(home, 2) == 1) | (own == 1) | (own == 2)


def first_body(ext_in, inner, q_near, q_rest, docs, ext, out):
    @pl.when(lax.rem(spots()[4], 2) == 1)
    def _():
        ext[0] = inner[0:CH]
        ext[1] = inner[CH : 2 * CH]

    @pl.when(first_is_early())
    def _():
        first_tile(ext, q_near, q_rest, docs, out)


def second_body(out_in, far_in, ext, q_near, q_rest, docs, out, far_out):
    @pl.when(jnp.logical_not(first_is_early()))
    def _():
        first_tile(ext, q_near, q_rest, docs, out)


def left_body(ext_in, late, q_near, q_rest, docs, ext, out):
    own, left, _, _, _ = spots()
    half = CH // 2

    @pl.when(own < 2)
    def _():
        ext[own] = late[...]

    q = jnp.concatenate([q_near[0:half], q_rest[half:CH]], axis=0)
    emit(out, attend(left, heads(q), ext, docs))


def own_tile_body(ext, owners, late, inner, outer, q, docs, out, key_out, value_out, keys, values, sems):
    own, _, _, _, home = spots()

    def put_cache(row, part):
        keys[row : row + part.shape[0]] = part[:, 0:256]
        values[row : row + part.shape[0]] = part[:, 256:512]

    count = jnp.where(lax.rem(home, 2) == 1, inner[2 * CH : 2 * CH + 1, :], outer[2 * CH : 2 * CH + 1, :]).astype(jnp.float32)
    for j in range(4):
        part = ext[1, j * 32 : (j + 1) * 32]
        put_cache(j * 32, jnp.where(count > 3.5 - j, part.astype(jnp.float32), 0.0).astype(jnp.bfloat16))
    for j in range(4):
        put_cache(CH + j * CH, owned_part(ext[2 + j], owners[j * CH : (j + 1) * CH] == home))

    @pl.when(own == 2)
    def _():
        put_cache(5 * CH, late[...])

    @pl.when((own != 2) & (lax.rem(home, 2) == 0))
    def _():
        put_cache(5 * CH, inner[0:CH])

    @pl.when((own != 2) & (lax.rem(home, 2) == 1))
    def _():
        put_cache(5 * CH, outer[0:CH])

    copies = [
        pltpu.make_async_copy(keys, key_out, sems.at[0]),
        pltpu.make_async_copy(values, value_out, sems.at[1]),
    ]
    for copy in copies:
        copy.start()
    emit(out, attend(own, heads(q), ext, docs))
    for copy in copies:
        copy.wait()


def join_body(s0, r1, r2, r3, out, sems):
    own, left, right, far, _ = spots()
    copies = []
    for i, (piece, at) in enumerate(((s0, own), (r1, left), (r2, far), (r3, right))):
        columns = pl.ds(pl.multiple_of(at * 512, 512), 512)
        copies.append(pltpu.make_async_copy(piece, out.at[:, columns], sems.at[i]))
    run(copies)


def layer(hidden, norm_gain, w_query, w_key, w_value, doc_start, block_owner):
    home = lax.axis_index("seq")
    rows = doc_start.shape[0]
    bf = jnp.bfloat16
    inside = pl.BlockSpec(memory_space=VM)
    outside = pl.BlockSpec(memory_space=pltpu.MemorySpace.HBM)
    wide = hidden.shape[1]

    def mover(body, outs, arrays, size):
        return pl.pallas_call(
            body,
            out_shape=[VM(s, bf) for s in outs],
            in_specs=[outside if x.size > CH * wide // 2 else pl.BlockSpec(memory_space=pl.ANY) for x in arrays],
            out_specs=[inside] * len(outs),
            scratch_shapes=[pltpu.SemaphoreType.DMA((len(outs),))],
            compiler_params=pltpu.CompilerParams(vmem_limit_bytes=2 << 20),
            cost_estimate=pl.CostEstimate(flops=0, bytes_accessed=size, transcendentals=0),
        )(*[pltpu.with_memory_space_constraint(x, HB) if x.size > CH * wide // 2 else x for x in arrays])

    own_a, own_b = mover(halves_body, [(CH // 2, wide)] * 2, [hidden], 2 << 20)
    left_a = ring(own_a, 1)
    right_b = ring(own_b, -1)
    left_b = ring(own_b, 1)
    right_a = ring(own_a, -1)
    far_a = ring(left_a, 1)
    far_b = ring(right_b, -1)
    row_number = home * rows + jnp.arange(rows, dtype=jnp.int32)
    lane = jnp.arange(HD, dtype=jnp.float32)
    lane_half = jnp.where(lane < HD // 2, lane, lane - HD // 2)
    frequency = jnp.power(ROPE_BASE, -lane_half * (2.0 / HD))
    angles = (row_number - doc_start).astype(jnp.float32)[:, None] * frequency[None, :]
    cosines, sines = jnp.cos(angles), jnp.where(lane < HD // 2, -1.0, 1.0)[None, :] * jnp.sin(angles)
    docs = jnp.broadcast_to((doc_start - home * rows)[:, None], (rows, HD))
    owners = jnp.broadcast_to(block_owner[:, None, None], (block_owner.shape[0], BLK, HD)).reshape(rows, HD)

    w_query, w_key, w_value = mover(
        weights_body, [w.shape for w in (w_query, w_key, w_value)], [w_query, w_key, w_value, docs, owners], 16 << 20
    )
    gain = norm_gain[None, :]
    flops = 2 * CH * wide * 1024
    scores = 8 * 2 * CH * 3 * CH * HD
    slots = (6, CH, 512)
    piece = (CH, 512)
    ext, q_own = call(own_body, [slots, piece], [own_a, own_b, gain, w_query, w_key, w_value, cosines, sines], flops)
    ext, q_near = call(
        near_body,
        [slots, piece],
        [ext, left_a, right_b, gain, w_query, w_key, w_value, cosines, sines],
        flops,
        alias=0,
    )
    ext, normed, inside_out, outside_out = call(
        rest_body,
        [slots, (CH, wide), (2 * CH + 16, 512), (2 * CH + 16, 512)],
        [ext, owners, right_a, left_b, gain, w_key, w_value, cosines, sines],
        flops // 2,
        alias=0,
    )
    outer = swap(outside_out, 1)
    inner = swap(inside_out, 0)
    (q_rest,) = call(rest_q_body, [piece], [normed, w_query, cosines, sines], flops // 2)
    ext, s1 = call(first_body, [slots, piece], [ext, inner, q_near, q_rest, docs], scores, alias=0)
    ext, normed, far = call(
        last_body,
        [slots, (CH, wide), piece],
        [ext, owners, far_a, far_b, gain, w_key, w_value, cosines, sines],
        flops // 2,
        alias=0,
    )
    ext, far, s2 = call(
        ahead_body,
        [slots, piece, piece],
        [ext, far, normed, w_query, cosines, sines, docs],
        flops,
        alias=0,
        aliases=2,
    )
    late = across(far, {0: 1, 1: 1, 2: -1})
    ext, s2 = call(
        far_body,
        [slots, piece],
        [ext, s2, outer, normed, w_query, cosines, sines, docs],
        flops,
        alias=0,
        aliases=2,
    )
    s1, s2 = call(second_body, [piece, piece], [s1, s2, ext, q_near, q_rest, docs], scores, alias=0, aliases=2)
    r2 = ring(s2, 2)
    r1 = ring(s1, 1)
    ext, s3 = call(left_body, [slots, piece], [ext, late, q_near, q_rest, docs], scores, alias=0)
    r3 = ring(s3, 3)
    cache = jax.ShapeDtypeStruct((rows + 2 * CH, 256), bf)
    s0, key_cache, value_cache = call(
        own_tile_body,
        [piece, cache, cache],
        [ext, owners, late, inner, outer, q_own, docs],
        scores,
        scratch=[VM((rows + 2 * CH, 256), bf)] * 2 + [pltpu.SemaphoreType.DMA((2,))],
    )
    (context,) = call(
        join_body,
        [jax.ShapeDtypeStruct((CH, 2048), bf)],
        [s0, r1, r2, r3],
        scratch=[pltpu.SemaphoreType.DMA((4,))],
    )
    return (context, key_cache, value_cache)


def solution(mesh):
    return jax.shard_map(
        layer,
        mesh=mesh,
        in_specs=(
            P(("seq", "tp"), None),
            P(),
            P(None, "tp"),
            P(None, "tp"),
            P(None, "tp"),
            P("seq"),
            P("seq"),
        ),
        out_specs=(P(("seq", "tp"), None), P("seq", "tp"), P("seq", "tp")),
        check_vma=False,
    )
```

```python
import jax
import jax.numpy as jnp
from jax import lax
from jax.experimental import pallas as pl
from jax.experimental.pallas import tpu as pltpu
from jax.sharding import PartitionSpec as P


HD = 128
EPS = 1e-05
ROPE_BASE = 500000.0
CH = 128
BLK = 32
VM = pltpu.MemorySpace.VMEM
HB = pltpu.MemorySpace.HBM


def ring(array, by):
    n = lax.axis_size("tp")
    return lax.ppermute(array, "tp", [(i, (i + by) % n) for i in range(n)])


def across(array, moves):
    homes, n = lax.axis_size("seq"), lax.axis_size("tp")
    pairs = [(h * n + t, (h + by) * n + t) for h in range(homes) for t, by in moves.items() if 0 <= h + by < homes]
    return lax.ppermute(array, ("seq", "tp"), pairs)


def swap(array, first):
    homes = lax.axis_size("seq")
    pairs = [p for h in range(first, homes - 1, 2) for p in ((h, h + 1), (h + 1, h))]
    return lax.ppermute(array, "seq", pairs)


def spots():
    me, home = lax.axis_index("tp"), lax.axis_index("seq")
    return [lax.rem(me + k, 4) for k in (0, 3, 1, 2)] + [home]


def vmem(x):
    return pltpu.with_memory_space_constraint(x, VM)


def call(body, outs, arrays, flops=0, alias=None, aliases=1, scratch=()):
    inside = pl.BlockSpec(memory_space=VM)
    moved = sum(x.size * x.dtype.itemsize for x in arrays)
    return pl.pallas_call(
        body,
        out_shape=[o if isinstance(o, jax.ShapeDtypeStruct) else VM(o, jnp.bfloat16) for o in outs],
        in_specs=[inside] * len(arrays),
        out_specs=[
            pl.BlockSpec(memory_space=HB) if isinstance(o, jax.ShapeDtypeStruct) else inside for o in outs
        ],
        scratch_shapes=list(scratch),
        input_output_aliases={} if alias is None else {alias + i: i for i in range(aliases)},
        compiler_params=pltpu.CompilerParams(vmem_limit_bytes=12 << 20),
        cost_estimate=pl.CostEstimate(flops=flops, bytes_accessed=moved, transcendentals=0),
    )(*[vmem(x) for x in arrays])


def normalize(x, gain):
    wide = x.astype(jnp.float32)
    inverse = lax.rsqrt(jnp.mean(wide * wide, axis=1, keepdims=True) + EPS)
    return (wide * inverse * gain).astype(jnp.bfloat16)


def rotate(x, cosine, sine):
    heads = x.shape[1] // HD
    parts = []
    for i in range(heads):
        one = x[:, i * HD : (i + 1) * HD]
        parts.append((one * cosine + pltpu.roll(one, HD // 2, 1) * sine).astype(jnp.bfloat16))
    return parts


def dot(a, b):
    return jnp.dot(a, b, preferred_element_type=jnp.float32)


def project_kv(normed, wk, wv, cosine, sine):
    keys = rotate(dot(normed, wk[...]), cosine, sine)
    values = dot(normed, wv[...]).astype(jnp.bfloat16)
    return keys, values


def project_q(normed, wq, cosine, sine):
    parts = []
    for i in range(wq.shape[1] // 256):
        parts += rotate(dot(normed, wq[:, i * 256 : (i + 1) * 256]), cosine, sine)
    return parts


def run(copies):
    for copy in copies:
        copy.start()
    for copy in copies:
        copy.wait()


def halves_body(hidden, a, b, sems):
    size = CH // 2
    run([pltpu.make_async_copy(hidden.at[i * size : (i + 1) * size], out, sems.at[i]) for i, out in enumerate((a, b))])


def weights_body(wq, wk, wv, after, after_too, wq_out, wk_out, wv_out, sems):
    run([pltpu.make_async_copy(w, out, sems.at[i]) for i, (w, out) in enumerate(((wq, wq_out), (wk, wk_out), (wv, wv_out)))])


def chunk_rows(at):
    return pl.ds(pl.multiple_of(at * CH, CH), CH)


def half_rows(at, offset):
    return pl.ds(pl.multiple_of(at * CH + offset, CH // 2), CH // 2)


def normalize_all(pieces, gain):
    return jnp.concatenate([normalize(piece[...], gain[...]) for piece in pieces], axis=0)


def put(ref, index, rows, parts):
    for i, part in enumerate(parts):
        ref[index, :, i * HD : (i + 1) * HD] = part[rows]


def kv_parts(normed, wk, wv, cosine, sine):
    keys, values = project_kv(normed, wk, wv, cosine, sine)
    return [*keys, values[:, :HD], values[:, HD:]]


def own_body(xa, xb, gain, wq, wk, wv, cosines, sines, ext, q_out):
    own = spots()[0]
    rows = chunk_rows(own)
    normed = normalize_all((xa, xb), gain)
    put(ext, 2 + own, slice(None), kv_parts(normed, wk, wv, cosines[rows], sines[rows]))
    for i, part in enumerate(project_q(normed, wq, cosines[rows], sines[rows])):
        q_out[:, i * HD : (i + 1) * HD] = part


def owned_part(part, live):
    live = jnp.concatenate([live] * (part.shape[1] // HD), axis=1)
    return jnp.where(live, part.astype(jnp.float32), 0.0).astype(jnp.bfloat16)


def near_body(ext_in, la, rb, gain, wq, wk, wv, cosines, sines, ext, q_out):
    _, left, right, _, _ = spots()
    half = CH // 2
    first, second = half_rows(left, 0), half_rows(right, half)
    cosine = jnp.concatenate([cosines[first], cosines[second]], axis=0)
    sine = jnp.concatenate([sines[first], sines[second]], axis=0)
    normed = normalize_all((la, rb), gain)
    for i, part in enumerate(kv_parts(normed, wk, wv, cosine, sine)):
        ext[2 + left, 0:half, i * HD : (i + 1) * HD] = part[:half]
        ext[2 + right, half:CH, i * HD : (i + 1) * HD] = part[half:]
    for i, part in enumerate(project_q(normed, wq, cosine, sine)):
        q_out[:, i * HD : (i + 1) * HD] = part


def rest_turns(cosines, sines):
    _, left, right, _, _ = spots()
    half = CH // 2
    first, second = half_rows(right, 0), half_rows(left, half)
    cosine = jnp.concatenate([cosines[first], cosines[second]], axis=0)
    sine = jnp.concatenate([sines[first], sines[second]], axis=0)
    return cosine, sine


def rest_body(ext_in, owners, ra, lb, gain, wk, wv, cosines, sines, ext, normed_out, inside_out, outside_out):
    _, left, right, _, home = spots()
    half = CH // 2
    normed = normalize_all((ra, lb), gain)
    normed_out[...] = normed
    for i, part in enumerate(kv_parts(normed, wk, wv, *rest_turns(cosines, sines))):
        ext[2 + right, 0:half, i * HD : (i + 1) * HD] = part[:half]
        ext[2 + left, half:CH, i * HD : (i + 1) * HD] = part[half:]
    count = jnp.sum(jnp.where(owners[3 * CH :] == home + 1, 1.0 / 32, 0.0), axis=0, keepdims=True)
    count = jnp.broadcast_to(jnp.concatenate([count] * 4, axis=1), (16, 512)).astype(jnp.bfloat16)

    def fill(to_right, to_left):
        to_right[0:CH] = ext[4]
        to_right[CH : 2 * CH] = ext[5]
        to_right[2 * CH :] = count
        to_left[0:CH] = owned_part(ext[2], owners[0:CH] == home - 1)

    @pl.when(lax.rem(home, 2) == 0)
    def _():
        fill(inside_out, outside_out)

    @pl.when(lax.rem(home, 2) == 1)
    def _():
        fill(outside_out, inside_out)


def rest_q_body(normed, wq, cosines, sines, q_out):
    for i, part in enumerate(project_q(normed[...], wq, *rest_turns(cosines, sines))):
        q_out[:, i * HD : (i + 1) * HD] = part


def attend(tile, q, ext, docs):
    window = 3 * CH
    doc = docs[chunk_rows(tile), 0:1]
    key_row = lax.broadcasted_iota(jnp.int32, (CH, window), 1) + (tile - 2) * CH
    row = lax.broadcasted_iota(jnp.int32, (CH, window), 0) + tile * CH
    allowed = (key_row >= doc) & (key_row <= row)
    allowed = jnp.concatenate([allowed, allowed], axis=0)
    near = ext[pl.ds(tile, 3)].reshape(window, 512)
    outs = []
    for g in range(2):
        pair = jnp.concatenate(q[2 * g : 2 * g + 2], axis=0)
        keys, values = near[:, g * HD : (g + 1) * HD], near[:, (2 + g) * HD : (3 + g) * HD]
        scores = lax.dot_general(pair, keys, (((1,), (1,)), ((), ())), preferred_element_type=jnp.float32) * HD ** (-0.5)
        scores = jnp.where(allowed, scores, -jnp.inf)
        highest = jnp.max(scores, axis=1, keepdims=True)
        weights = jnp.exp(scores - highest)
        weights = (weights * (1.0 / jnp.sum(weights, axis=1, keepdims=True))).astype(jnp.bfloat16)
        blended = dot(weights, values).astype(jnp.bfloat16)
        outs += [blended[:CH], blended[CH:]]
    return outs


def heads(q):
    return [q[:, i * HD : (i + 1) * HD] for i in range(4)]


def emit(out, parts):
    for i, part in enumerate(parts):
        out[:, i * HD : (i + 1) * HD] = part


def far_tile(ext, normed, wq, cosines, sines, docs, out):
    far = spots()[3]
    rows = chunk_rows(far)
    q = project_q(normed[...], wq, cosines[rows], sines[rows])
    emit(out, attend(far, q, ext, docs))


def far_is_ahead():
    own, _, _, _, home = spots()
    return (lax.rem(home, 2) == 1) & (own != 2)


def ahead_body(ext_in, late_in, normed, wq, cosines, sines, docs, ext, late_out, out):
    @pl.when(far_is_ahead())
    def _():
        far_tile(ext, normed, wq, cosines, sines, docs, out)


def far_body(ext_in, out_in, outer, normed, wq, cosines, sines, docs, ext, out):
    @pl.when(lax.rem(spots()[4], 2) == 0)
    def _():
        ext[0] = outer[0:CH]
        ext[1] = outer[CH : 2 * CH]

    @pl.when(jnp.logical_not(far_is_ahead()))
    def _():
        far_tile(ext, normed, wq, cosines, sines, docs, out)


def last_body(ext_in, owners, xa, xb, gain, wk, wv, cosines, sines, ext, normed_out, late_out):
    _, _, _, far, home = spots()
    rows = chunk_rows(far)
    normed = normalize_all((xa, xb), gain)
    normed_out[...] = normed
    parts = kv_parts(normed, wk, wv, cosines[rows], sines[rows])
    put(ext, 2 + far, slice(None), parts)
    live = (owners[0:CH] == home - 1) | (far > 0)
    for i, part in enumerate(parts):
        late_out[:, i * HD : (i + 1) * HD] = owned_part(part, live)


def first_tile(ext, q_near, q_rest, docs, out):
    half = CH // 2
    q = jnp.concatenate([q_rest[0:half], q_near[half:CH]], axis=0)
    emit(out, attend(spots()[2], heads(q), ext, docs))


def first_is_early():
    own, _, _, _, home = spots()
    return (lax.rem(home, 2) == 1) | (own == 1) | (own == 2)


def first_body(ext_in, inner, q_near, q_rest, docs, ext, out):
    @pl.when(lax.rem(spots()[4], 2) == 1)
    def _():
        ext[0] = inner[0:CH]
        ext[1] = inner[CH : 2 * CH]

    @pl.when(first_is_early())
    def _():
        first_tile(ext, q_near, q_rest, docs, out)


def second_body(out_in, far_in, ext, q_near, q_rest, docs, out, far_out):
    @pl.when(jnp.logical_not(first_is_early()))
    def _():
        first_tile(ext, q_near, q_rest, docs, out)


def left_body(ext_in, late, q_near, q_rest, docs, ext, out):
    own, left, _, _, _ = spots()
    half = CH // 2

    @pl.when(own < 2)
    def _():
        ext[own] = late[...]

    q = jnp.concatenate([q_near[0:half], q_rest[half:CH]], axis=0)
    emit(out, attend(left, heads(q), ext, docs))


def own_tile_body(ext, owners, late, inner, outer, q, docs, out, key_out, value_out, keys, values, sems):
    own, _, _, _, home = spots()

    def put_cache(row, part):
        keys[row : row + part.shape[0]] = part[:, 0:256]
        values[row : row + part.shape[0]] = part[:, 256:512]

    count = jnp.where(lax.rem(home, 2) == 1, inner[2 * CH : 2 * CH + 1, :], outer[2 * CH : 2 * CH + 1, :]).astype(jnp.float32)
    for j in range(4):
        part = ext[1, j * 32 : (j + 1) * 32]
        put_cache(j * 32, jnp.where(count > 3.5 - j, part.astype(jnp.float32), 0.0).astype(jnp.bfloat16))
    for j in range(4):
        put_cache(CH + j * CH, owned_part(ext[2 + j], owners[j * CH : (j + 1) * CH] == home))

    @pl.when(own == 2)
    def _():
        put_cache(5 * CH, late[...])

    @pl.when((own != 2) & (lax.rem(home, 2) == 0))
    def _():
        put_cache(5 * CH, inner[0:CH])

    @pl.when((own != 2) & (lax.rem(home, 2) == 1))
    def _():
        put_cache(5 * CH, outer[0:CH])

    copies = [
        pltpu.make_async_copy(keys, key_out, sems.at[0]),
        pltpu.make_async_copy(values, value_out, sems.at[1]),
    ]
    for copy in copies:
        copy.start()
    emit(out, attend(own, heads(q), ext, docs))
    for copy in copies:
        copy.wait()


def join_body(s0, r1, r2, r3, out, sems):
    own, left, right, far, _ = spots()
    copies = []
    for i, (piece, at) in enumerate(((s0, own), (r1, left), (r2, far), (r3, right))):
        columns = pl.ds(pl.multiple_of(at * 512, 512), 512)
        copies.append(pltpu.make_async_copy(piece, out.at[:, columns], sems.at[i]))
    run(copies)


def layer(hidden, norm_gain, w_query, w_key, w_value, doc_start, block_owner):
    home = lax.axis_index("seq")
    rows = doc_start.shape[0]
    bf = jnp.bfloat16
    inside = pl.BlockSpec(memory_space=VM)
    outside = pl.BlockSpec(memory_space=pltpu.MemorySpace.HBM)
    wide = hidden.shape[1]

    def mover(body, outs, arrays, size):
        return pl.pallas_call(
            body,
            out_shape=[VM(s, bf) for s in outs],
            in_specs=[outside if x.size > CH * wide // 2 else pl.BlockSpec(memory_space=pl.ANY) for x in arrays],
            out_specs=[inside] * len(outs),
            scratch_shapes=[pltpu.SemaphoreType.DMA((len(outs),))],
            compiler_params=pltpu.CompilerParams(vmem_limit_bytes=2 << 20),
            cost_estimate=pl.CostEstimate(flops=0, bytes_accessed=size, transcendentals=0),
        )(*[pltpu.with_memory_space_constraint(x, HB) if x.size > CH * wide // 2 else x for x in arrays])

    own_a, own_b = mover(halves_body, [(CH // 2, wide)] * 2, [hidden], 2 << 20)
    left_a = ring(own_a, 1)
    right_b = ring(own_b, -1)
    left_b = ring(own_b, 1)
    right_a = ring(own_a, -1)
    far_a = ring(left_a, 1)
    far_b = ring(right_b, -1)
    row_number = home * rows + jnp.arange(rows, dtype=jnp.int32)
    lane = jnp.arange(HD, dtype=jnp.float32)
    lane_half = jnp.where(lane < HD // 2, lane, lane - HD // 2)
    frequency = jnp.power(ROPE_BASE, -lane_half * (2.0 / HD))
    angles = (row_number - doc_start).astype(jnp.float32)[:, None] * frequency[None, :]
    cosines, sines = jnp.cos(angles), jnp.where(lane < HD // 2, -1.0, 1.0)[None, :] * jnp.sin(angles)
    docs = jnp.broadcast_to((doc_start - home * rows)[:, None], (rows, HD))
    owners = jnp.broadcast_to(block_owner[:, None, None], (block_owner.shape[0], BLK, HD)).reshape(rows, HD)

    w_query, w_key, w_value = mover(
        weights_body, [w.shape for w in (w_query, w_key, w_value)], [w_query, w_key, w_value, docs, owners], 16 << 20
    )
    gain = norm_gain[None, :]
    flops = 2 * CH * wide * 1024
    scores = 8 * 2 * CH * 3 * CH * HD
    slots = (6, CH, 512)
    piece = (CH, 512)
    ext, q_own = call(own_body, [slots, piece], [own_a, own_b, gain, w_query, w_key, w_value, cosines, sines], flops)
    ext, q_near = call(
        near_body,
        [slots, piece],
        [ext, left_a, right_b, gain, w_query, w_key, w_value, cosines, sines],
        flops,
        alias=0,
    )
    ext, normed, inside_out, outside_out = call(
        rest_body,
        [slots, (CH, wide), (2 * CH + 16, 512), (2 * CH + 16, 512)],
        [ext, owners, right_a, left_b, gain, w_key, w_value, cosines, sines],
        flops // 2,
        alias=0,
    )
    outer = swap(outside_out, 1)
    inner = swap(inside_out, 0)
    (q_rest,) = call(rest_q_body, [piece], [normed, w_query, cosines, sines], flops // 2)
    ext, s1 = call(first_body, [slots, piece], [ext, inner, q_near, q_rest, docs], scores, alias=0)
    ext, normed, far = call(
        last_body,
        [slots, (CH, wide), piece],
        [ext, owners, far_a, far_b, gain, w_key, w_value, cosines, sines],
        flops // 2,
        alias=0,
    )
    ext, far, s2 = call(
        ahead_body,
        [slots, piece, piece],
        [ext, far, normed, w_query, cosines, sines, docs],
        flops,
        alias=0,
        aliases=2,
    )
    late = across(far, {0: 1, 1: 1, 2: -1})
    ext, s2 = call(
        far_body,
        [slots, piece],
        [ext, s2, outer, normed, w_query, cosines, sines, docs],
        flops,
        alias=0,
        aliases=2,
    )
    s1, s2 = call(second_body, [piece, piece], [s1, s2, ext, q_near, q_rest, docs], scores, alias=0, aliases=2)
    r2 = ring(s2, 2)
    r1 = ring(s1, 1)
    ext, s3 = call(left_body, [slots, piece], [ext, late, q_near, q_rest, docs], scores, alias=0)
    r3 = ring(s3, 3)
    cache = jax.ShapeDtypeStruct((rows + 2 * CH, 256), bf)
    s0, key_cache, value_cache = call(
        own_tile_body,
        [piece, cache, cache],
        [ext, owners, late, inner, outer, q_own, docs],
        scores,
        scratch=[VM((rows + 2 * CH, 256), bf)] * 2 + [pltpu.SemaphoreType.DMA((2,))],
    )
    (context,) = call(
        join_body,
        [jax.ShapeDtypeStruct((CH, 2048), bf)],
        [s0, r1, r2, r3],
        scratch=[pltpu.SemaphoreType.DMA((4,))],
    )
    return (context, key_cache, value_cache)


def solution(mesh):
    return jax.shard_map(
        layer,
        mesh=mesh,
        in_specs=(
            P(("seq", "tp"), None),
            P(),
            P(None, "tp"),
            P(None, "tp"),
            P(None, "tp"),
            P("seq"),
            P("seq"),
        ),
        out_specs=(P(("seq", "tp"), None), P("seq", "tp"), P("seq", "tp")),
        check_vma=False,
    )
```

```python
import jax
import jax.numpy as jnp
from jax import lax
from jax.experimental import pallas as pl
from jax.experimental.pallas import tpu as pltpu
from jax.sharding import PartitionSpec as P


HD = 128
EPS = 1e-05
ROPE_BASE = 500000.0
CH = 128
BLK = 32
VM = pltpu.MemorySpace.VMEM
HB = pltpu.MemorySpace.HBM


def ring(array, by):
    n = lax.axis_size("tp")
    return lax.ppermute(array, "tp", [(i, (i + by) % n) for i in range(n)])


def across(array, moves):
    homes, n = lax.axis_size("seq"), lax.axis_size("tp")
    pairs = [(h * n + t, (h + by) * n + t) for h in range(homes) for t, by in moves.items() if 0 <= h + by < homes]
    return lax.ppermute(array, ("seq", "tp"), pairs)


def swap(array, first):
    homes = lax.axis_size("seq")
    pairs = [p for h in range(first, homes - 1, 2) for p in ((h, h + 1), (h + 1, h))]
    return lax.ppermute(array, "seq", pairs)


def spots():
    me, home = lax.axis_index("tp"), lax.axis_index("seq")
    return [lax.rem(me + k, 4) for k in (0, 3, 1, 2)] + [home]


def vmem(x):
    return pltpu.with_memory_space_constraint(x, VM)


def call(body, outs, arrays, flops=0, alias=None, aliases=1, scratch=()):
    inside = pl.BlockSpec(memory_space=VM)
    moved = sum(x.size * x.dtype.itemsize for x in arrays)
    return pl.pallas_call(
        body,
        out_shape=[o if isinstance(o, jax.ShapeDtypeStruct) else VM(o, jnp.bfloat16) for o in outs],
        in_specs=[inside] * len(arrays),
        out_specs=[
            pl.BlockSpec(memory_space=HB) if isinstance(o, jax.ShapeDtypeStruct) else inside for o in outs
        ],
        scratch_shapes=list(scratch),
        input_output_aliases={} if alias is None else {alias + i: i for i in range(aliases)},
        compiler_params=pltpu.CompilerParams(vmem_limit_bytes=12 << 20),
        cost_estimate=pl.CostEstimate(flops=flops, bytes_accessed=moved, transcendentals=0),
    )(*[vmem(x) for x in arrays])


def normalize(x, gain):
    wide = x.astype(jnp.float32)
    inverse = lax.rsqrt(jnp.mean(wide * wide, axis=1, keepdims=True) + EPS)
    return (wide * inverse * gain).astype(jnp.bfloat16)


def rotate(x, cosine, sine):
    heads = x.shape[1] // HD
    parts = []
    for i in range(heads):
        one = x[:, i * HD : (i + 1) * HD]
        parts.append((one * cosine + pltpu.roll(one, HD // 2, 1) * sine).astype(jnp.bfloat16))
    return parts


def dot(a, b):
    return jnp.dot(a, b, preferred_element_type=jnp.float32)


def project_kv(normed, wk, wv, cosine, sine):
    keys = rotate(dot(normed, wk[...]), cosine, sine)
    values = dot(normed, wv[...]).astype(jnp.bfloat16)
    return keys, values


def project_q(normed, wq, cosine, sine):
    parts = []
    for i in range(wq.shape[1] // 256):
        parts += rotate(dot(normed, wq[:, i * 256 : (i + 1) * 256]), cosine, sine)
    return parts


def run(copies):
    for copy in copies:
        copy.start()
    for copy in copies:
        copy.wait()


def halves_body(hidden, a, b, sems):
    size = CH // 2
    run([pltpu.make_async_copy(hidden.at[i * size : (i + 1) * size], out, sems.at[i]) for i, out in enumerate((a, b))])


def weights_body(wq, wk, wv, after, after_too, wq_out, wk_out, wv_out, sems):
    run([pltpu.make_async_copy(w, out, sems.at[i]) for i, (w, out) in enumerate(((wq, wq_out), (wk, wk_out), (wv, wv_out)))])


def chunk_rows(at):
    return pl.ds(pl.multiple_of(at * CH, CH), CH)


def half_rows(at, offset):
    return pl.ds(pl.multiple_of(at * CH + offset, CH // 2), CH // 2)


def normalize_all(pieces, gain):
    return jnp.concatenate([normalize(piece[...], gain[...]) for piece in pieces], axis=0)


def put(ref, index, rows, parts):
    for i, part in enumerate(parts):
        ref[index, :, i * HD : (i + 1) * HD] = part[rows]


def kv_parts(normed, wk, wv, cosine, sine):
    keys, values = project_kv(normed, wk, wv, cosine, sine)
    return [*keys, values[:, :HD], values[:, HD:]]


def own_body(xa, xb, gain, wq, wk, wv, cosines, sines, ext, q_out):
    own = spots()[0]
    rows = chunk_rows(own)
    normed = normalize_all((xa, xb), gain)
    put(ext, 2 + own, slice(None), kv_parts(normed, wk, wv, cosines[rows], sines[rows]))
    for i, part in enumerate(project_q(normed, wq, cosines[rows], sines[rows])):
        q_out[:, i * HD : (i + 1) * HD] = part


def owned_part(part, live):
    live = jnp.concatenate([live] * (part.shape[1] // HD), axis=1)
    return jnp.where(live, part.astype(jnp.float32), 0.0).astype(jnp.bfloat16)


def near_body(ext_in, la, rb, gain, wq, wk, wv, cosines, sines, ext, q_out):
    _, left, right, _, _ = spots()
    half = CH // 2
    first, second = half_rows(left, 0), half_rows(right, half)
    cosine = jnp.concatenate([cosines[first], cosines[second]], axis=0)
    sine = jnp.concatenate([sines[first], sines[second]], axis=0)
    normed = normalize_all((la, rb), gain)
    for i, part in enumerate(kv_parts(normed, wk, wv, cosine, sine)):
        ext[2 + left, 0:half, i * HD : (i + 1) * HD] = part[:half]
        ext[2 + right, half:CH, i * HD : (i + 1) * HD] = part[half:]
    for i, part in enumerate(project_q(normed, wq, cosine, sine)):
        q_out[:, i * HD : (i + 1) * HD] = part


def rest_turns(cosines, sines):
    _, left, right, _, _ = spots()
    half = CH // 2
    first, second = half_rows(right, 0), half_rows(left, half)
    cosine = jnp.concatenate([cosines[first], cosines[second]], axis=0)
    sine = jnp.concatenate([sines[first], sines[second]], axis=0)
    return cosine, sine


def rest_body(ext_in, owners, ra, lb, gain, wk, wv, cosines, sines, ext, normed_out, inside_out, outside_out):
    _, left, right, _, home = spots()
    half = CH // 2
    normed = normalize_all((ra, lb), gain)
    normed_out[...] = normed
    for i, part in enumerate(kv_parts(normed, wk, wv, *rest_turns(cosines, sines))):
        ext[2 + right, 0:half, i * HD : (i + 1) * HD] = part[:half]
        ext[2 + left, half:CH, i * HD : (i + 1) * HD] = part[half:]
    count = jnp.sum(jnp.where(owners[3 * CH :] == home + 1, 1.0 / 32, 0.0), axis=0, keepdims=True)
    count = jnp.broadcast_to(jnp.concatenate([count] * 4, axis=1), (16, 512)).astype(jnp.bfloat16)

    def fill(to_right, to_left):
        to_right[0:CH] = ext[4]
        to_right[CH : 2 * CH] = ext[5]
        to_right[2 * CH :] = count
        to_left[0:CH] = owned_part(ext[2], owners[0:CH] == home - 1)

    @pl.when(lax.rem(home, 2) == 0)
    def _():
        fill(inside_out, outside_out)

    @pl.when(lax.rem(home, 2) == 1)
    def _():
        fill(outside_out, inside_out)


def rest_q_body(normed, wq, cosines, sines, q_out):
    for i, part in enumerate(project_q(normed[...], wq, *rest_turns(cosines, sines))):
        q_out[:, i * HD : (i + 1) * HD] = part


def attend(tile, q, ext, docs):
    window = 3 * CH
    doc = docs[chunk_rows(tile), 0:1]
    key_row = lax.broadcasted_iota(jnp.int32, (CH, window), 1) + (tile - 2) * CH
    row = lax.broadcasted_iota(jnp.int32, (CH, window), 0) + tile * CH
    allowed = (key_row >= doc) & (key_row <= row)
    allowed = jnp.concatenate([allowed, allowed], axis=0)
    near = ext[pl.ds(tile, 3)].reshape(window, 512)
    outs = []
    for g in range(2):
        pair = jnp.concatenate(q[2 * g : 2 * g + 2], axis=0)
        keys, values = near[:, g * HD : (g + 1) * HD], near[:, (2 + g) * HD : (3 + g) * HD]
        scores = lax.dot_general(pair, keys, (((1,), (1,)), ((), ())), preferred_element_type=jnp.float32) * HD ** (-0.5)
        scores = jnp.where(allowed, scores, -jnp.inf)
        highest = jnp.max(scores, axis=1, keepdims=True)
        weights = jnp.exp(scores - highest)
        weights = (weights * (1.0 / jnp.sum(weights, axis=1, keepdims=True))).astype(jnp.bfloat16)
        blended = dot(weights, values).astype(jnp.bfloat16)
        outs += [blended[:CH], blended[CH:]]
    return outs


def heads(q):
    return [q[:, i * HD : (i + 1) * HD] for i in range(4)]


def emit(out, parts):
    for i, part in enumerate(parts):
        out[:, i * HD : (i + 1) * HD] = part


def far_body(ext_in, outer, normed, wq, cosines, sines, docs, ext, out):
    _, _, _, far, home = spots()
    rows = chunk_rows(far)

    @pl.when(lax.rem(home, 2) == 0)
    def _():
        ext[0] = outer[0:CH]
        ext[1] = outer[CH : 2 * CH]

    q = project_q(normed[...], wq, cosines[rows], sines[rows])
    emit(out, attend(far, q, ext, docs))


def half_body(x, gain, out):
    out[...] = normalize(x[...], gain[...])


def last_body(ext_in, owners, xa, xb, gain, wk, wv, cosines, sines, ext, normed_out, late_out):
    _, _, _, far, home = spots()
    rows = chunk_rows(far)
    normed = jnp.concatenate([xa[...], normalize(xb[...], gain[...])], axis=0)
    normed_out[...] = normed
    parts = kv_parts(normed, wk, wv, cosines[rows], sines[rows])
    put(ext, 2 + far, slice(None), parts)
    live = (owners[0:CH] == home - 1) | (far > 0)
    for i, part in enumerate(parts):
        late_out[:, i * HD : (i + 1) * HD] = owned_part(part, live)


def first_tile(ext, q_near, q_rest, docs, out):
    half = CH // 2
    q = jnp.concatenate([q_rest[0:half], q_near[half:CH]], axis=0)
    emit(out, attend(spots()[2], heads(q), ext, docs))


def first_is_early():
    own, _, _, _, home = spots()
    return (lax.rem(home, 2) == 1) | (own == 1) | (own == 2)


def first_body(ext_in, inner, q_near, q_rest, docs, ext, out):
    @pl.when(lax.rem(spots()[4], 2) == 1)
    def _():
        ext[0] = inner[0:CH]
        ext[1] = inner[CH : 2 * CH]

    @pl.when(first_is_early())
    def _():
        first_tile(ext, q_near, q_rest, docs, out)


def second_body(out_in, far_in, ext, q_near, q_rest, docs, out, far_out):
    @pl.when(jnp.logical_not(first_is_early()))
    def _():
        first_tile(ext, q_near, q_rest, docs, out)


def left_body(ext_in, late, q_near, q_rest, docs, ext, out):
    own, left, _, _, _ = spots()
    half = CH // 2

    @pl.when(own < 2)
    def _():
        ext[own] = late[...]

    q = jnp.concatenate([q_near[0:half], q_rest[half:CH]], axis=0)
    emit(out, attend(left, heads(q), ext, docs))


def own_tile_body(ext, owners, late, inner, outer, q, docs, out, key_out, value_out, keys, values, sems):
    own, _, _, _, home = spots()

    def put_cache(row, part):
        keys[row : row + part.shape[0]] = part[:, 0:256]
        values[row : row + part.shape[0]] = part[:, 256:512]

    count = jnp.where(lax.rem(home, 2) == 1, inner[2 * CH : 2 * CH + 1, :], outer[2 * CH : 2 * CH + 1, :]).astype(jnp.float32)
    for j in range(4):
        part = ext[1, j * 32 : (j + 1) * 32]
        put_cache(j * 32, jnp.where(count > 3.5 - j, part.astype(jnp.float32), 0.0).astype(jnp.bfloat16))
    for j in range(4):
        put_cache(CH + j * CH, owned_part(ext[2 + j], owners[j * CH : (j + 1) * CH] == home))

    @pl.when(own == 2)
    def _():
        put_cache(5 * CH, late[...])

    @pl.when((own != 2) & (lax.rem(home, 2) == 0))
    def _():
        put_cache(5 * CH, inner[0:CH])

    @pl.when((own != 2) & (lax.rem(home, 2) == 1))
    def _():
        put_cache(5 * CH, outer[0:CH])

    copies = [
        pltpu.make_async_copy(keys, key_out, sems.at[0]),
        pltpu.make_async_copy(values, value_out, sems.at[1]),
    ]
    for copy in copies:
        copy.start()
    emit(out, attend(own, heads(q), ext, docs))
    for copy in copies:
        copy.wait()


def join_body(s0, r1, r2, r3, out, sems):
    own, left, right, far, _ = spots()
    copies = []
    for i, (piece, at) in enumerate(((s0, own), (r1, left), (r2, far), (r3, right))):
        columns = pl.ds(pl.multiple_of(at * 512, 512), 512)
        copies.append(pltpu.make_async_copy(piece, out.at[:, columns], sems.at[i]))
    run(copies)


def layer(hidden, norm_gain, w_query, w_key, w_value, doc_start, block_owner):
    home = lax.axis_index("seq")
    rows = doc_start.shape[0]
    bf = jnp.bfloat16
    inside = pl.BlockSpec(memory_space=VM)
    outside = pl.BlockSpec(memory_space=pltpu.MemorySpace.HBM)
    wide = hidden.shape[1]

    def mover(body, outs, arrays, size):
        return pl.pallas_call(
            body,
            out_shape=[VM(s, bf) for s in outs],
            in_specs=[outside if x.size > CH * wide // 2 else pl.BlockSpec(memory_space=pl.ANY) for x in arrays],
            out_specs=[inside] * len(outs),
            scratch_shapes=[pltpu.SemaphoreType.DMA((len(outs),))],
            compiler_params=pltpu.CompilerParams(vmem_limit_bytes=2 << 20),
            cost_estimate=pl.CostEstimate(flops=0, bytes_accessed=size, transcendentals=0),
        )(*[pltpu.with_memory_space_constraint(x, HB) if x.size > CH * wide // 2 else x for x in arrays])

    own_a, own_b = mover(halves_body, [(CH // 2, wide)] * 2, [hidden], 2 << 20)
    left_a = ring(own_a, 1)
    right_b = ring(own_b, -1)
    left_b = ring(own_b, 1)
    right_a = ring(own_a, -1)
    far_a = ring(left_a, 1)
    far_b = ring(right_b, -1)
    row_number = home * rows + jnp.arange(rows, dtype=jnp.int32)
    lane = jnp.arange(HD, dtype=jnp.float32)
    lane_half = jnp.where(lane < HD // 2, lane, lane - HD // 2)
    frequency = jnp.power(ROPE_BASE, -lane_half * (2.0 / HD))
    angles = (row_number - doc_start).astype(jnp.float32)[:, None] * frequency[None, :]
    cosines, sines = jnp.cos(angles), jnp.where(lane < HD // 2, -1.0, 1.0)[None, :] * jnp.sin(angles)
    docs = jnp.broadcast_to((doc_start - home * rows)[:, None], (rows, HD))
    owners = jnp.broadcast_to(block_owner[:, None, None], (block_owner.shape[0], BLK, HD)).reshape(rows, HD)

    w_query, w_key, w_value = mover(
        weights_body, [w.shape for w in (w_query, w_key, w_value)], [w_query, w_key, w_value, docs, owners], 16 << 20
    )
    gain = norm_gain[None, :]
    flops = 2 * CH * wide * 1024
    scores = 8 * 2 * CH * 3 * CH * HD
    slots = (6, CH, 512)
    piece = (CH, 512)
    ext, q_own = call(own_body, [slots, piece], [own_a, own_b, gain, w_query, w_key, w_value, cosines, sines], flops)
    ext, q_near = call(
        near_body,
        [slots, piece],
        [ext, left_a, right_b, gain, w_query, w_key, w_value, cosines, sines],
        flops,
        alias=0,
    )
    ext, normed, inside_out, outside_out = call(
        rest_body,
        [slots, (CH, wide), (2 * CH + 16, 512), (2 * CH + 16, 512)],
        [ext, owners, right_a, left_b, gain, w_key, w_value, cosines, sines],
        flops // 2,
        alias=0,
    )
    outer = swap(outside_out, 1)
    inner = swap(inside_out, 0)
    (q_rest,) = call(rest_q_body, [piece], [normed, w_query, cosines, sines], flops // 2)
    ext, s1 = call(first_body, [slots, piece], [ext, inner, q_near, q_rest, docs], scores, alias=0)
    (far_a,) = call(half_body, [(CH // 2, wide)], [far_a, gain])
    ext, normed, far = call(
        last_body,
        [slots, (CH, wide), piece],
        [ext, owners, far_a, far_b, gain, w_key, w_value, cosines, sines],
        flops // 2,
        alias=0,
    )
    late = across(far, {0: 1, 1: 1, 2: -1})
    ext, s2 = call(
        far_body, [slots, piece], [ext, outer, normed, w_query, cosines, sines, docs], flops, alias=0
    )
    s1, s2 = call(second_body, [piece, piece], [s1, s2, ext, q_near, q_rest, docs], scores, alias=0, aliases=2)
    r2 = ring(s2, 2)
    r1 = ring(s1, 1)
    ext, s3 = call(left_body, [slots, piece], [ext, late, q_near, q_rest, docs], scores, alias=0)
    r3 = ring(s3, 3)
    cache = jax.ShapeDtypeStruct((rows + 2 * CH, 256), bf)
    s0, key_cache, value_cache = call(
        own_tile_body,
        [piece, cache, cache],
        [ext, owners, late, inner, outer, q_own, docs],
        scores,
        scratch=[VM((rows + 2 * CH, 256), bf)] * 2 + [pltpu.SemaphoreType.DMA((2,))],
    )
    (context,) = call(
        join_body,
        [jax.ShapeDtypeStruct((CH, 2048), bf)],
        [s0, r1, r2, r3],
        scratch=[pltpu.SemaphoreType.DMA((4,))],
    )
    return (context, key_cache, value_cache)


def solution(mesh):
    return jax.shard_map(
        layer,
        mesh=mesh,
        in_specs=(
            P(("seq", "tp"), None),
            P(),
            P(None, "tp"),
            P(None, "tp"),
            P(None, "tp"),
            P("seq"),
            P("seq"),
        ),
        out_specs=(P(("seq", "tp"), None), P("seq", "tp"), P("seq", "tp")),
        check_vma=False,
    )
```
